32 devices in a mesh: bx: 8 (over y, x, core), by: 4 (over z).
Axes of the slice: x: 2, y: 2, z: 4, core: 2. Of those that a mesh axis runs over, the one named last changes fastest.
Arguments:
- right_sides: float32 [8, 4, 128, 768], P('bx', 'by'), may hold values from -6 to 6
- skeleton_order: int32 [8, 4, 4, 768], P('bx', 'by'), may hold values from 0 to 767, as said below
- interp_first: float32 [8, 4, 384, 384], P('bx', 'by'), may hold values from -0.15625 to 0.15625
- interp_second: float32 [8, 4, 384, 192], P('bx', 'by'), may hold values from -0.15625 to 0.15625
- interp_third: float32 [8, 4, 384, 96], P('bx', 'by'), may hold values from -0.15625 to 0.15625
- interp_fourth: float32 [8, 4, 384, 48], P('bx', 'by'), may hold values from -0.15625 to 0.15625
- inverse_first: float32 [8, 4, 384, 384], P('bx', 'by'), may hold values from -0.25 to 0.25
- inverse_second: float32 [8, 4, 384, 192], P('bx', 'by'), may hold values from -0.25 to 0.25
- inverse_third: float32 [8, 4, 384, 96], P('bx', 'by'), may hold values from -0.25 to 0.25
- inverse_fourth: float32 [8, 4, 384, 48], P('bx', 'by'), may hold values from -0.25 to 0.25
- couple_first: float32 [8, 4, 5, 384, 384], P('bx', 'by'), may hold values from -0.09375 to 0.09375
- couple_second: float32 [8, 4, 5, 384, 192], P('bx', 'by'), may hold values from -0.09375 to 0.09375
- couple_third: float32 [8, 4, 5, 384, 96], P('bx', 'by'), may hold values from -0.09375 to 0.09375
- couple_fourth: float32 [8, 4, 5, 384, 48], P('bx', 'by'), may hold values from -0.09375 to 0.09375
- root_inverse: float32 [8, 4, 384, 48], P('bx', 'by'), may hold values from -0.21875 to 0.21875
Outputs:
- solution: float32 [8, 4, 128, 768], P('bx', 'by')
The draws below stay inside these ranges and needn't reach their ends.
Inputs may be any that keep to these rules, and one draw needn't show every extreme that they name: For every fine box and level l, skeleton_order[i, j, l, :] is a permutation of 0 to 767, the same at all fine boxes of one level-l box.
All inputs are finite; a program needn't handle non-finite values.
Results may differ from the reference program's by a relative error of at most 0.0003.
Values sent between devices are 32-bit elements; how exact they have to be, the bound alone decides.
A program may use at most 128 MiB of HBM per device.

```python
import jax
import jax.numpy as jnp
from jax import lax

SKEL = 384
BOX = 768
NRHS = 128
BOXES_X = 8
BOXES_Y = 4


def draw_skeleton_order(key, part):
    stacked = []
    for level_index, extent in enumerate(((1, 1), (1, 2), (2, 2), (2, 4))):
        group_x, group_y = extent
        box_count = BOXES_X // group_x * (BOXES_Y // group_y)
        subkeys = jax.random.split(jax.random.fold_in(key, level_index + 11), box_count)
        shuffles = jax.vmap(lambda subkey: jax.random.permutation(subkey, BOX))(subkeys)
        layout = shuffles.reshape(BOXES_X // group_x, BOXES_Y // group_y, BOX)
        layout = jnp.repeat(jnp.repeat(layout, group_x, axis=0), group_y, axis=1)
        stacked.append(layout)
    return jnp.stack(stacked, axis=2).astype(jnp.int32)


def level_of(rng, shape, shards, low, high):
    def one(axis_at, shards_of):
        steps = jax.random.uniform(jax.random.fold_in(jax.random.fold_in(rng, 6), axis_at), (shards_of,), jnp.float32, low / len(shards), high / len(shards))
        return jnp.repeat(jnp.exp(steps), shape[axis_at] // shards_of).reshape((-1,) + (1,) * (len(shape) - axis_at - 1))

    loudness = one(*shards[0])
    for cut in shards[1:]:
        loudness = loudness * one(*cut)
    return loudness


def scatter_about(stream_key, shape, deviation, bound, cuts=(), held_as=jnp.bfloat16):
    values = deviation * jax.random.normal(stream_key, shape, jnp.float32)
    if cuts:
        values = values * level_of(stream_key, shape, cuts, -0.22, 0.18)
    return jnp.clip(values, -bound, bound).astype(held_as)


def setup_inputs(seed: int = 0) -> dict:
    keys = jax.random.split(jax.random.key(seed), 16)
    return {
        "right_sides": scatter_about(keys[0], (BOXES_X, BOXES_Y, NRHS, BOX), 1.0, 6.0, ((0, 8), (1, 4)), jnp.float32),
        "skeleton_order": draw_skeleton_order(jax.random.fold_in(keys[15], 71), 0),
        "interp_first": scatter_about(keys[2], (BOXES_X, BOXES_Y, SKEL, SKEL), (4 * SKEL) ** -0.5, 0.15625, ((0, 8), (1, 4)), jnp.float32),
        "interp_second": scatter_about(keys[3], (BOXES_X, BOXES_Y, SKEL, SKEL // 2), (4 * SKEL) ** -0.5, 0.15625, ((0, 8), (1, 4)), jnp.float32),
        "interp_third": scatter_about(keys[4], (BOXES_X, BOXES_Y, SKEL, SKEL // 4), (4 * SKEL) ** -0.5, 0.15625, ((0, 8), (1, 4)), jnp.float32),
        "interp_fourth": scatter_about(keys[5], (BOXES_X, BOXES_Y, SKEL, SKEL // 8), (4 * SKEL) ** -0.5, 0.15625, ((0, 8), (1, 4)), jnp.float32),
        "inverse_first": scatter_about(keys[6], (BOXES_X, BOXES_Y, SKEL, SKEL), (SKEL * 5 // 4) ** -0.5, 0.25, ((0, 8), (1, 4)), jnp.float32),
        "inverse_second": scatter_about(keys[7], (BOXES_X, BOXES_Y, SKEL, SKEL // 2), (SKEL * 5 // 4) ** -0.5, 0.25, ((0, 8), (1, 4)), jnp.float32),
        "inverse_third": scatter_about(keys[8], (BOXES_X, BOXES_Y, SKEL, SKEL // 4), (SKEL * 5 // 4) ** -0.5, 0.25, ((0, 8), (1, 4)), jnp.float32),
        "inverse_fourth": scatter_about(keys[9], (BOXES_X, BOXES_Y, SKEL, SKEL // 8), (SKEL * 5 // 4) ** -0.5, 0.25, ((0, 8), (1, 4)), jnp.float32),
        "couple_first": scatter_about(keys[10], (BOXES_X, BOXES_Y, 5, SKEL, SKEL), (10 * SKEL) ** -0.5, 0.09375, ((0, 8), (1, 4)), jnp.float32),
        "couple_second": scatter_about(keys[11], (BOXES_X, BOXES_Y, 5, SKEL, SKEL // 2), (10 * SKEL) ** -0.5, 0.09375, ((0, 8), (1, 4)), jnp.float32),
        "couple_third": scatter_about(keys[12], (BOXES_X, BOXES_Y, 5, SKEL, SKEL // 4), (10 * SKEL) ** -0.5, 0.09375, ((0, 8), (1, 4)), jnp.float32),
        "couple_fourth": scatter_about(keys[13], (BOXES_X, BOXES_Y, 5, SKEL, SKEL // 8), (10 * SKEL) ** -0.5, 0.09375, ((0, 8), (1, 4)), jnp.float32),
        "root_inverse": scatter_about(keys[14], (BOXES_X, BOXES_Y, SKEL, SKEL // 8), (2 * SKEL) ** -0.5, 0.21875, ((0, 8), (1, 4)), jnp.float32),
    }


HIGHEST = lax.Precision.HIGHEST
GROUPS = ((1, 1), (1, 2), (2, 2), (2, 4))
MERGE_ALONG = (1, 0, 1)


def assemble(pieces, level_index):
    if level_index == 0:
        return pieces
    total_x = pieces.shape[0]
    total_y = pieces.shape[1]
    inner_shape = tuple(pieces.shape[2:-1])
    piece_width = pieces.shape[-1]
    inner_rank = len(inner_shape)
    middle = list(range(inner_rank))
    if level_index == 1:
        blocks = pieces.reshape((total_x, total_y // 2, 2) + inner_shape + (piece_width,))
        axes_order = [0, 1] + [3 + position for position in middle] + [2, 3 + inner_rank]
        shape_out = (total_x, total_y // 2)
    elif level_index == 2:
        blocks = pieces.reshape((total_x // 2, 2, total_y // 2, 2) + inner_shape + (piece_width,))
        axes_order = [0, 2] + [4 + position for position in middle] + [1, 3, 4 + inner_rank]
        shape_out = (total_x // 2, total_y // 2)
    else:
        blocks = pieces.reshape((total_x // 2, 2, total_y // 4, 2, 2) + inner_shape + (piece_width,))
        axes_order = [0, 2] + [5 + position for position in middle] + [3, 1, 4, 5 + inner_rank]
        shape_out = (total_x // 2, total_y // 4)
    arranged = jnp.transpose(blocks, axes_order)
    return arranged.reshape(shape_out + inner_shape + (piece_width * 2 ** level_index,))


def from_lower(field, axis_number):
    padding = jnp.zeros_like(lax.slice_in_dim(field, 0, 1, axis=axis_number))
    kept = lax.slice_in_dim(field, 0, field.shape[axis_number] - 1, axis=axis_number)
    return jnp.concatenate([padding, kept], axis=axis_number)


def from_upper(field, axis_number):
    padding = jnp.zeros_like(lax.slice_in_dim(field, 0, 1, axis=axis_number))
    kept = lax.slice_in_dim(field, 1, field.shape[axis_number], axis=axis_number)
    return jnp.concatenate([kept, padding], axis=axis_number)


def reference(right_sides, skeleton_order, interp_first, interp_second, interp_third, interp_fourth,
              inverse_first, inverse_second, inverse_third, inverse_fourth,
              couple_first, couple_second, couple_third, couple_fourth, root_inverse):
    interps = (interp_first, interp_second, interp_third, interp_fourth)
    inverses = (inverse_first, inverse_second, inverse_third, inverse_fourth)
    couples = (couple_first, couple_second, couple_third, couple_fourth)
    vector = right_sides
    stored = []
    skeleton = vector
    for level_index in range(4):
        group_x, group_y = GROUPS[level_index]
        perm_grid = skeleton_order[::group_x, ::group_y, level_index]
        arranged = jnp.take_along_axis(vector, perm_grid[:, :, None, :], axis=3)
        skel_part = arranged[..., :SKEL]
        redund_part = arranged[..., SKEL:]
        interp_full = assemble(interps[level_index], level_index)
        inverse_full = assemble(inverses[level_index], level_index)
        couple_full = assemble(couples[level_index], level_index)
        lowered = redund_part - jnp.einsum("abns,absr->abnr", skel_part, interp_full, precision=HIGHEST)
        solved = jnp.einsum("abnk,abkr->abnr", lowered, inverse_full, precision=HIGHEST)
        stacked = jnp.stack([solved, from_lower(solved, 0), from_upper(solved, 0),
                             from_lower(solved, 1), from_upper(solved, 1)], axis=2)
        skeleton = skel_part - jnp.einsum("abknr,abkrs->abns", stacked, couple_full, precision=HIGHEST)
        stored.append((perm_grid, interp_full, inverse_full, couple_full, solved))
        if level_index < 3:
            if MERGE_ALONG[level_index] == 1:
                vector = jnp.concatenate([skeleton[:, 0::2], skeleton[:, 1::2]], axis=-1)
            else:
                vector = jnp.concatenate([skeleton[0::2], skeleton[1::2]], axis=-1)
    skel_value = jnp.einsum("abns,abst->abnt", skeleton, assemble(root_inverse, 3), precision=HIGHEST)
    for level_index in (3, 2, 1, 0):
        perm_grid, interp_full, inverse_full, couple_full, solved = stored[level_index]
        products = jnp.einsum("abns,abkrs->abknr", skel_value, couple_full, precision=HIGHEST)
        update = (products[:, :, 0] + from_upper(products[:, :, 1], 0) + from_lower(products[:, :, 2], 0)
                  + from_upper(products[:, :, 3], 1) + from_lower(products[:, :, 4], 1))
        redund_sol = solved - jnp.einsum("abnk,abrk->abnr", update, inverse_full, precision=HIGHEST)
        skel_sol = skel_value - jnp.einsum("abnr,absr->abns", redund_sol, interp_full, precision=HIGHEST)
        combined = jnp.concatenate([skel_sol, redund_sol], axis=-1)
        inverse_perm = jnp.argsort(perm_grid, axis=-1).astype(jnp.int32)
        vector = jnp.take_along_axis(combined, inverse_perm[:, :, None, :], axis=3)
        if level_index > 0:
            lower_half = vector[..., :SKEL]
            upper_half = vector[..., SKEL:]
            count_x, count_y, rows_count = vector.shape[0], vector.shape[1], vector.shape[2]
            if MERGE_ALONG[level_index - 1] == 1:
                skel_value = jnp.stack([lower_half, upper_half], axis=2).reshape(count_x, 2 * count_y, rows_count, SKEL)
            else:
                skel_value = jnp.stack([lower_half, upper_half], axis=1).reshape(2 * count_x, count_y, rows_count, SKEL)
    return vector
```

```python
import functools

import jax
import jax.numpy as jnp
from jax import lax
from jax.experimental import pallas as pl
from jax.experimental.pallas import tpu as pltpu
from jax.sharding import PartitionSpec as P

REACH = ((1, 1), (1, 2), (2, 2), (2, 4))
F32 = jnp.float32
BF16 = jnp.bfloat16
MESH = pl.DeviceIdType.MESH
NN = (((1,), (0,)), ((), ()))
TN = (((0,), (0,)), ((), ()))
NT = (((1,), (1,)), ((), ()))


def halves(x):
    high = x.astype(BF16)
    return high, (x - high.astype(F32)).astype(BF16)


def product(a, b, dims):
    return lax.dot_general(a, b, dims, preferred_element_type=F32)


def dot3(a, b, dims):
    ah, al = halves(a)
    bh, bl = halves(b)
    return product(ah, bh, dims) + (product(ah, bl, dims) + product(al, bh, dims))


def pick_left(onehot, b, dims):
    bh, bl = halves(b)
    return product(onehot, bh, dims) + product(onehot, bl, dims)


class Reg:
    def __init__(self): self.c=None
    def __call__(self,name):
        if self.c: self.c.__exit__(None,None,None)
        self.c=jax.named_scope(name) if name else None
        if self.c: self.c.__enter__()


def flips(m):
    return (m >> 1) & 1, (m & 1) | ((m >> 2 & 1) << 1)


def kernel(size_x, size_y, *refs):
    (rhs, order_row, t0, t1, t2, t3, g0, g1, g2, g3, k0, k1, k2, k3, root, out) = refs[:16]
    (ybuf, vbuf, qsend, qrecv, urecv1, urecv2, urecv3, xrecv1, xrecv2, xrecv3, xpart, tg1, tg2, tg3,
     n0, n1, n2, n3, abuf, ypart, tpart, ssend, ptbuf, order_col, send, recv) = refs[16:]
    interps, inverses, couples = (t0, t1, t2, t3), (g0, g1, g2, g3), (k0, k1, k2, k3)
    urecvs = (None, urecv1, urecv2, urecv3)
    xrecvs = (None, xrecv1, xrecv2, xrecv3)
    tgs = (None, tg1, tg2, tg3)
    ns = (n0, n1, n2, n3)
    skel = t0.shape[2]
    box = 2 * skel
    i, j = lax.axis_index("bx"), lax.axis_index("by")
    bits = (lax.rem(j, 2), lax.rem(i, 2), lax.rem(lax.div(j, 2), 2))
    ranks = [jnp.int32(0), bits[0], bits[0] + 2 * bits[1], bits[0] + 2 * bits[1] + 4 * bits[2]]

    def toggled(value, mask):
        for b in (0, 1):
            if mask >> b & 1:
                value = value + (1 << b) * (1 - 2 * lax.rem(lax.div(value, 1 << b), 2))
        return value

    def member(m):
        mx, my = flips(m)
        return (toggled(i, mx), toggled(j, my))

    def rank_of(level, m):
        rank = jnp.int32(0)
        for b in range(level):
            bit = bits[b]
            rank = rank + (1 << b) * ((1 - bit) if m >> b & 1 else bit)
        return rank

    count = [0]

    def slot():
        count[0] += 1
        return count[0] - 1

    def neighbour(level, k):
        rx, ry = REACH[level]
        bx, by = lax.div(i, rx), lax.div(j, ry)
        if k == 1:
            return i >= rx, (i - rx, j)
        if k == 2:
            return i + rx < size_x, (i + rx, j)
        if k == 3:
            return j >= ry, (i, j - ry)
        return j + ry < size_y, (i, j + ry)

    opposite = {1: 2, 2: 1, 3: 4, 4: 3}
    level_has = [[k for k in (1, 2, 3, 4) if (REACH[l][0] < size_x if k < 3 else REACH[l][1] < size_y)] for l in range(4)]

    def rcopy(src, dst, s, dev):
        return pltpu.make_async_remote_copy(src, dst, send.at[s], recv.at[s], device_id=dev, device_id_type=MESH)

    reg = Reg()
    reg('zero')
    order_f = order_row[0, 0].astype(F32)
    order_f = jnp.concatenate([order_f, jnp.zeros((8 - order_f.shape[0], box), F32)], axis=0)
    order_col[...] = order_f.T.astype(jnp.int32)
    for level in range(4):
        for k in (1, 2, 3, 4):
            there, _ = neighbour(level, k)

            @pl.when(jnp.logical_not(there))
            def _():
                ybuf[level, pl.ds(k * skel, skel), :] = jnp.zeros((skel, ybuf.shape[2]), F32)
                qrecv[level, k - 1] = jnp.zeros((skel, ybuf.shape[2]), F32)

    reg('barrier')
    barrier = pltpu.get_barrier_semaphore()
    for m in range(1, 8):
        pl.semaphore_signal(barrier, 1, device_id=member(m), device_id_type=MESH)
    total = jnp.int32(7)
    greeted = set()
    for level in range(4):
        for k in level_has[level]:
            key = (k, REACH[level][0] if k < 3 else REACH[level][1])
            if key in greeted:
                continue
            greeted.add(key)
            there, dev = neighbour(level, k)

            @pl.when(there)
            def _():
                pl.semaphore_signal(barrier, 1, device_id=dev, device_id_type=MESH)
            total = total + there.astype(jnp.int32)
    pl.semaphore_wait(barrier, total)

    reg('sendint1')
    pending = []

    t_copies = [[], [], [], []]

    def send_interp(level):
        for m in [m for m in range(1, 1 << level) if not m & 2]:
            c = rcopy(interps[level].at[0, 0], tgs[level].at[ranks[level]], slot(), member(m))
            c.start()
            t_copies[level].append(c)
            pending.append(c)

    send_interp(1)

    def make_n(level):
        own = inverses[level][0, 0]
        if level == 0:
            ns[0][:skel, :] = -dot3(interps[0][0, 0], own, NN)
            ns[0][skel:, :] = own
            return
        cols = own.shape[0]
        tgs[level][ranks[level]] = interps[level][0, 0]
        for c in t_copies[level]:
            c.wait_recv()
        shared = []
        for m in [m for m in range(1 << level) if not m & 2 and level > 1]:
            block = rank_of(level, m)
            held = interps[level].at[0, 0] if m == 0 else tgs[level].at[block]
            c = rcopy(held, tgs[level].at[block], slot(), member(2))
            c.start()
            shared.append(c)
            pending.append(c)
        for c in shared:
            c.wait_recv()
        ns[level][:, :skel] = -dot3(own, tgs[level][...].reshape(skel, skel), NN)
        ns[level][:, skel:] = own

    def onehot_pt(level):
        lanes = lax.broadcasted_iota(jnp.int32, (box, box), 1)
        return jnp.where(lanes == order_col[:, level:level + 1], 1.0, 0.0).astype(BF16)

    def onehot_p(level):
        rows = lax.broadcasted_iota(jnp.int32, (box, box), 0)
        return jnp.where(rows == order_row[0, 0, level:level + 1, :], 1.0, 0.0).astype(BF16)

    for level in range(4):
        reg(f'f{level}_a')
        cols = skel >> level
        rank = ranks[level]
        rows = pl.ds(pl.multiple_of(rank * cols, cols), cols)
        if level == 0:
            make_n(0)
            abuf[...] = pick_left(onehot_pt(0), rhs[0, 0], NT)
        else:
            abuf[...] = pick_left(ptbuf[...], vbuf[level - 1], NN)
        reg(f'f{level}_y')
        y_own = dot3(ns[level][...], abuf[...], NN if level else TN)
        ypart[level, :cols, :] = y_own
        ybuf[level, rows, :] = y_own
        gathers = []
        for m in range(1, 1 << level):
            c = rcopy(ypart.at[level, pl.ds(0, cols), :], ybuf.at[level, rows, :], slot(), member(m))
            c.start()
            gathers.append(c)
            pending.append(c)
        reg(f'f{level}_ygwait')
        for c in gathers:
            c.wait_recv()
        reg(f'f{level}_nbsend')
        for k in level_has[level]:
            s = slot()
            far = opposite[k]
            there, dev = neighbour(level, k)
            c = rcopy(ybuf.at[level, pl.ds(0, skel), :], ybuf.at[level, pl.ds(far * skel, skel), :], s, dev)

            @pl.when(there)
            def _():
                c.start()
            pending.append((there, c))
        base = count[0] - len(level_has[level])
        if level < 2:
            send_interp(level + 2)
        reg(f'f{level}_make')
        if level < 3:
            make_n(level + 1)
            ptbuf[...] = onehot_pt(level + 1)
        reg(f'f{level}_nbwait')
        for k in level_has[level]:
            there, dev = neighbour(level, k)
            sent_as = level_has[level].index(opposite[k])
            c = rcopy(ybuf.at[level, pl.ds(0, skel), :], ybuf.at[level, pl.ds(k * skel, skel), :], base + sent_as, dev)

            @pl.when(there)
            def _():
                c.wait_recv()
        reg(f'f{level}_s')
        if level == 0:
            s_own = abuf[...][:skel] - dot3(couples[0][0, 0].reshape(5 * skel, skel), ybuf[0], TN)
        else:
            s_own = abuf[rows, :]
            for k in range(5):
                s_own = s_own - dot3(couples[level][0, 0, k], ybuf[level, k * skel:(k + 1) * skel, :], NN)
        ssend[level, :cols, :] = s_own
        wide = min(level + 1, 3)
        spot = pl.ds(pl.multiple_of(ranks[wide] * cols, cols), cols)
        vbuf[level, spot, :] = s_own
        gathers = []
        for m in range(1, 1 << wide):
            c = rcopy(ssend.at[level, pl.ds(0, cols), :], vbuf.at[level, spot, :], slot(), member(m))
            c.start()
            gathers.append(c)
            pending.append(c)
        reg(f'f{level}_sgwait')
        for c in gathers:
            c.wait_recv()

    reg('root')
    t_own = dot3(root[0, 0], vbuf[3, :skel, :], NN)

    for level in (3, 2, 1, 0):
        cols = skel >> level
        rank = ranks[level]
        members = 1 << level
        rows = pl.ds(pl.multiple_of(rank * cols, cols), cols)
        reg(f'b{level}_q')
        tpart[:cols, :] = t_own
        if level == 0:
            qsend[0] = dot3(couples[0][0, 0].reshape(5 * skel, cols), t_own, NN)
        else:
            for k in range(5):
                qsend[level, k * skel:(k + 1) * skel, :] = dot3(couples[level][0, 0, k], t_own, TN)
        base = count[0]
        for k in level_has[level]:
            s = slot()
            there, dev = neighbour(level, k)
            c = rcopy(qsend.at[level, pl.ds(k * skel, skel), :], qrecv.at[level, opposite[k] - 1], s, dev)

            @pl.when(there)
            def _():
                c.start()
            pending.append((there, c))
        reg(f'b{level}_t')
        y_own = ypart[level, :cols, :]
        abuf[:skel, :] = -dot3(interps[level][0, 0], y_own, TN if level else NN)
        abuf[skel:, :] = jnp.zeros_like(abuf[skel:, :])
        abuf[rows, :] = abuf[rows, :] + t_own
        rows_y = pl.ds(pl.multiple_of(skel + rank * cols, 8), cols)
        abuf[rows_y, :] = y_own
        ptbuf[...] = onehot_p(level) if level > 0 else onehot_pt(0)
        reg(f'b{level}_nbwait')
        for k in level_has[level]:
            there, dev = neighbour(level, k)
            sent_as = level_has[level].index(opposite[k])
            c = rcopy(qsend.at[level, pl.ds(k * skel, skel), :], qrecv.at[level, k - 1], base + sent_as, dev)

            @pl.when(there)
            def _():
                c.wait_recv()
        reg(f'b{level}_u')
        u = qsend[level, :skel, :] + ((qrecv[level, 0] + qrecv[level, 1]) + (qrecv[level, 2] + qrecv[level, 3]))
        if level > 0:
            qsend[level, :skel, :] = u
            gathers = []
            for m in range(1, members):
                far_rows = pl.ds(pl.multiple_of(rank_of(level, m) * cols, cols), cols)
                c = rcopy(qsend.at[level, far_rows, :], urecvs[level].at[m - 1], slot(), member(m))
                c.start()
                gathers.append(c)
                pending.append(c)
            reg(f'b{level}_uwait')
            for c in gathers:
                c.wait_recv()
            reg(f'b{level}_u2')
            u_own = qsend[level, rows, :]
            for m in range(1, members):
                u_own = u_own + urecvs[level][m - 1]
        else:
            u_own = u
        reg(f'b{level}_comb')
        comb = -dot3(ns[level][...], u_own, TN if level else NN)
        abuf[...] = abuf[...] + comb
        reg(f'b{level}_x')
        if level > 0:
            xpart[level] = pick_left(ptbuf[...], abuf[...], NN)
            size = box // members
            gathers = []
            for m in range(1, members):
                far_rows = pl.ds(pl.multiple_of(rank_of(level, m) * size, size), size)
                c = rcopy(xpart.at[level, far_rows, :], xrecvs[level].at[m - 1], slot(), member(m))
                c.start()
                gathers.append(c)
                pending.append(c)
            reg(f'b{level}_xwait')
            for c in gathers:
                c.wait_recv()
            reg(f'b{level}_x2')
            t_own = xpart[level, pl.ds(pl.multiple_of(rank * size, size), size), :]
            for m in range(1, members):
                t_own = t_own + xrecvs[level][m - 1]
        else:
            ch, cl = halves(abuf[...])
            pt = ptbuf[...]
            out[0, 0] = product(ch, pt, TN) + product(cl, pt, TN)

    reg('drain')
    for item in pending:
        if isinstance(item, tuple):
            there, c = item

            @pl.when(there)
            def _():
                c.wait_send()
        else:
            item.wait_send()
    reg(None)


def body(size_x, size_y, right_sides, skeleton_order, *weights):
    rows = right_sides.shape[2]
    box = right_sides.shape[3]
    skel = box // 2
    weights = [jnp.swapaxes(w, -1, -2) if w.shape[-1] < skel else w for w in weights]
    vm = lambda *shape: pltpu.VMEM(shape, F32)
    widths = [skel >> level for level in range(4)]
    scratch = [
        vm(4, 5 * skel, rows), vm(4, box, rows), vm(4, 5 * skel, rows), vm(4, 4, skel, rows),
        vm(1, widths[1], rows), vm(3, widths[2], rows), vm(7, widths[3], rows),
        vm(1, box // 2, rows), vm(3, box // 4, rows), vm(7, box // 8, rows),
        vm(4, box, rows),
        vm(2, widths[1], skel), vm(4, widths[2], skel), vm(8, widths[3], skel),
        vm(box, widths[0]), vm(widths[1], box), vm(widths[2], box), vm(widths[3], box),
        vm(box, rows), vm(4, skel, rows), vm(skel, rows), vm(4, skel, rows),
        pltpu.VMEM((box, box), BF16), pltpu.VMEM((box, 8), jnp.int32),
        pltpu.SemaphoreType.DMA((128,)), pltpu.SemaphoreType.DMA((128,)),
    ]
    return pl.pallas_call(
        functools.partial(kernel, size_x, size_y),
        out_shape=jax.ShapeDtypeStruct(right_sides.shape, F32),
        in_specs=[pl.BlockSpec(memory_space=pltpu.VMEM)] * (2 + len(weights)),
        out_specs=pl.BlockSpec(memory_space=pltpu.VMEM),
        scratch_shapes=scratch,
        compiler_params=pltpu.CompilerParams(
            collective_id=0, has_side_effects=True, vmem_limit_bytes=60 * 2**20
        ),
    )(right_sides, skeleton_order, *weights)


def solution(mesh):
    four = P("bx", "by", None, None)
    five = P("bx", "by", None, None, None)
    in_specs = (four,) * 10 + (five,) * 4 + (four,)
    return jax.shard_map(
        functools.partial(body, mesh.shape["bx"], mesh.shape["by"]),
        mesh=mesh, in_specs=in_specs, out_specs=four, check_vma=False,
    )
```

```python
import functools

import jax
import jax.numpy as jnp
from jax import lax
from jax.experimental import pallas as pl
from jax.experimental.pallas import tpu as pltpu
from jax.sharding import PartitionSpec as P

REACH = ((1, 1), (1, 2), (2, 2), (2, 4))
OPPOSITE = {1: 2, 2: 1, 3: 4, 4: 3}
F32 = jnp.float32
BF16 = jnp.bfloat16
MESH = pl.DeviceIdType.MESH
NN = (((1,), (0,)), ((), ()))
TN = (((0,), (0,)), ((), ()))
NT = (((1,), (1,)), ((), ()))


def halves(x):
    high = x.astype(BF16)
    return high, (x - high.astype(F32)).astype(BF16)


def product(a, b, dims):
    return lax.dot_general(a, b, dims, preferred_element_type=F32)


def dot3(a, b, dims):
    ah, al = halves(a)
    bh, bl = halves(b)
    return product(ah, bh, dims) + (product(ah, bl, dims) + product(al, bh, dims))


def pick_left(onehot, b, dims):
    bh, bl = halves(b)
    return product(onehot, bh, dims) + product(onehot, bl, dims)


def pick_right(a, onehot, dims):
    ah, al = halves(a)
    return product(ah, onehot, dims) + product(al, onehot, dims)


class Phases:
    def __init__(self):
        self.scope = None

    def __call__(self, name):
        if self.scope:
            self.scope.__exit__(None, None, None)
        self.scope = jax.named_scope(name) if name else None
        if self.scope:
            self.scope.__enter__()


def kernel(size_x, size_y, *refs):
    (rhs_in, order_in, t0_in, t1_in, t2_in, t3_in, g0_in, g1_in, g2_in, g3_in,
     k0_in, k1_in, k2_in, k3_in, root_in, out) = refs[:16]
    (rhs, order_row, t0, tg1, tg2, g0, g1, g2, k0, k1, k2,
     ybuf, vbuf, qsend, qrecv, urecv1, urecv2, xrecv1, xrecv2, xpart,
     n0, n1, n2, abuf, ypart, ssend, ptbuf, order_col,
     top, turned, v3, y3, yr3, q3, qr3, x3, back3, pick3, local, send, recv) = refs[16:]
    inverses, couples = (g0, g1, g2), (k0, k1, k2)
    urecvs, xrecvs, tgs, ns = (None, urecv1, urecv2), (None, xrecv1, xrecv2), (None, tg1, tg2), (n0, n1, n2)
    skel = t0.shape[0]
    box = 2 * skel
    rhs_count = ybuf.shape[2]
    share = v3.shape[1]
    kinds = top.shape[0] - 3
    phase = Phases()
    i, j = lax.axis_index("bx"), lax.axis_index("by")
    bits = (lax.rem(j, 2), lax.rem(i, 2), lax.rem(lax.div(j, 2), 2))
    inner = bits[0] != bits[2]
    outer = jnp.logical_not(inner)

    def flipped(b, m):
        return (1 - bits[b]) if m >> b & 1 else bits[b]

    def member(m):
        return (i + (flipped(1, m) - bits[1]), j + (flipped(0, m) - bits[0]) + 2 * (flipped(2, m) - bits[2]))

    def rank_of(level, m):
        rank = jnp.int32(0)
        for b in range(level):
            rank = rank + (1 << b) * flipped(b, m)
        return rank

    def part_of(m):
        return flipped(1, m) + 2 * flipped(2, m)

    def span(start, size):
        return pl.ds(pl.multiple_of(start * size, size), size)

    def neighbour(level, k):
        rx, ry = REACH[level]
        if k == 1:
            return i >= rx, (i - rx, j)
        if k == 2:
            return i + rx < size_x, (i + rx, j)
        if k == 3:
            return j >= ry, (i, j - ry)
        return j + ry < size_y, (i, j + ry)

    has = [[k for k in (1, 2, 3, 4) if (REACH[l][0] < size_x if k < 3 else REACH[l][1] < size_y)] for l in range(4)]
    cross = [[k for k in has[l] if k < 3] for l in range(4)]
    along = [[k for k in has[l] if k > 2] for l in range(4)]

    count = [0]
    pending = []

    def slot():
        count[0] += 1
        return count[0] - 1

    def rcopy(src, dst, s, dev):
        return pltpu.make_async_remote_copy(src, dst, send.at[s], recv.at[s], device_id=dev, device_id_type=MESH)

    def go(c, when=None):
        pending.append((when, c))
        if when is None:
            c.start()
        else:
            @pl.when(when)
            def _():
                c.start()

    def come(c, when=None):
        if when is None:
            c.wait_recv()
        else:
            @pl.when(when)
            def _():
                c.wait_recv()

    phase("start")
    rank = [rank_of(l, 0) for l in range(4)]
    loads = {}

    def load(name, src, dst):
        c = pltpu.make_async_copy(src, dst, local.at[len(loads)])
        loads[name] = c
        c.start()

    def need(*names):
        for name in names:
            loads[name].wait()

    load("order", order_in.at[0, 0], order_row)
    load("t0", t0_in.at[0, 0], t0)
    load("g0", g0_in.at[0, 0], g0)
    load("rhs", rhs_in.at[0, 0], rhs)
    load("t1", t1_in.at[0, 0], tg1.at[rank[1]])
    load("k0", k0_in.at[0, 0], k0)
    load("t2", t2_in.at[0, 0], tg2.at[rank[2]])
    load("g1", g1_in.at[0, 0], g1)
    load("t3", t3_in.at[0, 0], top.at[0, rank[3]])
    load("g3", g3_in.at[0, 0], top.at[1, rank[3]])
    load("root", root_in.at[0, 0], top.at[2, rank[3]])
    load("k3", k3_in.at[0, 0, pl.ds(0, kinds)], top.at[pl.ds(3, kinds), rank[3]])
    load("k1", k1_in.at[0, 0], k1)
    load("g2", g2_in.at[0, 0], g2)
    load("k2", k2_in.at[0, 0], k2)

    barrier = pltpu.get_barrier_semaphore()
    for m in range(1, 8):
        pl.semaphore_signal(barrier, 1, device_id=member(m), device_id_type=MESH)
    total = jnp.int32(7)
    greeted = set()
    for level in range(4):
        for k in has[level]:
            key = (k, REACH[level][0] if k < 3 else REACH[level][1])
            if key in greeted:
                continue
            greeted.add(key)
            there, dev = neighbour(level, k)

            @pl.when(there)
            def _():
                pl.semaphore_signal(barrier, 1, device_id=dev, device_id_type=MESH)
            total = total + there.astype(jnp.int32)

    for level in range(3):
        for k in (1, 2, 3, 4):
            there, _ = neighbour(level, k)

            @pl.when(jnp.logical_not(there))
            def _():
                ybuf[level, k * skel:(k + 1) * skel, :] = jnp.zeros((skel, rhs_count), F32)
                qrecv[level, k - 1] = jnp.zeros((skel, rhs_count), F32)
    for k in has[3]:
        there, _ = neighbour(3, k)

        @pl.when(jnp.logical_not(there))
        def _():
            yr3[k - 1] = jnp.zeros(yr3.shape[1:], F32)
            qr3[k - 1] = jnp.zeros(qr3.shape[1:], F32)
    turned[...] = jnp.zeros_like(turned)

    chunks = range((top.shape[0] + 1) // 2)
    slots_own, slots_in, slots_on = ([slot() for _ in chunks] for _ in range(3))
    slots_mate = [slot() for _ in range(4)]

    def chunk_copy(c, block, dev, s):
        at = pl.ds(2 * c, min(2, top.shape[0] - 2 * c))
        return rcopy(top.at[at, block], top.at[at, block], s, dev)

    def mate_copy(n, mine):
        block = rank_of(3, (0, 1, 5, 4)[n] ^ (0 if mine else 2))
        return rcopy(top.at[:, block], top.at[:, block], slots_mate[n], member(2))

    def outer_send(c):
        go(chunk_copy(c, rank[3], member(1), slots_own[c]), outer)

    def inner_send():
        for c in chunks:
            go(chunk_copy(c, rank[3], member(5), slots_in[c]), inner)

    def inner_forward(c):
        come(chunk_copy(c, rank_of(3, 1), member(1), slots_own[c]), inner)
        go(chunk_copy(c, rank_of(3, 1), member(5), slots_on[c]), inner)

    def mate_send(n):
        for c in chunks:
            if n == 2:
                come(chunk_copy(c, rank_of(3, 5), member(5), slots_in[c]), inner)
            if n == 3:
                come(chunk_copy(c, rank_of(3, 4), member(5), slots_on[c]), inner)
        go(mate_copy(n, True), inner)

    def onehot_pt(level):
        lanes = lax.broadcasted_iota(jnp.int32, (box, box), 1)
        return jnp.where(lanes == order_col[:, level:level + 1], 1.0, 0.0).astype(BF16)

    def onehot_p(level):
        rows = lax.broadcasted_iota(jnp.int32, (box, box), 0)
        return jnp.where(rows == order_row[level:level + 1, :], 1.0, 0.0).astype(BF16)

    def make_n(level):
        if level == 0:
            need("t0", "g0")
            n0[:skel, :] = -dot3(t0[...], g0[...], NN)
            n0[skel:, :] = g0[...]
            return
        need(f"g{level}")
        own = inverses[level][...]
        ns[level][:, :skel] = -dot3(own, tgs[level][...].reshape(skel, skel), NN)
        ns[level][:, skel:] = own

    need("order")
    order_f = order_row[...].astype(F32)
    order_f = jnp.concatenate([order_f, jnp.zeros((8 - order_f.shape[0], box), F32)], axis=0)
    order_col[...] = order_f.T.astype(jnp.int32)

    phase("f0_make")
    make_n(0)
    phase("f0_a")
    need("rhs")
    abuf[...] = pick_left(onehot_pt(0), rhs[...], NT)
    phase("f0_y")
    y_own = dot3(n0[...], abuf[...], TN)
    ybuf[0, :skel, :] = y_own
    ypart[0] = y_own
    phase("f0_barrier")
    pl.semaphore_wait(barrier, total)
    phase("f0_send")
    slots_y0 = {k: slot() for k in has[0]}
    for k in along[0] + cross[0]:
        there, dev = neighbour(0, k)
        far = OPPOSITE[k]
        go(rcopy(ypart.at[0], ybuf.at[0, pl.ds(far * skel, skel), :], slots_y0[k], dev), there)
    need("t1")
    t1_copy = rcopy(tg1.at[rank[1]], tg1.at[rank[1]], slot(), member(1))
    go(t1_copy)
    need("t3", "g3", "root", "k3")
    inner_send()
    mate_send(0)
    phase("f0_s")
    need("k0")
    s_own = abuf[:skel, :] - dot3(k0[0], ypart[0], TN)
    ptbuf[...] = onehot_pt(1)
    for k in cross[0] + along[0]:
        there, dev = neighbour(0, k)
        phase(f"f0_wait{k}")
        come(rcopy(ypart.at[0], ybuf.at[0, pl.ds(k * skel, skel), :], slots_y0[OPPOSITE[k]], dev), there)
        phase(f"f0_s{k}")
        s_own = s_own - dot3(k0[k], ybuf[0, k * skel:(k + 1) * skel, :], TN)
    ssend[0] = s_own
    vbuf[0, span(rank[1], skel), :] = s_own
    give = rcopy(ssend.at[0], vbuf.at[0, span(rank[1], skel), :], slot(), member(1))
    go(give)
    need("t2")
    t2_slots = [slot() for _ in range(3)]
    go(rcopy(tg2.at[rank[2]], tg2.at[rank[2]], t2_slots[0], member(1)))
    go(rcopy(tg2.at[rank[2]], tg2.at[rank[2]], t2_slots[1], member(2)))
    outer_send(0)
    phase("f0_n1")
    come(t1_copy)
    make_n(1)
    phase("f0_gwait")
    come(give)

    for level in (1, 2):
        phase(f"f{level}_a")
        cols = skel >> level
        mine = rank[level]
        rows = span(mine, cols)
        abuf[...] = pick_left(ptbuf[...], vbuf[level - 1], NN)
        phase(f"f{level}_y")
        y_own = dot3(ns[level][...], abuf[...], NN)
        ypart[level, :cols, :] = y_own
        ybuf[level, rows, :] = y_own

        def at(k, m):
            return ybuf.at[level, pl.ds(pl.multiple_of(k * skel + rank_of(level, m) * cols, cols), cols), :]

        def pair(k, m, to, s):
            return rcopy(at(k, m), at(k, m), s, member(to))

        own_src = ypart.at[level, pl.ds(0, cols), :]
        s_a = [slot() for _ in range(3)]
        s_c = {k: [slot(), slot()] for k in cross[level]}
        s_b = {k: slot() for k in along[level]}
        s_d = {k: [slot() for _ in range(3)] for k in along[level]}
        s_e = {k: [slot(), slot()] for k in cross[level]}
        phase(f"f{level}_send")
        go(rcopy(own_src, at(0, 0), s_a[0], member(1)))
        for k in along[level]:
            there, dev = neighbour(level, k)
            go(rcopy(own_src, at(OPPOSITE[k], 0), s_b[k], dev), there)
        if level == 2:
            go(rcopy(own_src, at(0, 0), s_a[1], member(2)))
        for k in cross[level]:
            there, dev = neighbour(level, k)
            go(rcopy(own_src, at(OPPOSITE[k], 0), s_c[k][0], dev), there)
        if level == 1:
            ptbuf[...] = onehot_pt(2)
        phase(f"f{level}_ywait")
        come(pair(0, 1, 1, s_a[0]))
        if level == 2:
            go(pair(0, 1, 2, s_a[2]))
        for k in cross[level]:
            there, dev = neighbour(level, k)
            go(rcopy(at(0, 1), at(OPPOSITE[k], 1), s_c[k][1], dev), there)
        if level == 1:
            outer_send(1)
            inner_forward(0)
        else:
            come(pair(0, 2, 2, s_a[1]))
            come(pair(0, 3, 2, s_a[2]))
            inner_forward(2)
        phase(f"f{level}_s0")
        need(f"k{level}")
        s_own = abuf[rows, :] - dot3(couples[level][0], ybuf[level, :skel, :], NN)
        phase(f"f{level}_relay")
        for k in cross[level]:
            there, dev = neighbour(level, k)
            come(rcopy(own_src, at(k, 0), s_c[OPPOSITE[k]][0], dev), there)
            if level == 2:
                go(pair(k, 0, 2, s_e[k][0]), there)
        for k in along[level]:
            there, dev = neighbour(level, k)
            come(rcopy(own_src, at(k, 0), s_b[OPPOSITE[k]], dev), there)
            go(pair(k, 0, 1, s_d[k][0]), there)
            if level == 2:
                go(pair(k, 0, 2, s_d[k][1]), there)
        for k in cross[level]:
            there, dev = neighbour(level, k)
            come(rcopy(own_src, at(k, 1), s_c[OPPOSITE[k]][1], dev), there)
            if level == 2:
                go(pair(k, 1, 2, s_e[k][1]), there)
        if level == 2:
            phase("f2_pick3")

            @pl.when(inner)
            def _():
                o = order_row[3:4, :]
                block = turned.shape[1]
                o = o + sum((block - cols) * (o >= cols * b).astype(jnp.int32) for b in range(1, 8))
                lines = lax.broadcasted_iota(jnp.int32, pick3.shape, 0)
                pick3[...] = jnp.where(lines == o, 1.0, 0.0).astype(BF16)
            mate_send(1)
            mate_send(2)
        for k in cross[level]:
            there, dev = neighbour(level, k)
            phase(f"f{level}_cross{k}")
            if level == 2:
                come(pair(k, 2, 2, s_e[k][0]), there)
                come(pair(k, 3, 2, s_e[k][1]), there)
            s_own = s_own - dot3(couples[level][k], ybuf[level, k * skel:(k + 1) * skel, :], NN)
        for k in along[level]:
            there, dev = neighbour(level, k)
            phase(f"f{level}_along{k}")
            come(pair(k, 1, 1, s_d[k][0]), there)
            if level == 2:
                go(pair(k, 1, 2, s_d[k][2]), there)
                come(pair(k, 2, 2, s_d[k][1]), there)
                come(pair(k, 3, 2, s_d[k][2]), there)
            s_own = s_own - dot3(couples[level][k], ybuf[level, k * skel:(k + 1) * skel, :], NN)
        if level == 2:
            turned[:, :cols] = s_own.T
            continue
        phase("f1_gsend")
        ssend[1, :cols, :] = s_own
        at_v = lambda m: vbuf.at[1, span(rank_of(2, m), cols), :]
        vbuf[1, span(rank[2], cols), :] = s_own
        s_g = [slot() for _ in range(3)]
        go(rcopy(ssend.at[1, pl.ds(0, cols), :], at_v(0), s_g[0], member(1)))
        go(rcopy(ssend.at[1, pl.ds(0, cols), :], at_v(0), s_g[1], member(2)))
        outer_send(2)
        come(rcopy(tg2.at[rank_of(2, 1)], tg2.at[rank_of(2, 1)], t2_slots[0], member(1)))
        go(rcopy(tg2.at[rank_of(2, 1)], tg2.at[rank_of(2, 1)], t2_slots[2], member(2)))
        come(rcopy(tg2.at[rank_of(2, 2)], tg2.at[rank_of(2, 2)], t2_slots[1], member(2)))
        come(rcopy(tg2.at[rank_of(2, 3)], tg2.at[rank_of(2, 3)], t2_slots[2], member(2)))
        phase("f1_n2")
        make_n(2)
        phase("f1_gwait")
        come(rcopy(at_v(1), at_v(1), s_g[0], member(1)))
        go(rcopy(at_v(1), at_v(1), s_g[2], member(2)))
        inner_forward(1)
        come(rcopy(at_v(2), at_v(2), s_g[1], member(2)))
        come(rcopy(at_v(3), at_v(3), s_g[2], member(2)))

    phase("l3_send")
    own_part = span(part_of(0), share)
    s_t = [slot() for _ in range(8)]
    s_x = [slot() for _ in range(8)]
    s_y3 = {k: slot() for k in has[3]}
    s_q3 = {k: slot() for k in has[3]}
    aside = lambda m: (m & 1) ^ (m >> 2 & 1)
    for m in range(1, 8):
        go(rcopy(turned.at[span(part_of(m), share)], v3.at[rank[3]], s_t[m], member(m)), outer if aside(m) else inner)
    mate_send(3)
    for n in range(4):
        come(mate_copy(n, False), inner)

    @pl.when(inner)
    def _():
        phase("l3_in")
        v3[rank[3]] = turned[own_part, :]
        for m in range(1, 8):
            come(rcopy(turned.at[own_part], v3.at[rank_of(3, m)], s_t[m], member(m)))
        full = lambda n: top[n].reshape(skel, skel)
        phase("l3_y")
        a = pick_right(jnp.concatenate([v3[b] for b in range(8)], axis=1), pick3[...], NN)
        s0, r0 = a[:, :skel], a[:, skel:]
        y = dot3(r0 - dot3(s0, full(0), NT), full(1), NT)
        y3[...] = y
        for k in has[3]:
            there, dev = neighbour(3, k)

            @pl.when(there)
            def _():
                rcopy(y3, yr3.at[OPPOSITE[k] - 1], s_y3[k], dev).start()
        phase("l3_s")
        s = s0 - dot3(y, full(3), NT)
        for k in has[3]:
            there, dev = neighbour(3, k)
            come(rcopy(y3, yr3.at[k - 1], s_y3[OPPOSITE[k]], dev), there)
            s = s - dot3(yr3[k - 1], full(3 + k), NT)
        phase("l3_q")
        t = dot3(s, full(2), NT)
        for k in has[3]:
            q3[k - 1] = dot3(t, full(3 + k), NN)
            there, dev = neighbour(3, k)

            @pl.when(there)
            def _():
                rcopy(q3.at[k - 1], qr3.at[OPPOSITE[k] - 1], s_q3[k], dev).start()
        u = dot3(t, full(3), NN)
        phase("l3_u")
        for k in has[3]:
            there, dev = neighbour(3, k)
            come(rcopy(q3.at[k - 1], qr3.at[k - 1], s_q3[OPPOSITE[k]], dev), there)
            u = u + qr3[k - 1]
        phase("l3_x")
        xr = y - dot3(u, full(1), NN)
        xs = t - dot3(xr, full(0), NN)
        xv = pick_right(jnp.concatenate([xs, xr], axis=1), pick3[...], NT)
        wide = turned.shape[1]
        for b in range(8):
            x3[b] = xv[:, b * wide:(b + 1) * wide]
        for m in range(1, 8):
            rcopy(x3.at[rank_of(3, m)], back3.at[own_part], s_x[m], member(m)).start()
        back3[own_part, :] = x3[rank[3]]
        phase(None)

    phase("l3_out")
    for m in range(1, 8):
        come(rcopy(x3.at[rank[3]], back3.at[span(part_of(m), share)], s_x[m], member(m)), outer if aside(m) else inner)
    t_own = back3[...].T[:skel >> 2]

    for level in (2, 1, 0):
        phase(f"b{level}_q")
        cols = skel >> level
        members = 1 << level
        rows = span(rank[level], cols)
        if level == 0:
            qsend[0] = dot3(k0[...].reshape(5 * skel, skel), t_own, NN)
        else:
            for k in range(5):
                qsend[level, k * skel:(k + 1) * skel, :] = dot3(couples[level][k], t_own, TN)
        s_q = {k: slot() for k in has[level]}
        for k in has[level]:
            there, dev = neighbour(level, k)
            go(rcopy(qsend.at[level, pl.ds(k * skel, skel), :], qrecv.at[level, OPPOSITE[k] - 1], s_q[k], dev), there)
        phase(f"b{level}_t")
        y_own = ypart[level, :cols, :]
        if level == 0:
            abuf[:skel, :] = t_own - dot3(t0[...], y_own, NN)
            abuf[skel:, :] = y_own
        else:
            abuf[:skel, :] = -dot3(tgs[level][rank[level]], y_own, TN)
            abuf[skel:, :] = jnp.zeros((skel, rhs_count), F32)
            abuf[rows, :] = abuf[rows, :] + t_own
            abuf[pl.ds(pl.multiple_of(skel + rank[level] * cols, 8), cols), :] = y_own
        ptbuf[...] = onehot_p(level) if level > 0 else onehot_pt(0)
        phase(f"b{level}_nbwait")
        for k in has[level]:
            there, dev = neighbour(level, k)
            come(rcopy(qsend.at[level, pl.ds(k * skel, skel), :], qrecv.at[level, k - 1], s_q[OPPOSITE[k]], dev), there)
        phase(f"b{level}_u")
        u = qsend[level, :skel, :] + ((qrecv[level, 0] + qrecv[level, 1]) + (qrecv[level, 2] + qrecv[level, 3]))
        if level > 0:
            qsend[level, :skel, :] = u
            gathers = []
            for m in range(1, members):
                c = rcopy(qsend.at[level, span(rank_of(level, m), cols), :], urecvs[level].at[m - 1], slot(), member(m))
                go(c)
                gathers.append(c)
            for c in gathers:
                come(c)
            u_own = qsend[level, rows, :]
            for m in range(1, members):
                u_own = u_own + urecvs[level][m - 1]
        else:
            u_own = u
        phase(f"b{level}_comb")
        abuf[...] = abuf[...] - dot3(ns[level][...], u_own, TN if level else NN)
        phase(f"b{level}_x")
        if level > 0:
            xpart[level] = pick_left(ptbuf[...], abuf[...], NN)
            size = box // members
            gathers = []
            for m in range(1, members):
                c = rcopy(xpart.at[level, span(rank_of(level, m), size), :], xrecvs[level].at[m - 1], slot(), member(m))
                go(c)
                gathers.append(c)
            phase(f"b{level}_xwait")
            for c in gathers:
                come(c)
            t_own = xpart[level, span(rank[level], size), :]
            for m in range(1, members):
                t_own = t_own + xrecvs[level][m - 1]
        else:
            ch, cl = halves(abuf[...])
            pt = ptbuf[...]
            out[0, 0] = product(ch, pt, TN) + product(cl, pt, TN)

    phase("drain")
    for when, c in pending:
        if when is None:
            c.wait_send()
        else:
            @pl.when(when)
            def _():
                c.wait_send()

    @pl.when(inner)
    def _():
        for k in has[3]:
            there, dev = neighbour(3, k)

            @pl.when(there)
            def _():
                rcopy(y3, yr3.at[OPPOSITE[k] - 1], s_y3[k], dev).wait_send()
                rcopy(q3.at[k - 1], qr3.at[OPPOSITE[k] - 1], s_q3[k], dev).wait_send()
        for m in range(1, 8):
            rcopy(x3.at[rank_of(3, m)], back3.at[own_part], s_x[m], member(m)).wait_send()
    phase(None)


def body(size_x, size_y, right_sides, skeleton_order, *weights):
    rows = right_sides.shape[2]
    box = right_sides.shape[3]
    skel = box // 2
    weights = [jnp.swapaxes(w, -1, -2) if w.shape[-1] < skel else w for w in weights]
    vm = lambda *shape: pltpu.VMEM(shape, F32)
    widths = [skel >> level for level in range(4)]
    share = rows // 4
    kinds = 5 if size_y > REACH[3][1] else 3
    lanes = -(-widths[2] // 128) * 128
    scratch = [
        vm(rows, box), pltpu.VMEM((4, box), jnp.int32), vm(skel, skel), vm(2, widths[1], skel), vm(4, widths[2], skel),
        vm(skel, skel), vm(widths[1], skel), vm(widths[2], skel),
        vm(5, skel, skel), vm(5, widths[1], skel), vm(5, widths[2], skel),
        vm(3, 5 * skel, rows), vm(2, box, rows), vm(3, 5 * skel, rows), vm(3, 4, skel, rows),
        vm(1, widths[1], rows), vm(3, widths[2], rows),
        vm(1, box // 2, rows), vm(3, box // 4, rows),
        vm(3, box, rows),
        vm(box, widths[0]), vm(widths[1], box), vm(widths[2], box),
        vm(box, rows), vm(3, skel, rows), vm(2, skel, rows),
        pltpu.VMEM((box, box), BF16), pltpu.VMEM((box, 8), jnp.int32),
        vm(3 + kinds, 8, widths[3], skel), vm(rows, lanes), vm(8, share, lanes),
        vm(share, skel), vm(kinds - 1, share, skel), vm(kinds - 1, share, skel), vm(kinds - 1, share, skel),
        vm(8, share, lanes), vm(rows, lanes), pltpu.VMEM((8 * lanes, box), BF16),
        pltpu.SemaphoreType.DMA((16,)),
        pltpu.SemaphoreType.DMA((160,)), pltpu.SemaphoreType.DMA((160,)),
    ]
    return pl.pallas_call(
        functools.partial(kernel, size_x, size_y),
        out_shape=jax.ShapeDtypeStruct(right_sides.shape, F32),
        in_specs=[pl.BlockSpec(memory_space=pl.ANY)] * (2 + len(weights)),
        out_specs=pl.BlockSpec(memory_space=pltpu.VMEM),
        scratch_shapes=scratch,
        compiler_params=pltpu.CompilerParams(
            collective_id=0, has_side_effects=True, vmem_limit_bytes=60 * 2**20
        ),
    )(right_sides, skeleton_order, *weights)


def solution(mesh):
    four = P("bx", "by", None, None)
    five = P("bx", "by", None, None, None)
    in_specs = (four,) * 10 + (five,) * 4 + (four,)
    return jax.shard_map(
        functools.partial(body, mesh.shape["bx"], mesh.shape["by"]),
        mesh=mesh, in_specs=in_specs, out_specs=four, check_vma=False,
    )
```

```python
import functools

import jax
import jax.numpy as jnp
from jax import lax
from jax.experimental import pallas as pl
from jax.experimental.pallas import tpu as pltpu
from jax.sharding import PartitionSpec as P

REACH = ((1, 1), (1, 2), (2, 2), (2, 4))
OPPOSITE = {1: 2, 2: 1, 3: 4, 4: 3}
F32 = jnp.float32
BF16 = jnp.bfloat16
MESH = pl.DeviceIdType.MESH
NN = (((1,), (0,)), ((), ()))
TN = (((0,), (0,)), ((), ()))
NT = (((1,), (1,)), ((), ()))


def halves(x):
    high = x.astype(BF16)
    return high, (x - high.astype(F32)).astype(BF16)


def product(a, b, dims):
    return lax.dot_general(a, b, dims, preferred_element_type=F32)


def dot3(a, b, dims):
    ah, al = halves(a)
    bh, bl = halves(b)
    return product(ah, bh, dims) + (product(ah, bl, dims) + product(al, bh, dims))


def pick_left(onehot, b, dims):
    bh, bl = halves(b)
    return product(onehot, bh, dims) + product(onehot, bl, dims)


def pick_right(a, onehot, dims):
    ah, al = halves(a)
    return product(ah, onehot, dims) + product(al, onehot, dims)


class Phases:
    def __init__(self):
        self.scope = None

    def __call__(self, name):
        if self.scope:
            self.scope.__exit__(None, None, None)
        self.scope = jax.named_scope(name) if name else None
        if self.scope:
            self.scope.__enter__()


def kernel(size_x, size_y, *refs):
    (rhs_in, order_in, t0_in, t1_in, t2_in, t3_in, g0_in, g1_in, g2_in, g3_in,
     k0_in, k1_in, k2_in, k3_in, root_in, out) = refs[:16]
    (rhs, order_row, t0, tg1, g0, g1, k0, k1,
     ybuf, vbuf, qsend, qrecv, urecv1, xrecv1, xpart, base0, base1,
     n0, n1, abuf, ypart, ssend, ptbuf, order_col,
     mid, turned, v2, y2, yr2, q2, qr2, x2, back2, pick2, turn2, t2,
     top, v3, y3, yr3, q3, qr3, x3, pick3, local, send, recv) = refs[16:]
    skel = t0.shape[0]
    box = 2 * skel
    rhs_count = ybuf.shape[2]
    half, share = v2.shape[1], v3.shape[1]
    kinds = top.shape[0] - 3
    phase = Phases()
    i, j = lax.axis_index("bx"), lax.axis_index("by")
    bits = (lax.rem(j, 2), lax.rem(i, 2), lax.rem(lax.div(j, 2), 2))
    inner = bits[0] != bits[2]
    outer = jnp.logical_not(inner)

    def flipped(b, m):
        return (1 - bits[b]) if m >> b & 1 else bits[b]

    def member(m):
        return (i + (flipped(1, m) - bits[1]), j + (flipped(0, m) - bits[0]) + 2 * (flipped(2, m) - bits[2]))

    def rank_of(level, m):
        rank = jnp.int32(0)
        for b in range(level):
            rank = rank + (1 << b) * flipped(b, m)
        return rank

    def span(start, size):
        return pl.ds(pl.multiple_of(start * size, size), size)

    def neighbour(level, k):
        rx, ry = REACH[level]
        if k == 1:
            return i >= rx, (i - rx, j)
        if k == 2:
            return i + rx < size_x, (i + rx, j)
        if k == 3:
            return j >= ry, (i, j - ry)
        return j + ry < size_y, (i, j + ry)

    has = [[k for k in (1, 2, 3, 4) if (REACH[l][0] < size_x if k < 3 else REACH[l][1] < size_y)] for l in range(4)]
    cross = [[k for k in has[l] if k < 3] for l in range(4)]
    along = [[k for k in has[l] if k > 2] for l in range(4)]

    count = [0]
    pending = []

    def slot():
        count[0] += 1
        return count[0] - 1

    def rcopy(src, dst, s, dev):
        return pltpu.make_async_remote_copy(src, dst, send.at[s], recv.at[s], device_id=dev, device_id_type=MESH)

    def go(c, when=None):
        make = c if callable(c) else lambda: c
        pending.append((when, make))
        if when is None:
            make().start()
        else:
            @pl.when(when)
            def _():
                make().start()

    def come(c, when=None):
        if when is None:
            c.wait_recv()
        else:
            @pl.when(when)
            def _():
                c.wait_recv()

    phase("start")
    rank = [rank_of(l, 0) for l in range(4)]
    loads = {}

    def load(name, src, dst):
        c = pltpu.make_async_copy(src, dst, local.at[len(loads)])
        loads[name] = c
        c.start()

    def need(*names):
        for name in names:
            loads[name].wait()

    load("order", order_in.at[0, 0], order_row)
    load("t0", t0_in.at[0, 0], t0)
    load("g0", g0_in.at[0, 0], g0)
    load("rhs", rhs_in.at[0, 0], rhs)
    load("t1", t1_in.at[0, 0], tg1.at[rank[1]])
    load("k0", k0_in.at[0, 0], k0)
    load("g1", g1_in.at[0, 0], g1)
    load("t2", t2_in.at[0, 0], mid.at[0, rank[2]])
    load("g2", g2_in.at[0, 0], mid.at[1, rank[2]])
    load("k2", k2_in.at[0, 0], mid.at[pl.ds(2, 5), rank[2]])
    load("t3", t3_in.at[0, 0], top.at[0, rank[3]])
    load("g3", g3_in.at[0, 0], top.at[1, rank[3]])
    load("root", root_in.at[0, 0], top.at[2, rank[3]])
    load("k3", k3_in.at[0, 0, pl.ds(0, kinds)], top.at[pl.ds(3, kinds), rank[3]])
    load("k1", k1_in.at[0, 0], k1)

    barrier = pltpu.get_barrier_semaphore()
    for m in range(1, 8):
        pl.semaphore_signal(barrier, 1, device_id=member(m), device_id_type=MESH)
    total = jnp.int32(7)
    greeted = set()
    for level in range(4):
        for k in has[level]:
            key = (k, REACH[level][0] if k < 3 else REACH[level][1])
            if key in greeted:
                continue
            greeted.add(key)
            there, dev = neighbour(level, k)

            @pl.when(there)
            def _():
                pl.semaphore_signal(barrier, 1, device_id=dev, device_id_type=MESH)
            total = total + there.astype(jnp.int32)

    for level in range(2):
        for k in (1, 2, 3, 4):
            there, _ = neighbour(level, k)

            @pl.when(jnp.logical_not(there))
            def _():
                ybuf[level, k * skel:(k + 1) * skel, :] = jnp.zeros((skel, rhs_count), F32)
                qrecv[level, k - 1] = jnp.zeros((skel, rhs_count), F32)
    turned[...] = jnp.zeros_like(turned)

    chunks = range((top.shape[0] + 1) // 2)
    slots_own, slots_in, slots_on = ([slot() for _ in chunks] for _ in range(3))
    slots_mate = [slot() for _ in range(4)]

    def chunk_copy(c, block, dev, s):
        at = pl.ds(2 * c, min(2, top.shape[0] - 2 * c))
        return rcopy(top.at[at, block], top.at[at, block], s, dev)

    def mate_copy(n, mine):
        block = rank_of(3, (0, 1, 5, 4)[n] ^ (0 if mine else 2))
        return rcopy(top.at[:, block], top.at[:, block], slots_mate[n], member(2))

    def outer_send(c):
        go(chunk_copy(c, rank[3], member(1), slots_own[c]), outer)

    def inner_send():
        for c in chunks:
            go(chunk_copy(c, rank[3], member(5), slots_in[c]), inner)

    def inner_forward(c):
        come(chunk_copy(c, rank_of(3, 1), member(1), slots_own[c]), inner)
        go(chunk_copy(c, rank_of(3, 1), member(5), slots_on[c]), inner)

    def mate_send(n):
        for c in chunks:
            if n == 2:
                come(chunk_copy(c, rank_of(3, 5), member(5), slots_in[c]), inner)
            if n == 3:
                come(chunk_copy(c, rank_of(3, 4), member(5), slots_on[c]), inner)
        go(lambda: mate_copy(n, True), inner)

    near = [None, None, None] + [neighbour(2, k)[0] for k in (1, 2, 3, 4)]
    slots_mid = [slot() for _ in near]
    slots_mid_own = [slot() for _ in near]
    slots_mid_on = [slot() for _ in near]

    near_in = [inner if there is None else jnp.logical_and(inner, there) for there in near]
    near_out = [outer if there is None else jnp.logical_and(outer, there) for there in near]

    def mid_copy(n, m, to, s):
        block = rank_of(2, m)
        return rcopy(mid.at[n, block], mid.at[n, block], s, member(to))

    def used(n):
        return n < 3 or n - 2 in has[2]

    def mid_send(*wanted):
        for n in filter(used, wanted):
            go(mid_copy(n, 0, 1, slots_mid[n]), near_in[n])

    def mid_share(*wanted):
        for n in filter(used, wanted):
            go(mid_copy(n, 0, 2, slots_mid_own[n]), near_out[n])

    def mid_forward(*wanted):
        for n in filter(used, wanted):
            come(mid_copy(n, 1, 1, slots_mid[n]), near_out[n])
            go(lambda n=n: mid_copy(n, 1, 2, slots_mid_on[n]), near_out[n])

    def mid_full(n):
        come(mid_copy(n, 2, 2, slots_mid_own[n]), near[n])
        come(mid_copy(n, 3, 2, slots_mid_on[n]), near[n])

    def onehot_pt(level):
        lanes = lax.broadcasted_iota(jnp.int32, (box, box), 1)
        return jnp.where(lanes == order_col[:, level:level + 1], 1.0, 0.0).astype(BF16)

    def onehot_p(level):
        rows = lax.broadcasted_iota(jnp.int32, (box, box), 0)
        return jnp.where(rows == order_row[level:level + 1, :], 1.0, 0.0).astype(BF16)

    def make_n(level):
        if level == 0:
            need("t0", "g0")
            n0[:skel, :] = -dot3(t0[...], g0[...], NN)
            n0[skel:, :] = g0[...]
            return
        need("g1")
        n1[:, :skel] = -dot3(g1[...], tg1[...].reshape(skel, skel), NN)
        n1[:, skel:] = g1[...]

    need("order")
    order_f = order_row[...].astype(F32)
    order_f = jnp.concatenate([order_f, jnp.zeros((8 - order_f.shape[0], box), F32)], axis=0)
    order_col[...] = order_f.T.astype(jnp.int32)

    phase("f0_make")
    make_n(0)
    phase("f0_a")
    need("rhs")
    abuf[...] = pick_left(onehot_pt(0), rhs[...], NT)
    phase("f0_y")
    y_own = dot3(n0[...], abuf[...], TN)
    ybuf[0, :skel, :] = y_own
    ypart[0] = y_own
    phase("f0_barrier")
    pl.semaphore_wait(barrier, total)
    phase("f0_send")
    slots_y0 = {k: slot() for k in has[0]}
    for k in along[0] + cross[0]:
        there, dev = neighbour(0, k)
        far = OPPOSITE[k]
        go(rcopy(ypart.at[0], ybuf.at[0, pl.ds(far * skel, skel), :], slots_y0[k], dev), there)
    need("t1")
    t1_copy = rcopy(tg1.at[rank[1]], tg1.at[rank[1]], slot(), member(1))
    go(t1_copy)
    need("t3", "g3", "root", "k3")
    inner_send()
    mate_send(0)
    phase("f0_s")
    need("k0")
    s_own = abuf[:skel, :] - dot3(k0[0], ypart[0], TN)
    ptbuf[...] = onehot_pt(1)
    for k in cross[0] + along[0]:
        there, dev = neighbour(0, k)
        phase(f"f0_wait{k}")
        come(rcopy(ypart.at[0], ybuf.at[0, pl.ds(k * skel, skel), :], slots_y0[OPPOSITE[k]], dev), there)
        phase(f"f0_s{k}")
        s_own = s_own - dot3(k0[k], ybuf[0, k * skel:(k + 1) * skel, :], TN)
    ssend[0] = s_own
    vbuf[span(rank[1], skel), :] = s_own
    give = rcopy(ssend.at[0], vbuf.at[span(rank[1], skel), :], slot(), member(1))
    go(give)
    need("t2", "g2", "k2")
    mid_send(0)
    mid_share(*range(7))
    outer_send(0)
    base0[:skel, :] = -dot3(t0[...], ypart[0], NN)
    base0[skel:, :] = ypart[0]
    phase("f0_n1")
    come(t1_copy)
    make_n(1)
    phase("f0_gwait")
    come(give)

    phase("f1_a")
    cols = skel >> 1
    rows = span(rank[1], cols)
    abuf[...] = pick_left(ptbuf[...], vbuf[...], NN)
    phase("f1_y")
    y_own = dot3(n1[...], abuf[...], NN)
    ypart[1, :cols, :] = y_own
    ybuf[1, rows, :] = y_own

    def at(k, m):
        return ybuf.at[1, pl.ds(pl.multiple_of(k * skel + rank_of(1, m) * cols, cols), cols), :]

    own_src = ypart.at[1, pl.ds(0, cols), :]
    s_a = slot()
    s_c = {k: [slot(), slot()] for k in cross[1]}
    s_b = {k: slot() for k in along[1]}
    s_d = {k: slot() for k in along[1]}
    phase("f1_send")
    mate = rcopy(own_src, at(0, 0), s_a, member(1))
    go(mate)
    for k in along[1]:
        there, dev = neighbour(1, k)
        go(rcopy(own_src, at(OPPOSITE[k], 0), s_b[k], dev), there)
    for k in cross[1]:
        there, dev = neighbour(1, k)
        go(rcopy(own_src, at(OPPOSITE[k], 0), s_c[k][0], dev), there)
    mid_send(1)
    outer_send(1)
    base1[:skel, :] = -dot3(tg1[rank[1]], y_own, TN)
    base1[skel:, :] = jnp.zeros((skel, rhs_count), F32)
    base1[pl.ds(pl.multiple_of(skel + rank[1] * cols, cols), cols), :] = y_own
    phase("f1_ywait")
    come(mate)
    for k in cross[1]:
        there, dev = neighbour(1, k)
        go(rcopy(at(0, 1), at(OPPOSITE[k], 1), s_c[k][1], dev), there)
    inner_forward(0)
    mid_forward(0)
    phase("f1_s0")
    need("k1")
    s_own = abuf[rows, :] - dot3(k1[0], ybuf[1, :skel, :], NN)
    phase("f1_relay")
    for k in cross[1]:
        there, dev = neighbour(1, k)
        come(rcopy(own_src, at(k, 0), s_c[OPPOSITE[k]][0], dev), there)
    for k in along[1]:
        there, dev = neighbour(1, k)
        come(rcopy(own_src, at(k, 0), s_b[OPPOSITE[k]], dev), there)
        go(rcopy(at(k, 0), at(k, 0), s_d[k], member(1)), there)
    mid_send(2)
    for k in cross[1]:
        there, dev = neighbour(1, k)
        phase(f"f1_cross{k}")
        come(rcopy(own_src, at(k, 1), s_c[OPPOSITE[k]][1], dev), there)
        s_own = s_own - dot3(k1[k], ybuf[1, k * skel:(k + 1) * skel, :], NN)
    for k in along[1]:
        there, dev = neighbour(1, k)
        phase(f"f1_along{k}")
        come(rcopy(at(k, 1), at(k, 1), s_d[k], member(1)), there)
        s_own = s_own - dot3(k1[k], ybuf[1, k * skel:(k + 1) * skel, :], NN)
    turned[:, :cols] = s_own.T

    phase("l2_send")
    s_t2 = [slot() for _ in range(4)]
    half_of = lambda m: span(flipped(1, m), half)
    go(rcopy(turned.at[half_of(1)], v2.at[rank[2]], s_t2[1], member(1)), inner)
    go(rcopy(turned.at[half_of(3)], v2.at[rank[2]], s_t2[3], member(3)), inner)
    go(rcopy(turned.at[half_of(2)], v2.at[rank[2]], s_t2[2], member(2)), outer)
    mid_send(3, 4, 5, 6)
    outer_send(2)
    inner_forward(1)
    inner_forward(2)

    def wide_pick(pick, level, width, lanes):
        o = order_row[level:level + 1, :]
        o = o + sum((lanes - width) * (o >= width * b).astype(jnp.int32) for b in range(1, box // width))
        lines = lax.broadcasted_iota(jnp.int32, pick.shape, 0)
        pick[...] = jnp.where(lines == o, 1.0, 0.0).astype(BF16)

    def beside(k):
        there, (to_i, to_j) = neighbour(2, k)
        if k > 2:
            step = 1 + 2 * (1 - bits[2]) if k == 4 else -(1 + 2 * bits[2])
            to_i, to_j = i, j + step
        return there, (to_i, to_j)

    s_y2 = {k: slot() for k in has[2]}
    s_q2 = {k: slot() for k in has[2]}
    s_t3 = {m: slot() for m in (1, 4)}
    s_x3 = {m: slot() for m in (1, 4)}
    s_x2 = {m: slot() for m in (1, 2, 3)}
    s_y3 = {k: slot() for k in has[3]}
    s_q3 = {k: slot() for k in has[3]}
    quarter_of = lambda m: span(flipped(2, m), share)
    y2_copy = lambda k: rcopy(y2, yr2.at[OPPOSITE[k] - 1], s_y2[k], beside(k)[1])
    q2_copy = lambda k: rcopy(q2.at[k - 1], qr2.at[OPPOSITE[k] - 1], s_q2[k], beside(k)[1])
    y3_copy = lambda k: rcopy(y3, yr3.at[OPPOSITE[k] - 1], s_y3[k], neighbour(3, k)[1])
    q3_copy = lambda k: rcopy(q3.at[k - 1], qr3.at[OPPOSITE[k] - 1], s_q3[k], neighbour(3, k)[1])
    up_copy = lambda m: rcopy(turn2.at[quarter_of(m)], v3.at[bits[2]], s_t3[m], member(m))
    down_copy = lambda m: rcopy(x3.at[flipped(2, m)], t2.at[quarter_of(0)], s_x3[m], member(m))
    out_copy = lambda m: rcopy(x2.at[rank_of(2, m)], back2.at[half_of(0)], s_x2[m], member(m))

    @pl.when(outer)
    def _():
        phase("l2_pick")
        wide_pick(pick2, 2, cols, turned.shape[1])
        mid_forward(1)
        v2[rank[2]] = turned[half_of(0), :]
        phase("l2_in")
        come(rcopy(turned.at[half_of(0)], v2.at[rank_of(2, 2)], s_t2[2], member(2)))
        come(rcopy(turned.at[half_of(0)], v2.at[rank_of(2, 1)], s_t2[1], member(1)))
        come(rcopy(turned.at[half_of(0)], v2.at[rank_of(2, 3)], s_t2[3], member(3)))
        phase("l2_a")
        full = lambda n: mid[n].reshape(skel, skel)
        a = pick_right(jnp.concatenate([v2[b] for b in range(4)], axis=1), pick2[...], NN)
        s0, r0 = a[:, :skel], a[:, skel:]
        phase("l2_y")
        mid_full(0)
        mid_full(1)
        y = dot3(r0 - dot3(s0, full(0), NT), full(1), NT)
        y2[...] = y
        for k in has[2]:
            @pl.when(beside(k)[0])
            def _():
                y2_copy(k).start()
        phase("l2_s")
        mid_forward(2)
        mid_full(2)
        turn2[...] = s0 - dot3(y, full(2), NT)
        for k in has[2]:
            mid_forward(2 + k)
        for k in has[2]:
            phase(f"l2_s{k}")

            @pl.when(beside(k)[0])
            def _():
                mid_full(2 + k)
                rcopy(y2, yr2.at[k - 1], s_y2[OPPOSITE[k]], beside(k)[1]).wait_recv()
                turn2[...] = turn2[...] - dot3(yr2[k - 1], full(2 + k), NT)
        for m in (4, 1):
            up_copy(m).start()
        phase(None)

    @pl.when(inner)
    def _():
        phase("l3_pick")
        wide_pick(pick3, 3, skel, skel)
        for n in (1, 2, 3):
            mate_send(n)
        for n in range(4):
            come(mate_copy(n, False))
        phase("l3_in")
        for m in (1, 4):
            come(rcopy(turn2.at[quarter_of(0)], v3.at[flipped(2, m)], s_t3[m], member(m)))
        full = lambda n: top[n].reshape(skel, skel)
        phase("l3_y")
        a = pick_right(jnp.concatenate([v3[0], v3[1]], axis=1), pick3[...], NN)
        s0, r0 = a[:, :skel], a[:, skel:]
        y = dot3(r0 - dot3(s0, full(0), NT), full(1), NT)
        y3[...] = y
        for k in has[3]:
            @pl.when(neighbour(3, k)[0])
            def _():
                y3_copy(k).start()
        phase("l3_s")
        v3[0] = s0 - dot3(y, full(3), NT)
        for k in has[3]:
            phase(f"l3_s{k}")

            @pl.when(neighbour(3, k)[0])
            def _():
                rcopy(y3, yr3.at[k - 1], s_y3[OPPOSITE[k]], neighbour(3, k)[1]).wait_recv()
                v3[0] = v3[0] - dot3(yr3[k - 1], full(3 + k), NT)
        phase("l3_q")
        t = dot3(v3[0], full(2), NT)
        for k in has[3]:
            @pl.when(neighbour(3, k)[0])
            def _():
                q3[k - 1] = dot3(t, full(3 + k), NN)
                q3_copy(k).start()
        v3[0] = dot3(t, full(3), NN)
        for k in has[3]:
            phase(f"l3_u{k}")

            @pl.when(neighbour(3, k)[0])
            def _():
                rcopy(q3.at[k - 1], qr3.at[k - 1], s_q3[OPPOSITE[k]], neighbour(3, k)[1]).wait_recv()
                v3[0] = v3[0] + qr3[k - 1]
        phase("l3_x")
        xr = y - dot3(v3[0], full(1), NN)
        xs = t - dot3(xr, full(0), NN)
        xv = pick_right(jnp.concatenate([xs, xr], axis=1), pick3[...], NT)
        x3[0], x3[1] = xv[:, :skel], xv[:, skel:]
        for m in (4, 1):
            down_copy(m).start()
        phase(None)

    @pl.when(outer)
    def _():
        phase("l2_tin")
        for m in (1, 4):
            come(rcopy(x3.at[bits[2]], t2.at[quarter_of(m)], s_x3[m], member(m)))
        full = lambda n: mid[n].reshape(skel, skel)
        phase("l2_q")
        t = t2[...]
        for k in reversed(has[2]):
            @pl.when(beside(k)[0])
            def _():
                q2[k - 1] = dot3(t, full(2 + k), NN)
                q2_copy(k).start()
        yr2[0] = dot3(t, full(2), NN)
        for k in has[2]:
            phase(f"l2_u{k}")

            @pl.when(beside(k)[0])
            def _():
                rcopy(q2.at[k - 1], qr2.at[k - 1], s_q2[OPPOSITE[k]], beside(k)[1]).wait_recv()
                yr2[0] = yr2[0] + qr2[k - 1]
        phase("l2_x")
        xr = y2[...] - dot3(yr2[0], full(1), NN)
        xs = t - dot3(xr, full(0), NN)
        xv = pick_right(jnp.concatenate([xs, xr], axis=1), pick2[...], NT)
        wide = turned.shape[1]
        for b in range(4):
            x2[b] = xv[:, b * wide:(b + 1) * wide]
        for m in (3, 1, 2):
            out_copy(m).start()
        back2[half_of(0), :] = x2[rank[2]]
        phase(None)

    phase("l2_out")
    ptbuf[...] = onehot_p(1)
    come(rcopy(x2.at[rank[2]], back2.at[half_of(2)], s_x2[2], member(2)), outer)
    for m in (1, 3):
        come(rcopy(x2.at[rank[2]], back2.at[half_of(m)], s_x2[m], member(m)), inner)
    t_own = back2[...].T[:skel >> 1]

    for level in (1, 0):
        phase(f"b{level}_q")
        cols = skel >> level
        rows = span(rank[level], cols)
        s_q = {k: slot() for k in has[level]}
        for k in along[level] + cross[level]:
            at_k = pl.ds(k * skel, skel)
            qsend[level, at_k, :] = dot3(k1[k], t_own, TN) if level else dot3(k0[k], t_own, NN)
            there, dev = neighbour(level, k)
            go(rcopy(qsend.at[level, at_k, :], qrecv.at[level, OPPOSITE[k] - 1], s_q[k], dev), there)
        u = dot3(k1[0], t_own, TN) if level else dot3(k0[0], t_own, NN)
        phase(f"b{level}_t")
        if level == 0:
            abuf[...] = base0[...]
            abuf[:skel, :] = abuf[:skel, :] + t_own
            ptbuf[...] = onehot_pt(0)
        else:
            abuf[...] = base1[...]
            abuf[rows, :] = abuf[rows, :] + t_own
        for k in cross[level] + along[level]:
            phase(f"b{level}_wait{k}")
            there, dev = neighbour(level, k)
            come(rcopy(qsend.at[level, pl.ds(k * skel, skel), :], qrecv.at[level, k - 1], s_q[OPPOSITE[k]], dev), there)
        phase(f"b{level}_u")
        u = u + ((qrecv[level, 0] + qrecv[level, 1]) + (qrecv[level, 2] + qrecv[level, 3]))
        if level > 0:
            qsend[level, :skel, :] = u
            c = rcopy(qsend.at[level, span(rank_of(level, 1), cols), :], urecv1.at[0], slot(), member(1))
            go(c)
            come(c)
            u = qsend[level, rows, :] + urecv1[0]
        phase(f"b{level}_comb")
        abuf[...] = abuf[...] - (dot3(n1[...], u, TN) if level else dot3(n0[...], u, NN))
        phase(f"b{level}_x")
        if level > 0:
            xpart[...] = pick_left(ptbuf[...], abuf[...], NN)
            c = rcopy(xpart.at[span(rank_of(level, 1), skel), :], xrecv1.at[0], slot(), member(1))
            go(c)
            phase(f"b{level}_xwait")
            come(c)
            t_own = xpart[span(rank[level], skel), :] + xrecv1[0]
        else:
            ch, cl = halves(abuf[...])
            pt = ptbuf[...]
            out[0, 0] = product(ch, pt, TN) + product(cl, pt, TN)

    phase("drain")
    for when, make in pending:
        if when is None:
            make().wait_send()
        else:
            @pl.when(when)
            def _():
                make().wait_send()

    @pl.when(inner)
    def _():
        for k in has[3]:
            @pl.when(neighbour(3, k)[0])
            def _():
                y3_copy(k).wait_send()
                q3_copy(k).wait_send()
        for m in (4, 1):
            down_copy(m).wait_send()

    @pl.when(outer)
    def _():
        for k in has[2]:
            @pl.when(beside(k)[0])
            def _():
                y2_copy(k).wait_send()
                q2_copy(k).wait_send()
        for m in (4, 1):
            up_copy(m).wait_send()
        for m in (3, 1, 2):
            out_copy(m).wait_send()
    phase(None)


def body(size_x, size_y, right_sides, skeleton_order, *weights):
    rows = right_sides.shape[2]
    box = right_sides.shape[3]
    skel = box // 2
    weights = [jnp.swapaxes(w, -1, -2) if w.shape[-1] < skel else w for w in weights]
    vm = lambda *shape: pltpu.VMEM(shape, F32)
    widths = [skel >> level for level in range(4)]
    half, share = rows // 2, rows // 4
    kinds = 5 if size_y > REACH[3][1] else 3
    lanes = -(-widths[1] // 128) * 128
    scratch = [
        vm(rows, box), pltpu.VMEM((4, box), jnp.int32), vm(skel, skel), vm(2, widths[1], skel),
        vm(skel, skel), vm(widths[1], skel), vm(5, skel, skel), vm(5, widths[1], skel),
        vm(2, 5 * skel, rows), vm(box, rows), vm(2, 5 * skel, rows), vm(2, 4, skel, rows),
        vm(1, widths[1], rows), vm(1, skel, rows), vm(box, rows), vm(box, rows), vm(box, rows),
        vm(box, skel), vm(widths[1], box),
        vm(box, rows), vm(2, skel, rows), vm(1, skel, rows),
        pltpu.VMEM((box, box), BF16), pltpu.VMEM((box, 8), jnp.int32),
        vm(7, 4, widths[2], skel), vm(rows, lanes), vm(4, half, lanes),
        vm(half, skel), vm(4, half, skel), vm(4, half, skel), vm(4, half, skel),
        vm(4, half, lanes), vm(rows, lanes), pltpu.VMEM((4 * lanes, box), BF16), vm(half, skel), vm(half, skel),
        vm(3 + kinds, 8, widths[3], skel), vm(2, share, skel),
        vm(share, skel), vm(kinds - 1, share, skel), vm(kinds - 1, share, skel), vm(kinds - 1, share, skel),
        vm(2, share, skel), pltpu.VMEM((box, box), BF16),
        pltpu.SemaphoreType.DMA((16,)),
        pltpu.SemaphoreType.DMA((128,)), pltpu.SemaphoreType.DMA((128,)),
    ]
    return pl.pallas_call(
        functools.partial(kernel, size_x, size_y),
        out_shape=jax.ShapeDtypeStruct(right_sides.shape, F32),
        in_specs=[pl.BlockSpec(memory_space=pl.ANY)] * (2 + len(weights)),
        out_specs=pl.BlockSpec(memory_space=pltpu.VMEM),
        scratch_shapes=scratch,
        compiler_params=pltpu.CompilerParams(
            collective_id=0, has_side_effects=True, vmem_limit_bytes=60 * 2**20
        ),
    )(right_sides, skeleton_order, *weights)


def solution(mesh):
    four = P("bx", "by", None, None)
    five = P("bx", "by", None, None, None)
    in_specs = (four,) * 10 + (five,) * 4 + (four,)
    return jax.shard_map(
        functools.partial(body, mesh.shape["bx"], mesh.shape["by"]),
        mesh=mesh, in_specs=in_specs, out_specs=four, check_vma=False,
    )
```

```python
import functools

import jax
import jax.numpy as jnp
from jax import lax
from jax.experimental import pallas as pl
from jax.experimental.pallas import tpu as pltpu
from jax.sharding import PartitionSpec as P

REACH = ((1, 1), (1, 2), (2, 2), (2, 4))
OPPOSITE = {1: 2, 2: 1, 3: 4, 4: 3}
F32 = jnp.float32
BF16 = jnp.bfloat16
MESH = pl.DeviceIdType.MESH
NN = (((1,), (0,)), ((), ()))
TN = (((0,), (0,)), ((), ()))
NT = (((1,), (1,)), ((), ()))


def halves(x):
    high = x.astype(BF16)
    return high, (x - high.astype(F32)).astype(BF16)


def product(a, b, dims):
    return lax.dot_general(a, b, dims, preferred_element_type=F32)


def dot3(a, b, dims):
    ah, al = halves(a)
    bh, bl = halves(b)
    return product(ah, bh, dims) + (product(ah, bl, dims) + product(al, bh, dims))


def lanes_summed(x):
    wide = x.shape[1] // 2
    return x[:, :wide] + x[:, wide:]


def rows_summed(x):
    tall = x.shape[0] // 2
    return x[:tall] + x[tall:]


def dot_left(a, b, dims):
    ah, al = halves(a)
    bh, bl = halves(b)
    return lanes_summed(product(ah, jnp.concatenate([bh, bl], axis=1), dims)) + product(al, bh, dims)


def dot_right(a, b, dims):
    ah, al = halves(a)
    bh, bl = halves(b)
    return rows_summed(product(jnp.concatenate([ah, al], axis=0), bh, dims)) + product(ah, bl, dims)


def pick_left(onehot, b, dims):
    return lanes_summed(product(onehot, jnp.concatenate(halves(b), axis=1 if dims == NN else 0), dims))


def pick_right(a, onehot, dims):
    if dims == TN:
        return rows_summed(product(jnp.concatenate(halves(a), axis=1), onehot, dims))
    return rows_summed(product(jnp.concatenate(halves(a), axis=0), onehot, dims))


class Phases:
    def __init__(self):
        self.scope = None

    def __call__(self, name):
        if self.scope:
            self.scope.__exit__(None, None, None)
        self.scope = jax.named_scope(name) if name else None
        if self.scope:
            self.scope.__enter__()


def kernel(size_x, size_y, *refs):
    (rhs_in, order_in, t0_in, t1_in, t2_in, t3_in, g0_in, g1_in, g2_in, g3_in,
     k0_in, k1_in, k2_in, k3_in, root_in, out) = refs[:16]
    (rhs, order_row, t0, tg1, g0, g1, k0, k1,
     ybuf, vbuf, qsend, qrecv, urecv1, xrecv1, xpart, base1,
     n1, abuf, ypart, ssend, ptbuf, order_col, wbuf, wpart, kmate, kturn, krows, tfull, nsend, nrecv,
     mid, turned, v2, y2, yr2, q2, qr2, x2, back2, pick2, turn2, t2,
     top, v3, y3, yr3, q3, qr3, x3, pick3, local, send, recv) = refs[16:]
    skel = t0.shape[0]
    box = 2 * skel
    rhs_count = ybuf.shape[2]
    half, share = v2.shape[1], v3.shape[1]
    kinds = top.shape[0] - 3
    phase = Phases()
    i, j = lax.axis_index("bx"), lax.axis_index("by")
    bits = (lax.rem(j, 2), lax.rem(i, 2), lax.rem(lax.div(j, 2), 2))
    inner = bits[0] != bits[2]
    outer = jnp.logical_not(inner)

    def flipped(b, m):
        return (1 - bits[b]) if m >> b & 1 else bits[b]

    def member(m):
        return (i + (flipped(1, m) - bits[1]), j + (flipped(0, m) - bits[0]) + 2 * (flipped(2, m) - bits[2]))

    def rank_of(level, m):
        rank = jnp.int32(0)
        for b in range(level):
            rank = rank + (1 << b) * flipped(b, m)
        return rank

    def span(start, size):
        return pl.ds(pl.multiple_of(start * size, size), size)

    def neighbour(level, k):
        rx, ry = REACH[level]
        if k == 1:
            return i >= rx, (i - rx, j)
        if k == 2:
            return i + rx < size_x, (i + rx, j)
        if k == 3:
            return j >= ry, (i, j - ry)
        return j + ry < size_y, (i, j + ry)

    has = [[k for k in (1, 2, 3, 4) if (REACH[l][0] < size_x if k < 3 else REACH[l][1] < size_y)] for l in range(4)]
    cross = [[k for k in has[l] if k < 3] for l in range(4)]
    along = [[k for k in has[l] if k > 2] for l in range(4)]

    count = [0]
    pending = []

    def slot():
        count[0] += 1
        return count[0] - 1

    def rcopy(src, dst, s, dev):
        return pltpu.make_async_remote_copy(src, dst, send.at[s], recv.at[s], device_id=dev, device_id_type=MESH)

    def go(c, when=None):
        make = c if callable(c) else lambda: c
        pending.append((when, make))
        if when is None:
            make().start()
        else:
            @pl.when(when)
            def _():
                make().start()

    def come(c, when=None):
        if when is None:
            c.wait_recv()
        else:
            @pl.when(when)
            def _():
                c.wait_recv()

    phase("start")
    rank = [rank_of(l, 0) for l in range(4)]
    loads = {}

    def load(name, src, dst):
        c = pltpu.make_async_copy(src, dst, local.at[len(loads)])
        loads[name] = c
        c.start()

    def need(*names):
        for name in names:
            loads[name].wait()

    load("order", order_in.at[0, 0], order_row)
    load("t0", t0_in.at[0, 0], t0)
    load("g0", g0_in.at[0, 0], g0)
    load("rhs", rhs_in.at[0, 0], rhs)
    load("t1", t1_in.at[0, 0], tg1.at[rank[1]])
    load("k0", k0_in.at[0, 0], k0)
    load("g1", g1_in.at[0, 0], g1)
    load("t2", t2_in.at[0, 0], mid.at[0, rank[2]])
    load("g2", g2_in.at[0, 0], mid.at[1, rank[2]])
    load("k2", k2_in.at[0, 0], mid.at[pl.ds(2, 5), rank[2]])
    load("t3", t3_in.at[0, 0], top.at[0, rank[3]])
    load("g3", g3_in.at[0, 0], top.at[1, rank[3]])
    load("root", root_in.at[0, 0], top.at[2, rank[3]])
    load("k3", k3_in.at[0, 0, pl.ds(0, kinds)], top.at[pl.ds(3, kinds), rank[3]])
    load("k1", k1_in.at[0, 0], k1)

    barrier = pltpu.get_barrier_semaphore()
    for m in range(1, 8):
        pl.semaphore_signal(barrier, 1, device_id=member(m), device_id_type=MESH)
    total = jnp.int32(7)
    greeted = set()
    for level in range(4):
        for k in has[level]:
            key = (k, REACH[level][0] if k < 3 else REACH[level][1])
            if key in greeted:
                continue
            greeted.add(key)
            there, dev = neighbour(level, k)

            @pl.when(there)
            def _():
                pl.semaphore_signal(barrier, 1, device_id=dev, device_id_type=MESH)
            total = total + there.astype(jnp.int32)

    for level in range(2):
        for k in (1, 2, 3, 4):
            there, _ = neighbour(level, k)

            @pl.when(jnp.logical_not(there))
            def _():
                ybuf[level, k * skel:(k + 1) * skel, :] = jnp.zeros((skel, rhs_count), F32)
                qrecv[level, k - 1] = jnp.zeros((skel, rhs_count), F32)
    for k in along[1]:
        there, _ = neighbour(1, k)

        @pl.when(jnp.logical_not(there))
        def _():
            nrecv[k - 3] = jnp.zeros(nrecv.shape[1:], F32)
    turned[...] = jnp.zeros_like(turned)

    chunks = range((top.shape[0] + 1) // 2)
    slots_own, slots_in, slots_on = ([slot() for _ in chunks] for _ in range(3))
    slots_mate = [slot() for _ in range(4)]

    def chunk_copy(c, block, dev, s):
        at = pl.ds(2 * c, min(2, top.shape[0] - 2 * c))
        return rcopy(top.at[at, block], top.at[at, block], s, dev)

    def mate_copy(n, mine):
        block = rank_of(3, (0, 1, 5, 4)[n] ^ (0 if mine else 2))
        return rcopy(top.at[:, block], top.at[:, block], slots_mate[n], member(2))

    def outer_send(c):
        go(chunk_copy(c, rank[3], member(1), slots_own[c]), outer)

    def inner_send():
        for c in chunks:
            go(chunk_copy(c, rank[3], member(5), slots_in[c]), inner)

    def inner_forward(c):
        come(chunk_copy(c, rank_of(3, 1), member(1), slots_own[c]), inner)
        go(chunk_copy(c, rank_of(3, 1), member(5), slots_on[c]), inner)

    def mate_send(n):
        for c in chunks:
            if n == 2:
                come(chunk_copy(c, rank_of(3, 5), member(5), slots_in[c]), inner)
            if n == 3:
                come(chunk_copy(c, rank_of(3, 4), member(5), slots_on[c]), inner)
        go(lambda: mate_copy(n, True), inner)

    near = [None, None, None] + [neighbour(2, k)[0] for k in (1, 2, 3, 4)]
    slots_mid = [slot() for _ in near]
    slots_mid_own = [slot() for _ in near]
    slots_mid_on = [slot() for _ in near]

    near_in = [inner if there is None else jnp.logical_and(inner, there) for there in near]
    near_out = [outer if there is None else jnp.logical_and(outer, there) for there in near]

    def mid_copy(n, m, to, s):
        block = rank_of(2, m)
        return rcopy(mid.at[n, block], mid.at[n, block], s, member(to))

    def used(n):
        return n < 3 or n - 2 in has[2]

    def mid_send(*wanted):
        for n in filter(used, wanted):
            go(mid_copy(n, 0, 1, slots_mid[n]), near_in[n])

    def mid_share(*wanted):
        for n in filter(used, wanted):
            go(mid_copy(n, 0, 2, slots_mid_own[n]), near_out[n])

    def mid_forward(*wanted):
        for n in filter(used, wanted):
            come(mid_copy(n, 1, 1, slots_mid[n]), near_out[n])
            go(lambda n=n: mid_copy(n, 1, 2, slots_mid_on[n]), near_out[n])

    def mid_full(n):
        come(mid_copy(n, 2, 2, slots_mid_own[n]), near[n])
        come(mid_copy(n, 3, 2, slots_mid_on[n]), near[n])

    def onehot_pt(level):
        lanes = lax.broadcasted_iota(jnp.int32, (box, box), 1)
        return jnp.where(lanes == order_col[:, level:level + 1], 1.0, 0.0).astype(BF16)

    def onehot_p(level):
        rows = lax.broadcasted_iota(jnp.int32, (box, box), 0)
        return jnp.where(rows == order_row[level:level + 1, :], 1.0, 0.0).astype(BF16)

    need("order")
    order_f = order_row[...].astype(F32)
    order_f = jnp.concatenate([order_f, jnp.zeros((8 - order_f.shape[0], box), F32)], axis=0)
    order_col[...] = order_f.T.astype(jnp.int32)

    phase("f0_a")
    need("rhs")
    abuf[...] = pick_left(onehot_pt(0), rhs[...], NT)
    phase("f0_y")
    need("t0", "g0")
    y_own = dot_left(g0[...], abuf[skel:, :] - dot_left(t0[...], abuf[:skel, :], TN), TN)
    ybuf[0, :skel, :] = y_own
    ypart[0] = y_own
    phase("f0_barrier")
    pl.semaphore_wait(barrier, total)
    phase("f0_send")
    slots_y0 = {k: slot() for k in has[0]}
    for k in along[0] + cross[0]:
        there, dev = neighbour(0, k)
        far = OPPOSITE[k]
        go(rcopy(ypart.at[0], ybuf.at[0, pl.ds(far * skel, skel), :], slots_y0[k], dev), there)
    need("t2", "g2", "k2", "t3", "g3", "root", "k3")
    mid_send(0)
    outer_send(0)
    inner_send()
    mate_send(0)
    phase("f0_s")
    need("k0")
    s_own = abuf[:skel, :] - dot_left(k0[0], ypart[0], TN)
    ptbuf[...] = onehot_pt(1)
    for k in cross[0] + along[0]:
        there, dev = neighbour(0, k)
        phase(f"f0_wait{k}")
        come(rcopy(ypart.at[0], ybuf.at[0, pl.ds(k * skel, skel), :], slots_y0[OPPOSITE[k]], dev), there)
        phase(f"f0_s{k}")
        s_own = s_own - dot_left(k0[k], ybuf[0, k * skel:(k + 1) * skel, :], TN)
    ssend[0] = s_own
    vbuf[span(rank[1], skel), :] = s_own
    give = rcopy(ssend.at[0], vbuf.at[span(rank[1], skel), :], slot(), member(1))
    go(give)
    mid_send(1)
    outer_send(1)
    mid_share(*range(7))
    phase("f0_gwait")
    need("t1", "g1", "k1")
    come(give)

    phase("f1_a")
    cols = skel >> 1
    rows = span(rank[1], cols)
    abuf[...] = pick_left(ptbuf[...], vbuf[...], NN)
    phase("f1_w")
    w_own = abuf[pl.ds(pl.multiple_of(skel + rank[1] * cols, cols), cols), :] - dot_left(tg1[rank[1]], abuf[:skel, :], NN)
    wpart[...] = w_own
    wbuf[rows, :] = w_own
    give_w = rcopy(wpart, wbuf.at[rows, :], slot(), member(1))
    go(give_w)
    ptbuf[...] = onehot_p(1)
    phase("f1_wwait")
    come(give_w)
    phase("f1_y")
    y_own = dot_left(g1[...], wbuf[...], NN)
    ypart[1, :cols, :] = y_own
    ybuf[1, rows, :] = y_own

    def at(k, m):
        return ybuf.at[1, pl.ds(pl.multiple_of(k * skel + rank_of(1, m) * cols, cols), cols), :]

    own_src = ypart.at[1, pl.ds(0, cols), :]
    s_a = slot()
    s_c = {k: [slot(), slot()] for k in cross[1]}
    s_b = {k: slot() for k in along[1]}
    s_d = {k: slot() for k in along[1]}
    phase("f1_send")
    mate = rcopy(own_src, at(0, 0), s_a, member(1))
    go(mate)
    for k in along[1]:
        there, dev = neighbour(1, k)
        go(rcopy(own_src, at(OPPOSITE[k], 0), s_b[k], dev), there)
    for k in cross[1]:
        there, dev = neighbour(1, k)
        go(rcopy(own_src, at(OPPOSITE[k], 0), s_c[k][0], dev), there)
    mid_send(2)
    outer_send(2)
    base1[:skel, :] = -dot_left(tg1[rank[1]], y_own, TN)
    base1[skel:, :] = jnp.zeros((skel, rhs_count), F32)
    base1[pl.ds(pl.multiple_of(skel + rank[1] * cols, cols), cols), :] = y_own
    phase("f1_ywait")
    come(mate)
    for k in cross[1]:
        there, dev = neighbour(1, k)
        go(rcopy(at(0, 1), at(OPPOSITE[k], 1), s_c[k][1], dev), there)
    inner_forward(0)
    mid_forward(0)
    phase("f1_s0")
    s_own = abuf[rows, :] - dot_left(k1[0], ybuf[1, :skel, :], NN)
    phase("f1_relay")
    for k in cross[1]:
        there, dev = neighbour(1, k)
        come(rcopy(own_src, at(k, 0), s_c[OPPOSITE[k]][0], dev), there)
    for k in along[1]:
        there, dev = neighbour(1, k)
        come(rcopy(own_src, at(k, 0), s_b[OPPOSITE[k]], dev), there)
        go(rcopy(at(k, 0), at(k, 0), s_d[k], member(1)), there)
    mid_send(3)
    for k in cross[1]:
        there, dev = neighbour(1, k)
        phase(f"f1_cross{k}")
        come(rcopy(own_src, at(k, 1), s_c[OPPOSITE[k]][1], dev), there)
        s_own = s_own - dot_left(k1[k], ybuf[1, k * skel:(k + 1) * skel, :], NN)
    for k in along[1]:
        there, dev = neighbour(1, k)
        phase(f"f1_along{k}")
        come(rcopy(at(k, 1), at(k, 1), s_d[k], member(1)), there)
        s_own = s_own - dot_left(k1[k], ybuf[1, k * skel:(k + 1) * skel, :], NN)
    turned[:, :cols] = s_own.T

    phase("l2_send")
    s_t2 = [slot() for _ in range(4)]
    half_of = lambda m: span(flipped(1, m), half)
    go(rcopy(turned.at[half_of(1)], v2.at[rank[2]], s_t2[1], member(1)), inner)
    go(rcopy(turned.at[half_of(3)], v2.at[rank[2]], s_t2[3], member(3)), inner)
    go(rcopy(turned.at[half_of(2)], v2.at[rank[2]], s_t2[2], member(2)), outer)
    mid_send(4, 5, 6)
    t1_copy = rcopy(tg1.at[rank[1]], tg1.at[rank[1]], slot(), member(1))
    go(t1_copy)
    mate_k = {k: rcopy(k1.at[k], kmate.at[k - 3], slot(), member(1)) for k in along[1]}
    for k in along[1]:
        go(mate_k[k], neighbour(1, k)[0])
    inner_forward(1)
    inner_forward(2)

    def wide_pick(pick, level, width, lanes):
        o = order_row[level:level + 1, :]
        o = o + sum((lanes - width) * (o >= width * b).astype(jnp.int32) for b in range(1, box // width))
        lines = lax.broadcasted_iota(jnp.int32, pick.shape, 0)
        pick[...] = jnp.where(lines == o, 1.0, 0.0).astype(BF16)

    def beside(k):
        there, (to_i, to_j) = neighbour(2, k)
        if k > 2:
            step = 1 + 2 * (1 - bits[2]) if k == 4 else -(1 + 2 * bits[2])
            to_i, to_j = i, j + step
        return there, (to_i, to_j)

    s_y2 = {k: slot() for k in has[2]}
    s_q2 = {k: slot() for k in has[2]}
    s_t3 = {m: slot() for m in (1, 4)}
    s_x3 = {m: slot() for m in (1, 4)}
    s_x2 = {m: slot() for m in (1, 2, 3)}
    s_y3 = {k: slot() for k in has[3]}
    s_q3 = {k: slot() for k in has[3]}
    quarter_of = lambda m: span(flipped(2, m), share)
    y2_copy = lambda k: rcopy(y2, yr2.at[OPPOSITE[k] - 1], s_y2[k], beside(k)[1])
    q2_copy = lambda k: rcopy(q2.at[k - 1], qr2.at[OPPOSITE[k] - 1], s_q2[k], beside(k)[1])
    y3_copy = lambda k: rcopy(y3, yr3.at[OPPOSITE[k] - 1], s_y3[k], neighbour(3, k)[1])
    q3_copy = lambda k: rcopy(q3.at[k - 1], qr3.at[OPPOSITE[k] - 1], s_q3[k], neighbour(3, k)[1])
    up_copy = lambda m: rcopy(turn2.at[quarter_of(m)], v3.at[bits[2]], s_t3[m], member(m))
    down_copy = lambda m: rcopy(x3.at[flipped(2, m)], t2.at[quarter_of(0)], s_x3[m], member(m))
    out_copy = lambda m: rcopy(x2.at[flipped(1, m)], back2.at[half_of(0)], s_x2[m], member(m))

    @pl.when(outer)
    def _():
        phase("l2_pick")
        wide_pick(pick2, 2, cols, turned.shape[1])
        mid_forward(1)
        v2[rank[2]] = turned[half_of(0), :]
        phase("l2_in")
        come(rcopy(turned.at[half_of(0)], v2.at[rank_of(2, 2)], s_t2[2], member(2)))
        come(rcopy(turned.at[half_of(0)], v2.at[rank_of(2, 1)], s_t2[1], member(1)))
        come(rcopy(turned.at[half_of(0)], v2.at[rank_of(2, 3)], s_t2[3], member(3)))
        phase("l2_a")
        full = lambda n: mid[n].reshape(skel, skel)
        a = pick_right(jnp.concatenate([v2[b] for b in range(4)], axis=1), pick2[...], NN)
        s0, r0 = a[:, :skel], a[:, skel:]
        phase("l2_y")
        mid_full(0)
        mid_full(1)
        y = dot_right(r0 - dot_right(s0, full(0), NT), full(1), NT)
        y2[...] = y
        for k in has[2]:
            @pl.when(beside(k)[0])
            def _():
                y2_copy(k).start()
        phase("l2_s")
        mid_forward(2)
        mid_full(2)
        turn2[...] = s0 - dot_right(y, full(2), NT)
        for k in has[2]:
            mid_forward(2 + k)
        for k in has[2]:
            phase(f"l2_s{k}")

            @pl.when(beside(k)[0])
            def _():
                mid_full(2 + k)
                rcopy(y2, yr2.at[k - 1], s_y2[OPPOSITE[k]], beside(k)[1]).wait_recv()
                turn2[...] = turn2[...] - dot_right(yr2[k - 1], full(2 + k), NT)
        for m in (4, 1):
            up_copy(m).start()
        phase(None)

    @pl.when(inner)
    def _():
        phase("l3_pick")
        wide_pick(pick3, 3, skel, skel)
        for n in (1, 2, 3):
            mate_send(n)
        for n in range(4):
            come(mate_copy(n, False))
        phase("l3_in")
        for m in (1, 4):
            come(rcopy(turn2.at[quarter_of(0)], v3.at[flipped(2, m)], s_t3[m], member(m)))
        full = lambda n: top[n].reshape(skel, skel)
        phase("l3_y")
        a = pick_right(jnp.concatenate([v3[0], v3[1]], axis=1), pick3[...], NN)
        s0, r0 = a[:, :skel], a[:, skel:]
        y = dot_right(r0 - dot_right(s0, full(0), NT), full(1), NT)
        y3[...] = y
        for k in has[3]:
            @pl.when(neighbour(3, k)[0])
            def _():
                y3_copy(k).start()
        phase("l3_s")
        v3[0] = s0 - dot_right(y, full(3), NT)
        for k in has[3]:
            phase(f"l3_s{k}")

            @pl.when(neighbour(3, k)[0])
            def _():
                rcopy(y3, yr3.at[k - 1], s_y3[OPPOSITE[k]], neighbour(3, k)[1]).wait_recv()
                v3[0] = v3[0] - dot_right(yr3[k - 1], full(3 + k), NT)
        phase("l3_q")
        t = dot_right(v3[0], full(2), NT)
        for k in has[3]:
            @pl.when(neighbour(3, k)[0])
            def _():
                q3[k - 1] = dot_right(t, full(3 + k), NN)
                q3_copy(k).start()
        v3[0] = dot_right(t, full(3), NN)
        for k in has[3]:
            phase(f"l3_u{k}")

            @pl.when(neighbour(3, k)[0])
            def _():
                rcopy(q3.at[k - 1], qr3.at[k - 1], s_q3[OPPOSITE[k]], neighbour(3, k)[1]).wait_recv()
                v3[0] = v3[0] + qr3[k - 1]
        phase("l3_x")
        xr = y - dot_right(v3[0], full(1), NN)
        xs = t - dot_right(xr, full(0), NN)
        xv = pick_right(jnp.concatenate([xs, xr], axis=1), pick3[...], NT)
        x3[0], x3[1] = xv[:, :skel], xv[:, skel:]
        for m in (4, 1):
            down_copy(m).start()
        phase(None)

    phase("b1_make")
    come(t1_copy)
    n1[:, :skel] = -dot3(g1[...], tg1[...].reshape(skel, skel), NN)
    n1[:, skel:] = g1[...]
    for k in along[1]:
        there, _ = neighbour(1, k)

        @pl.when(there)
        def _():
            mate_k[k].wait_recv()
            for n, block in enumerate((k1[k], kmate[k - 3])):
                kturn[...] = block.T
                krows[k - 3, n] = kturn[rows, :]

    @pl.when(outer)
    def _():
        phase("l2_tin")
        pick2[:box, :] = onehot_p(2)
        for m in (1, 4):
            come(rcopy(x3.at[bits[2]], t2.at[quarter_of(m)], s_x3[m], member(m)))
        full = lambda n: mid[n].reshape(skel, skel)
        phase("l2_q")
        t = t2[...]
        for k in reversed(has[2]):
            @pl.when(beside(k)[0])
            def _():
                q2[k - 1] = dot_right(t, full(2 + k), NN)
                q2_copy(k).start()
        yr2[0] = dot_right(t, full(2), NN)
        for k in has[2]:
            phase(f"l2_u{k}")

            @pl.when(beside(k)[0])
            def _():
                rcopy(q2.at[k - 1], qr2.at[k - 1], s_q2[OPPOSITE[k]], beside(k)[1]).wait_recv()
                yr2[0] = yr2[0] + qr2[k - 1]
        phase("l2_x")
        xr = y2[...] - dot_right(yr2[0], full(1), NN)
        xs = t - dot_right(xr, full(0), NN)
        x = jnp.concatenate([xs, xr], axis=1)
        x2[bits[1]] = pick_right(x, pick2[span(bits[1], skel), :], NT)
        out_copy(1).start()
        x2[1 - bits[1]] = pick_right(x, pick2[span(1 - bits[1], skel), :], NT)
        out_copy(3).start()
        out_copy(2).start()
        back2[half_of(0), :] = x2[bits[1]]
        phase(None)

    phase("l2_out")
    come(rcopy(x2.at[bits[1]], back2.at[half_of(2)], s_x2[2], member(2)), outer)
    for m in (1, 3):
        come(rcopy(x2.at[bits[1]], back2.at[half_of(m)], s_x2[m], member(m)), inner)

    phase("b1_q")
    tfull[...] = back2[...].T
    t_own = tfull[rows, :]
    others = span(rank_of(1, 1), cols)
    s_q = {k: slot() for k in has[1]}
    for k in cross[1]:
        at_k = pl.ds(k * skel, skel)
        qsend[1, at_k, :] = dot_left(k1[k], t_own, TN)
        there, dev = neighbour(1, k)
        go(rcopy(qsend.at[1, at_k, :], qrecv.at[1, OPPOSITE[k] - 1], s_q[k], dev), there)
    for k in along[1]:
        there, dev = neighbour(1, k)

        @pl.when(there)
        def _():
            nsend[k - 3] = dot_left(krows[k - 3, 0], t_own, NN) + dot_left(krows[k - 3, 1], tfull[others, :], NN)
        go(rcopy(nsend.at[k - 3], nrecv.at[OPPOSITE[k] - 3], s_q[k], dev), there)
    phase("b1_q0")
    u = dot_left(k1[0], t_own, TN)
    abuf[...] = base1[...]
    abuf[rows, :] = abuf[rows, :] + t_own
    for k in cross[1]:
        phase(f"b1_wait{k}")
        there, dev = neighbour(1, k)
        come(rcopy(qsend.at[1, pl.ds(k * skel, skel), :], qrecv.at[1, k - 1], s_q[OPPOSITE[k]], dev), there)
        u = u + qrecv[1, k - 1]
    phase("b1_u")
    qsend[1, :skel, :] = u
    give_u = rcopy(qsend.at[1, others, :], urecv1.at[0], slot(), member(1))
    go(give_u)
    come(give_u)
    u = qsend[1, rows, :] + urecv1[0]
    for k in along[1]:
        phase(f"b1_wait{k}")
        there, dev = neighbour(1, k)
        come(rcopy(nsend.at[k - 3], nrecv.at[k - 3], s_q[OPPOSITE[k]], dev), there)
        u = u + nrecv[k - 3]
    phase("b1_comb")
    abuf[...] = abuf[...] - dot_left(n1[...], u, TN)
    phase("b1_x")
    both = jnp.concatenate(halves(abuf[...]), axis=1)
    for m in (1, 0):
        spot = span(rank_of(1, m), skel)
        xpart[spot, :] = lanes_summed(product(ptbuf[spot, :], both, NN))
        if m:
            give_x = rcopy(xpart.at[spot, :], xrecv1.at[0], slot(), member(1))
            go(give_x)
    phase("b1_xwait")
    ptbuf[...] = onehot_pt(0)
    come(give_x)
    t_own = xpart[span(rank[1], skel), :] + xrecv1[0]

    phase("b0_q")
    s_q = {k: slot() for k in has[0]}
    for k in along[0] + cross[0]:
        at_k = pl.ds(k * skel, skel)
        qsend[0, at_k, :] = dot_left(k0[k], t_own, NN)
        there, dev = neighbour(0, k)
        go(rcopy(qsend.at[0, at_k, :], qrecv.at[0, OPPOSITE[k] - 1], s_q[k], dev), there)
    u = dot_left(k0[0], t_own, NN)
    for k in cross[0] + along[0]:
        phase(f"b0_wait{k}")
        there, dev = neighbour(0, k)
        come(rcopy(qsend.at[0, pl.ds(k * skel, skel), :], qrecv.at[0, k - 1], s_q[OPPOSITE[k]], dev), there)
        u = u + qrecv[0, k - 1]
    phase("b0_x")
    xr = ypart[0] - dot_left(g0[...], u, NN)
    abuf[skel:, :] = xr
    abuf[:skel, :] = t_own - dot_left(t0[...], xr, NN)
    phase("b0_out")
    rhs[...] = pick_right(abuf[...], ptbuf[...], TN)
    result = pltpu.make_async_copy(rhs, out.at[0, 0], local.at[15])
    result.start()

    phase("drain")
    for when, make in pending:
        if when is None:
            make().wait_send()
        else:
            @pl.when(when)
            def _():
                make().wait_send()

    @pl.when(inner)
    def _():
        for k in has[3]:
            @pl.when(neighbour(3, k)[0])
            def _():
                y3_copy(k).wait_send()
                q3_copy(k).wait_send()
        for m in (4, 1):
            down_copy(m).wait_send()

    @pl.when(outer)
    def _():
        for k in has[2]:
            @pl.when(beside(k)[0])
            def _():
                y2_copy(k).wait_send()
                q2_copy(k).wait_send()
        for m in (4, 1):
            up_copy(m).wait_send()
        for m in (3, 1, 2):
            out_copy(m).wait_send()
    result.wait()
    phase(None)


def body(size_x, size_y, right_sides, skeleton_order, *weights):
    rows = right_sides.shape[2]
    box = right_sides.shape[3]
    skel = box // 2
    weights = [jnp.swapaxes(w, -1, -2) if w.shape[-1] < skel else w for w in weights]
    vm = lambda *shape: pltpu.VMEM(shape, F32)
    widths = [skel >> level for level in range(4)]
    half, share = rows // 2, rows // 4
    kinds = 5 if size_y > REACH[3][1] else 3
    lanes = -(-widths[1] // 128) * 128
    scratch = [
        vm(rows, box), pltpu.VMEM((4, box), jnp.int32), vm(skel, skel), vm(2, widths[1], skel),
        vm(skel, skel), vm(widths[1], skel), vm(5, skel, skel), vm(5, widths[1], skel),
        vm(2, 5 * skel, rows), vm(box, rows), vm(2, 5 * skel, rows), vm(2, 4, skel, rows),
        vm(1, widths[1], rows), vm(1, skel, rows), vm(box, rows), vm(box, rows),
        vm(widths[1], box),
        vm(box, rows), vm(2, skel, rows), vm(1, skel, rows),
        pltpu.VMEM((box, box), BF16), pltpu.VMEM((box, 8), jnp.int32),
        vm(skel, rows), vm(widths[1], rows), vm(2, widths[1], skel), vm(skel, widths[1]), vm(2, 2, widths[1], widths[1]),
        vm(skel, rows), vm(2, widths[1], rows), vm(2, widths[1], rows),
        vm(7, 4, widths[2], skel), vm(rows, lanes), vm(4, half, lanes),
        vm(half, skel), vm(4, half, skel), vm(4, half, skel), vm(4, half, skel),
        vm(2, half, skel), vm(rows, skel), pltpu.VMEM((4 * lanes, box), BF16), vm(half, skel), vm(half, skel),
        vm(3 + kinds, 8, widths[3], skel), vm(2, share, skel),
        vm(share, skel), vm(kinds - 1, share, skel), vm(kinds - 1, share, skel), vm(kinds - 1, share, skel),
        vm(2, share, skel), pltpu.VMEM((box, box), BF16),
        pltpu.SemaphoreType.DMA((16,)),
        pltpu.SemaphoreType.DMA((128,)), pltpu.SemaphoreType.DMA((128,)),
    ]
    return pl.pallas_call(
        functools.partial(kernel, size_x, size_y),
        out_shape=jax.ShapeDtypeStruct(right_sides.shape, F32),
        in_specs=[pl.BlockSpec(memory_space=pl.ANY)] * (2 + len(weights)),
        out_specs=pl.BlockSpec(memory_space=pl.ANY),
        scratch_shapes=scratch,
        compiler_params=pltpu.CompilerParams(
            collective_id=0, has_side_effects=True, vmem_limit_bytes=48 * 2**20
        ),
    )(*[pltpu.with_memory_space_constraint(a, pltpu.HBM) for a in (right_sides, skeleton_order, *weights)])


def solution(mesh):
    four = P("bx", "by", None, None)
    five = P("bx", "by", None, None, None)
    in_specs = (four,) * 10 + (five,) * 4 + (four,)
    return jax.shard_map(
        functools.partial(body, mesh.shape["bx"], mesh.shape["by"]),
        mesh=mesh, in_specs=in_specs, out_specs=four, check_vma=False,
    )
```

```python
import functools

import jax
import jax.numpy as jnp
from jax import lax
from jax.experimental import pallas as pl
from jax.experimental.pallas import tpu as pltpu
from jax.sharding import PartitionSpec as P

REACH = ((1, 1), (1, 2), (2, 2), (2, 4))
OPPOSITE = {1: 2, 2: 1, 3: 4, 4: 3}
F32 = jnp.float32
BF16 = jnp.bfloat16
MESH = pl.DeviceIdType.MESH
NN = (((1,), (0,)), ((), ()))
TN = (((0,), (0,)), ((), ()))
NT = (((1,), (1,)), ((), ()))


def halves(x):
    high = x.astype(BF16)
    return high, (x - high.astype(F32)).astype(BF16)


def product(a, b, dims):
    return lax.dot_general(a, b, dims, preferred_element_type=F32)


def dot3(a, b, dims):
    ah, al = halves(a)
    bh, bl = halves(b)
    return product(ah, bh, dims) + (product(ah, bl, dims) + product(al, bh, dims))


def lanes_summed(x):
    wide = x.shape[1] // 2
    return x[:, :wide] + x[:, wide:]


def rows_summed(x):
    tall = x.shape[0] // 2
    return x[:tall] + x[tall:]


def dot_left(a, b, dims):
    ah, al = halves(a)
    bh, bl = halves(b)
    return lanes_summed(product(ah, jnp.concatenate([bh, bl], axis=1), dims)) + product(al, bh, dims)


def dot_right(a, b, dims):
    ah, al = halves(a)
    bh, bl = halves(b)
    return rows_summed(product(jnp.concatenate([ah, al], axis=0), bh, dims)) + product(ah, bl, dims)


def pick_left(onehot, b, dims):
    return lanes_summed(product(onehot, jnp.concatenate(halves(b), axis=1 if dims == NN else 0), dims))


def pick_right(a, onehot, dims):
    if dims == TN:
        return rows_summed(product(jnp.concatenate(halves(a), axis=1), onehot, dims))
    return rows_summed(product(jnp.concatenate(halves(a), axis=0), onehot, dims))


def dot_left_of(ah, al, b, dims):
    bh, bl = halves(b)
    return lanes_summed(product(ah, jnp.concatenate([bh, bl], axis=1), dims)) + product(al, bh, dims)


def dot_right_of(a, bh, bl, dims):
    ah, al = halves(a)
    return rows_summed(product(jnp.concatenate([ah, al], axis=0), bh, dims)) + product(ah, bl, dims)


class Phases:
    def __init__(self):
        self.scope = None

    def __call__(self, name):
        if self.scope:
            self.scope.__exit__(None, None, None)
        self.scope = jax.named_scope(name) if name else None
        if self.scope:
            self.scope.__enter__()


def kernel(size_x, size_y, *refs):
    (rhs_in, order_in, t0_in, t1_in, t2_in, t3_in, g0_in, g1_in, g2_in, g3_in,
     k0_in, k1_in, k2_in, k3_in, root_in, out) = refs[:16]
    (rhs, order_row, t0, tg1, g0, g1, k0, k1,
     ybuf, vbuf, qsend, qrecv, xrecv1, xpart, base1,
     abuf, ypart, ssend, ptbuf, order_col, wbuf, wpart, kgive, kturn, krows, tfull, nsend, nrecv,
     k0h, k0l, n1h, n1l, midh, midl, toph, topl, mid, turned, v2, y2, yr2, q2, qr2, x2, back2, pick2, turn2, t2,
     top, v3, y3, yr3, q3, qr3, x3, pick3, local, ready, send, recv) = refs[16:]
    skel = t0.shape[0]
    box = 2 * skel
    rhs_count = ybuf.shape[2]
    half, share = v2.shape[1], v3.shape[1]
    kinds = top.shape[0] - 3
    phase = Phases()
    i, j = lax.axis_index("bx"), lax.axis_index("by")
    bits = (lax.rem(j, 2), lax.rem(i, 2), lax.rem(lax.div(j, 2), 2))
    inner = bits[0] != bits[2]
    outer = jnp.logical_not(inner)

    def flipped(b, m):
        return (1 - bits[b]) if m >> b & 1 else bits[b]

    def member(m):
        return (i + (flipped(1, m) - bits[1]), j + (flipped(0, m) - bits[0]) + 2 * (flipped(2, m) - bits[2]))

    def rank_of(level, m):
        rank = jnp.int32(0)
        for b in range(level):
            rank = rank + (1 << b) * flipped(b, m)
        return rank

    def span(start, size):
        return pl.ds(pl.multiple_of(start * size, size), size)

    def neighbour(level, k):
        rx, ry = REACH[level]
        if k == 1:
            return i >= rx, (i - rx, j)
        if k == 2:
            return i + rx < size_x, (i + rx, j)
        if k == 3:
            return j >= ry, (i, j - ry)
        return j + ry < size_y, (i, j + ry)

    has = [[k for k in (1, 2, 3, 4) if (REACH[l][0] < size_x if k < 3 else REACH[l][1] < size_y)] for l in range(4)]
    cross = [[k for k in has[l] if k < 3] for l in range(4)]
    along = [[k for k in has[l] if k > 2] for l in range(4)]

    count = [0]
    pending = []

    def slot():
        count[0] += 1
        return count[0] - 1

    def rcopy(src, dst, s, dev):
        return pltpu.make_async_remote_copy(src, dst, send.at[s], recv.at[s], device_id=dev, device_id_type=MESH)

    def go(c, when=None):
        make = c if callable(c) else lambda: c
        entry = (when, make)
        pending.append(entry)
        if when is None:
            make().start()
        else:
            @pl.when(when)
            def _():
                make().start()
        return entry

    def settle(entries):
        for when, make in entries:
            if when is None:
                make().wait_send()
            else:
                @pl.when(when)
                def _():
                    make().wait_send()
        pending[:] = [entry for entry in pending if not any(entry is e for e in entries)]

    def come(c, when=None):
        if when is None:
            c.wait_recv()
        else:
            @pl.when(when)
            def _():
                c.wait_recv()

    phase("start")
    rank = [rank_of(l, 0) for l in range(4)]
    loads = {}

    def load(name, src, dst):
        c = pltpu.make_async_copy(src, dst, local.at[len(loads)])
        loads[name] = c
        c.start()

    def need(*names):
        for name in names:
            loads[name].wait()

    load("order", order_in.at[0, 0], order_row)
    load("t0", t0_in.at[0, 0], t0)
    load("g0", g0_in.at[0, 0], g0)
    load("rhs", rhs_in.at[0, 0], rhs)
    load("t1", t1_in.at[0, 0], tg1.at[rank[1]])
    load("k0", k0_in.at[0, 0], k0)
    load("g1", g1_in.at[0, 0], g1.at[rank[1]])
    load("t2", t2_in.at[0, 0], mid.at[0, rank[2]])
    load("g2", g2_in.at[0, 0], mid.at[1, rank[2]])
    load("k2", k2_in.at[0, 0], mid.at[pl.ds(2, 5), rank[2]])
    load("t3", t3_in.at[0, 0], top.at[0, rank[3]])
    load("g3", g3_in.at[0, 0], top.at[1, rank[3]])
    load("root", root_in.at[0, 0], top.at[2, rank[3]])
    load("k3", k3_in.at[0, 0, pl.ds(0, kinds)], top.at[pl.ds(3, kinds), rank[3]])
    load("k1", k1_in.at[0, 0], k1)

    barrier = pltpu.get_barrier_semaphore()
    for m in range(1, 8):
        pl.semaphore_signal(barrier, 1, device_id=member(m), device_id_type=MESH)
    total = jnp.int32(7)
    greeted = set()
    for level in range(4):
        for k in has[level]:
            key = (k, REACH[level][0] if k < 3 else REACH[level][1])
            if key in greeted:
                continue
            greeted.add(key)
            there, dev = neighbour(level, k)

            @pl.when(there)
            def _():
                pl.semaphore_signal(barrier, 1, device_id=dev, device_id_type=MESH)
            total = total + there.astype(jnp.int32)

    for level in range(2):
        for k in (1, 2, 3, 4):
            there, _ = neighbour(level, k)

            @pl.when(jnp.logical_not(there))
            def _():
                ybuf[level, k * skel:(k + 1) * skel, :] = jnp.zeros((skel, rhs_count), F32)
                qrecv[level, k - 1] = jnp.zeros((skel, rhs_count), F32)
    for k in along[1]:
        there, _ = neighbour(1, k)

        @pl.when(jnp.logical_not(there))
        def _():
            nrecv[k - 3] = jnp.zeros(nrecv.shape[1:], F32)
    turned[...] = jnp.zeros_like(turned)

    chunks = range((top.shape[0] + 1) // 2)
    slots_in, slots_on = ([slot() for _ in chunks] for _ in range(2))
    slots_mate = [slot() for _ in range(4)]
    slots_mid = [slot() for _ in range(7)]
    slots_own = slots_mid[:len(chunks)]
    among = slots_in + slots_on + slots_mate
    among = among + [slot() for _ in range(14 - len(among))]
    slots_mid_own, slots_mid_on = among[:7], among[7:14]

    def chunk_copy(c, block, dev, s):
        at = pl.ds(2 * c, min(2, top.shape[0] - 2 * c))
        return rcopy(top.at[at, block], top.at[at, block], s, dev)

    def mate_copy(n, mine):
        block = rank_of(3, (0, 1, 5, 4)[n] ^ (0 if mine else 2))
        return rcopy(top.at[:, block], top.at[:, block], slots_mate[n], member(2))

    def outer_send(c):
        go(chunk_copy(c, rank[3], member(1), slots_own[c]), outer)

    def inner_send():
        for c in chunks:
            go(chunk_copy(c, rank[3], member(5), slots_in[c]), inner)

    def inner_forward(c):
        come(chunk_copy(c, rank_of(3, 1), member(1), slots_own[c]), inner)
        go(chunk_copy(c, rank_of(3, 1), member(5), slots_on[c]), inner)

    def mate_send(n):
        for c in chunks:
            if n == 2:
                come(chunk_copy(c, rank_of(3, 5), member(5), slots_in[c]), inner)
            if n == 3:
                come(chunk_copy(c, rank_of(3, 4), member(5), slots_on[c]), inner)
        go(lambda: mate_copy(n, True), inner)

    near = [None, None, None] + [neighbour(2, k)[0] for k in (1, 2, 3, 4)]

    near_in = [inner if there is None else jnp.logical_and(inner, there) for there in near]
    near_out = [outer if there is None else jnp.logical_and(outer, there) for there in near]

    def mid_copy(n, m, to, s):
        block = rank_of(2, m)
        return rcopy(mid.at[n, block], mid.at[n, block], s, member(to))

    def used(n):
        return n < 3 or n - 2 in has[2]

    def mid_send(*wanted):
        for n in filter(used, wanted):
            go(mid_copy(n, 0, 1, slots_mid[n]), near_in[n])

    def mid_share(*wanted):
        for n in filter(used, wanted):
            go(mid_copy(n, 0, 2, slots_mid_own[n]), near_out[n])

    def mid_forward(*wanted):
        for n in filter(used, wanted):
            come(mid_copy(n, 1, 1, slots_mid[n]), near_out[n])
            go(lambda n=n: mid_copy(n, 1, 2, slots_mid_on[n]), near_out[n])

    def mid_full(n):
        come(mid_copy(n, 2, 2, slots_mid_own[n]), near[n])
        come(mid_copy(n, 3, 2, slots_mid_on[n]), near[n])

    def onehot_pt(level):
        lanes = lax.broadcasted_iota(jnp.int32, (box, box), 1)
        return jnp.where(lanes == order_col[:, level:level + 1], 1.0, 0.0).astype(BF16)

    def onehot_p(level):
        rows = lax.broadcasted_iota(jnp.int32, (box, box), 0)
        return jnp.where(rows == order_row[level:level + 1, :], 1.0, 0.0).astype(BF16)

    need("order")
    order_f = order_row[...].astype(F32)
    order_f = jnp.concatenate([order_f, jnp.zeros((8 - order_f.shape[0], box), F32)], axis=0)
    order_col[...] = order_f.T.astype(jnp.int32)

    phase("f0_a")
    need("rhs")
    abuf[...] = pick_left(onehot_pt(0), rhs[...], NT)
    phase("f0_y")
    need("t0", "g0")
    y_own = dot_left(g0[...], abuf[skel:, :] - dot_left(t0[...], abuf[:skel, :], TN), TN)
    ybuf[0, :skel, :] = y_own
    ypart[0] = y_own
    phase("f0_barrier")
    pl.semaphore_wait(barrier, total)
    phase("f0_send")
    slots_y0 = {k: slot() for k in has[0]}
    early = []
    for k in along[0] + cross[0]:
        there, dev = neighbour(0, k)
        far = OPPOSITE[k]
        early.append(go(rcopy(ypart.at[0], ybuf.at[0, pl.ds(far * skel, skel), :], slots_y0[k], dev), there))
    need("t2", "g2", "k2", "t3", "g3", "root", "k3")
    mid_send(0)
    outer_send(0)
    inner_send()
    mate_send(0)
    phase("f0_split")
    need("k0")
    for k in range(5):
        k0h[k], k0l[k] = halves(k0[k])
    phase("f0_s")
    s_own = abuf[:skel, :] - dot_left_of(k0h[0], k0l[0], ypart[0], TN)
    ptbuf[...] = onehot_pt(1)
    for k in cross[0] + along[0]:
        there, dev = neighbour(0, k)
        phase(f"f0_wait{k}")
        come(rcopy(ypart.at[0], ybuf.at[0, pl.ds(k * skel, skel), :], slots_y0[OPPOSITE[k]], dev), there)
        phase(f"f0_s{k}")
        s_own = s_own - dot_left_of(k0h[k], k0l[k], ybuf[0, k * skel:(k + 1) * skel, :], TN)
    ssend[0] = s_own
    vbuf[span(rank[1], skel), :] = s_own
    s_give = slot()
    give = rcopy(ssend.at[0], vbuf.at[span(rank[1], skel), :], s_give, member(1))
    early.append(go(give))
    mid_send(1)
    outer_send(1)
    mid_share(*range(7))
    phase("f0_gwait")
    need("t1", "g1", "k1")
    come(give)

    phase("f1_a")
    cols = skel >> 1
    rows = span(rank[1], cols)
    abuf[...] = pick_left(ptbuf[...], vbuf[...], NN)
    phase("f1_w")
    w_own = abuf[pl.ds(pl.multiple_of(skel + rank[1] * cols, cols), cols), :] - dot_left(tg1[rank[1]], abuf[:skel, :], NN)
    wpart[...] = w_own
    wbuf[rows, :] = w_own
    give_w = rcopy(wpart, wbuf.at[rows, :], slot(), member(1))
    go(give_w)
    ptbuf[...] = onehot_p(1)
    phase("f1_wwait")
    come(give_w)
    phase("f1_y")
    y_own = dot_left(g1[rank[1]], wbuf[...], NN)
    ypart[1, :cols, :] = y_own
    ybuf[1, rows, :] = y_own

    def at(k, m):
        return ybuf.at[1, pl.ds(pl.multiple_of(k * skel + rank_of(1, m) * cols, cols), cols), :]

    own_src = ypart.at[1, pl.ds(0, cols), :]
    s_a = slot()
    s_c = {k: [slot(), slot()] for k in cross[1]}
    s_b = {k: slot() for k in along[1]}
    s_d = {k: slot() for k in along[1]}
    phase("f1_send")
    mate = rcopy(own_src, at(0, 0), s_a, member(1))
    go(mate)
    for k in along[1]:
        there, dev = neighbour(1, k)
        early.append(go(rcopy(own_src, at(OPPOSITE[k], 0), s_b[k], dev), there))
    for k in cross[1]:
        there, dev = neighbour(1, k)
        early.append(go(rcopy(own_src, at(OPPOSITE[k], 0), s_c[k][0], dev), there))
    mid_send(2)
    outer_send(2)
    base1[:skel, :] = -dot_left(tg1[rank[1]], y_own, TN)
    base1[skel:, :] = jnp.zeros((skel, rhs_count), F32)
    base1[pl.ds(pl.multiple_of(skel + rank[1] * cols, cols), cols), :] = y_own
    phase("f1_ywait")
    come(mate)
    for k in cross[1]:
        there, dev = neighbour(1, k)
        go(rcopy(at(0, 1), at(OPPOSITE[k], 1), s_c[k][1], dev), there)
    inner_forward(0)
    mid_forward(0)
    phase("f1_s0")
    s_own = abuf[rows, :] - dot_left(k1[0], ybuf[1, :skel, :], NN)
    phase("f1_relay")
    for k in cross[1]:
        there, dev = neighbour(1, k)
        come(rcopy(own_src, at(k, 0), s_c[OPPOSITE[k]][0], dev), there)
    for k in along[1]:
        there, dev = neighbour(1, k)
        come(rcopy(own_src, at(k, 0), s_b[OPPOSITE[k]], dev), there)
        go(rcopy(at(k, 0), at(k, 0), s_d[k], member(1)), there)
    mid_send(3)
    for k in cross[1]:
        there, dev = neighbour(1, k)
        phase(f"f1_cross{k}")
        come(rcopy(own_src, at(k, 1), s_c[OPPOSITE[k]][1], dev), there)
        s_own = s_own - dot_left(k1[k], ybuf[1, k * skel:(k + 1) * skel, :], NN)
    for k in along[1]:
        there, dev = neighbour(1, k)
        phase(f"f1_along{k}")
        come(rcopy(at(k, 1), at(k, 1), s_d[k], member(1)), there)
        s_own = s_own - dot_left(k1[k], ybuf[1, k * skel:(k + 1) * skel, :], NN)
    turned[:, :cols] = s_own.T

    phase("l2_send")
    s_t2 = {m: slot() for m in (1, 2, 3)}
    half_of = lambda m: span(flipped(1, m), half)
    go(rcopy(turned.at[half_of(1)], v2.at[rank[2]], s_t2[1], member(1)), inner)
    go(rcopy(turned.at[half_of(3)], v2.at[rank[2]], s_t2[3], member(3)), inner)
    across = go(rcopy(turned.at[half_of(2)], v2.at[rank[2]], s_t2[2], member(2)), outer)
    pending.pop()
    mid_send(4, 5, 6)
    s_t1 = [slot(), slot(), slot()]
    s_k1 = {k: slot() for k in along[1]}
    near1 = {k: neighbour(1, k)[0] for k in along[1]}
    near1_in = {k: jnp.logical_and(inner, near1[k]) for k in along[1]}
    near1_out = {k: jnp.logical_and(outer, near1[k]) for k in along[1]}
    t1_copy = lambda: rcopy(tg1.at[rank[1]], tg1.at[rank[1]], s_t1[0], member(1))
    part = cols // 2
    g1_part = lambda n: g1.at[rank[1], pl.ds(n * part, part), :]
    g1_copy = lambda n: rcopy(g1_part(n), g1_part(n), s_t1[1 + n], member(1))
    k1_copy = lambda k: rcopy(kgive.at[k - 3], krows.at[k - 3, 1], s_k1[k], member(1))
    others = span(rank_of(1, 1), cols)
    for k in along[1]:
        @pl.when(near1[k])
        def _():
            kturn[...] = k1[k].T
            krows[k - 3, 0] = kturn[rows, :]
            kgive[k - 3] = kturn[others, :]
    part = cols // 2
    g1_part = lambda n: g1.at[rank[1], pl.ds(n * part, part), :]
    g1_copy = lambda n: rcopy(g1_part(n), g1_part(n), s_t1[1 + n], member(1))

    def late_send(when, near, *wanted):
        for n in wanted:
            if n == 3:
                for k in along[1]:
                    go(lambda k=k: k1_copy(k), near[k])
            else:
                go(t1_copy if n == 0 else lambda n=n: g1_copy(n - 1), when)

    def late_make():
        come(t1_copy())
        come(g1_copy(0))
        come(g1_copy(1))
        own = g1[...].reshape(skel, skel)
        n1h[:, :skel], n1l[:, :skel] = halves(-dot3(own, tg1[...].reshape(skel, skel), NN))
        n1h[:, skel:], n1l[:, skel:] = halves(own)

    inner_forward(1)
    inner_forward(2)

    def wide_pick(pick, level, width, lanes):
        o = order_row[level:level + 1, :]
        o = o + sum((lanes - width) * (o >= width * b).astype(jnp.int32) for b in range(1, box // width))
        lines = lax.broadcasted_iota(jnp.int32, pick.shape, 0)
        pick[...] = jnp.where(lines == o, 1.0, 0.0).astype(BF16)

    def beside(k):
        there, (to_i, to_j) = neighbour(2, k)
        if k > 2:
            step = 1 + 2 * (1 - bits[2]) if k == 4 else -(1 + 2 * bits[2])
            to_i, to_j = i, j + step
        return there, (to_i, to_j)

    s_y2 = s_q2 = {k: slot() for k in has[2]}
    s_y3 = {k: s_y2[k] for k in has[3]}
    s_q3 = {k: slot() for k in has[3]}
    s_t3 = s_x3 = {m: slot() for m in (1, 4)}
    s_x2 = s_t2
    quarter_of = lambda m: span(flipped(2, m), share)
    y2_copy = lambda k: rcopy(y2, yr2.at[OPPOSITE[k] - 1], s_y2[k], beside(k)[1])
    q2_copy = lambda k: rcopy(q2.at[k - 1], qr2.at[OPPOSITE[k] - 1], s_q2[k], beside(k)[1])
    y3_copy = lambda k: rcopy(y3, yr3.at[OPPOSITE[k] - 1], s_y3[k], neighbour(3, k)[1])
    q3_copy = lambda k: rcopy(q3.at[k - 1], qr3.at[OPPOSITE[k] - 1], s_q3[k], neighbour(3, k)[1])
    up_copy = lambda m: rcopy(turn2.at[quarter_of(m)], v3.at[bits[2]], s_t3[m], member(m))
    down_copy = lambda m: rcopy(x3.at[flipped(2, m)], t2.at[quarter_of(0)], s_x3[m], member(m))
    out_copy = lambda m: rcopy(x2.at[flipped(1, m)], back2.at[half_of(0)], s_x2[m], member(m))

    late_send(outer, near1_out, 0)

    @pl.when(outer)
    def _():
        phase("l2_pick")
        wide_pick(pick2, 2, cols, turned.shape[1])
        mid_forward(1)
        full = lambda n: mid[n].reshape(skel, skel)
        for n in (0, 1):
            mid_full(n)
            midh[n], midl[n] = halves(full(n))
        v2[rank[2]] = turned[half_of(0), :]
        phase("l2_in")
        come(rcopy(turned.at[half_of(0)], v2.at[rank_of(2, 2)], s_t2[2], member(2)))
        come(rcopy(turned.at[half_of(0)], v2.at[rank_of(2, 1)], s_t2[1], member(1)))
        come(rcopy(turned.at[half_of(0)], v2.at[rank_of(2, 3)], s_t2[3], member(3)))
        phase("l2_a")
        a = pick_right(jnp.concatenate([v2[b] for b in range(4)], axis=1), pick2[...], NN)
        s0, r0 = a[:, :skel], a[:, skel:]
        phase("l2_y")
        y = dot_right_of(r0 - dot_right_of(s0, midh[0], midl[0], NT), midh[1], midl[1], NT)
        y2[...] = y
        for k in has[2]:
            @pl.when(beside(k)[0])
            def _():
                y2_copy(k).start()
        late_send(outer, near1_out, 1, 2)
        phase("l2_s")
        mid_forward(2)
        mid_full(2)
        turn2[...] = s0 - dot_right(y, full(2), NT)
        for k in has[2]:
            mid_forward(2 + k)
        for k in has[2]:
            phase(f"l2_s{k}")

            @pl.when(beside(k)[0])
            def _():
                mid_full(2 + k)
                rcopy(y2, yr2.at[k - 1], s_y2[OPPOSITE[k]], beside(k)[1]).wait_recv()
                turn2[...] = turn2[...] - dot_right(yr2[k - 1], full(2 + k), NT)
        for m in (4, 1):
            up_copy(m).start()
        late_send(outer, near1_out, 3)
        phase("l2_split")
        midh[2], midl[2] = halves(full(2))
        for k in has[2]:
            @pl.when(beside(k)[0])
            def _():
                midh[2 + k], midl[2 + k] = halves(full(2 + k))
        phase(None)

    @pl.when(inner)
    def _():
        phase("l3_pick")
        wide_pick(pick3, 3, skel, skel)
        for n in (1, 2, 3):
            mate_send(n)
        for n in range(4):
            come(mate_copy(n, False))
        for n in range(3 + kinds):
            toph[n], topl[n] = halves(top[n].reshape(skel, skel))
        phase("l3_in")
        for m in (1, 4):
            come(rcopy(turn2.at[quarter_of(0)], v3.at[flipped(2, m)], s_t3[m], member(m)))
        late_send(inner, near1_in, 0, 1)
        phase("l3_y")
        a = pick_right(jnp.concatenate([v3[0], v3[1]], axis=1), pick3[...], NN)
        s0, r0 = a[:, :skel], a[:, skel:]
        y = dot_right_of(r0 - dot_right_of(s0, toph[0], topl[0], NT), toph[1], topl[1], NT)
        y3[...] = y
        for k in has[3]:
            @pl.when(neighbour(3, k)[0])
            def _():
                y3_copy(k).start()
        phase("l3_s")
        v3[0] = s0 - dot_right_of(y, toph[3], topl[3], NT)
        for k in has[3]:
            phase(f"l3_s{k}")

            @pl.when(neighbour(3, k)[0])
            def _():
                rcopy(y3, yr3.at[k - 1], s_y3[OPPOSITE[k]], neighbour(3, k)[1]).wait_recv()
                v3[0] = v3[0] - dot_right_of(yr3[k - 1], toph[3 + k], topl[3 + k], NT)
        phase("l3_q")
        t = dot_right_of(v3[0], toph[2], topl[2], NT)
        for k in has[3]:
            @pl.when(neighbour(3, k)[0])
            def _():
                q3[k - 1] = dot_right_of(t, toph[3 + k], topl[3 + k], NN)
                q3_copy(k).start()
        v3[0] = dot_right_of(t, toph[3], topl[3], NN)
        for k in has[3]:
            phase(f"l3_u{k}")

            @pl.when(neighbour(3, k)[0])
            def _():
                rcopy(q3.at[k - 1], qr3.at[k - 1], s_q3[OPPOSITE[k]], neighbour(3, k)[1]).wait_recv()
                v3[0] = v3[0] + qr3[k - 1]
        phase("l3_x")
        xr = y - dot_right_of(v3[0], toph[1], topl[1], NN)
        xs = t - dot_right_of(xr, toph[0], topl[0], NN)
        xv = pick_right(jnp.concatenate([xs, xr], axis=1), pick3[...], NT)
        x3[0], x3[1] = xv[:, :skel], xv[:, skel:]
        for m in (4, 1):
            down_copy(m).start()
        pl.semaphore_wait(ready, 1)
        late_send(inner, near1_in, 3, 2)
        phase(None)

    @pl.when(outer)
    def _():
        phase("l2_tin")
        pick2[:box, :] = onehot_p(2)
        for m in (1, 4):
            come(rcopy(x3.at[bits[2]], t2.at[quarter_of(m)], s_x3[m], member(m)))
        pl.semaphore_signal(ready, 1, device_id=member(1), device_id_type=MESH)
        phase("l2_q")
        t = t2[...]
        for k in reversed(has[2]):
            @pl.when(beside(k)[0])
            def _():
                q2[k - 1] = dot_right_of(t, midh[2 + k], midl[2 + k], NN)
                y2_copy(k).wait_send()
                q2_copy(k).start()
        yr2[0] = dot_right_of(t, midh[2], midl[2], NN)
        for k in has[2]:
            phase(f"l2_u{k}")

            @pl.when(beside(k)[0])
            def _():
                rcopy(q2.at[k - 1], qr2.at[k - 1], s_q2[OPPOSITE[k]], beside(k)[1]).wait_recv()
                yr2[0] = yr2[0] + qr2[k - 1]
        phase("l2_x")
        xr = y2[...] - dot_right_of(yr2[0], midh[1], midl[1], NN)
        xs = t - dot_right_of(xr, midh[0], midl[0], NN)
        x = jnp.concatenate([xs, xr], axis=1)
        x2[bits[1]] = pick_right(x, pick2[span(bits[1], skel), :], NT)
        out_copy(1).start()
        x2[1 - bits[1]] = pick_right(x, pick2[span(1 - bits[1], skel), :], NT)
        out_copy(3).start()
        across[1]().wait_send()
        out_copy(2).start()
        back2[half_of(0), :] = x2[bits[1]]
        phase(None)

    phase("l2_out")
    come(rcopy(x2.at[bits[1]], back2.at[half_of(2)], s_x2[2], member(2)), outer)
    for m in (1, 3):
        come(rcopy(x2.at[bits[1]], back2.at[half_of(m)], s_x2[m], member(m)), inner)

    phase("b1_settle")
    settle(early)
    phase("b1_q")
    tfull[...] = back2[...].T
    t_own = tfull[rows, :]
    s_q = {k: s_c[k][0] if k < 3 else s_b[k] for k in has[1]}
    for k in cross[1]:
        at_k = pl.ds(k * skel, skel)
        qsend[1, at_k, :] = dot_left(k1[k], t_own, TN)
        there, dev = neighbour(1, k)
        go(rcopy(qsend.at[1, at_k, :], qrecv.at[1, OPPOSITE[k] - 1], s_q[k], dev), there)
    for k in along[1]:
        there, dev = neighbour(1, k)

        @pl.when(there)
        def _():
            k1_copy(k).wait_recv()
            nsend[k - 3] = dot_left(krows[k - 3, 0], t_own, NN) + dot_left(krows[k - 3, 1], tfull[others, :], NN)
        go(rcopy(nsend.at[k - 3], nrecv.at[OPPOSITE[k] - 3], s_q[k], dev), there)
    phase("b1_q0")
    u = dot_left(k1[0], t_own, TN)
    abuf[...] = base1[...]
    abuf[rows, :] = abuf[rows, :] + t_own
    phase("b1_late")
    late_make()
    for k in cross[1]:
        phase(f"b1_wait{k}")
        there, dev = neighbour(1, k)
        come(rcopy(qsend.at[1, pl.ds(k * skel, skel), :], qrecv.at[1, k - 1], s_q[OPPOSITE[k]], dev), there)
        u = u + qrecv[1, k - 1]
    qsend[1, :skel, :] = u
    for k in along[1]:
        phase(f"b1_wait{k}")
        there, dev = neighbour(1, k)
        come(rcopy(nsend.at[k - 3], nrecv.at[k - 3], s_q[OPPOSITE[k]], dev), there)
        qsend[1, rows, :] = qsend[1, rows, :] + nrecv[k - 3]
    phase("b1_comb")
    abuf[...] = abuf[...] - dot_left_of(n1h[...], n1l[...], qsend[1, :skel, :], TN)
    phase("b1_x")
    both = jnp.concatenate(halves(abuf[...]), axis=1)
    for m in (1, 0):
        spot = span(rank_of(1, m), skel)
        xpart[spot, :] = lanes_summed(product(ptbuf[spot, :], both, NN))
        if m:
            give_x = rcopy(xpart.at[spot, :], xrecv1.at[0], s_give, member(1))
            go(give_x)
    phase("b1_xwait")
    ptbuf[...] = onehot_pt(0)
    come(give_x)
    t_own = xpart[span(rank[1], skel), :] + xrecv1[0]

    phase("b0_q")
    s_q = slots_y0
    for k in cross[0] + along[0]:
        at_k = pl.ds(k * skel, skel)
        if k % 2:
            two = slice(k, k + 2)
            qsend[0, k * skel:(k + 2) * skel, :] = dot_left_of(
                k0h[two].reshape(2 * skel, skel), k0l[two].reshape(2 * skel, skel), t_own, NN)
        there, dev = neighbour(0, k)
        go(rcopy(qsend.at[0, at_k, :], qrecv.at[0, OPPOSITE[k] - 1], s_q[k], dev), there)
    u = dot_left_of(k0h[0], k0l[0], t_own, NN)
    for k in cross[0] + along[0]:
        phase(f"b0_wait{k}")
        there, dev = neighbour(0, k)
        come(rcopy(qsend.at[0, pl.ds(k * skel, skel), :], qrecv.at[0, k - 1], s_q[OPPOSITE[k]], dev), there)
        u = u + qrecv[0, k - 1]
    phase("b0_x")
    xr = ypart[0] - dot_left(g0[...], u, NN)
    abuf[skel:, :] = xr
    abuf[:skel, :] = t_own - dot_left(t0[...], xr, NN)
    phase("b0_out")
    rhs[...] = pick_right(abuf[...], ptbuf[...], TN)
    result = pltpu.make_async_copy(rhs, out.at[0, 0], local.at[0])
    result.start()

    assert count[0] <= send.shape[0], count[0]
    phase("drain")
    for when, make in pending:
        if when is None:
            make().wait_send()
        else:
            @pl.when(when)
            def _():
                make().wait_send()

    @pl.when(inner)
    def _():
        for k in has[3]:
            @pl.when(neighbour(3, k)[0])
            def _():
                y3_copy(k).wait_send()
                q3_copy(k).wait_send()
        for m in (4, 1):
            down_copy(m).wait_send()

    @pl.when(outer)
    def _():
        for k in has[2]:
            @pl.when(beside(k)[0])
            def _():
                q2_copy(k).wait_send()
        for m in (4, 1):
            up_copy(m).wait_send()
        for m in (3, 1, 2):
            out_copy(m).wait_send()
    result.wait()
    phase(None)


def body(size_x, size_y, right_sides, skeleton_order, *weights):
    rows = right_sides.shape[2]
    box = right_sides.shape[3]
    skel = box // 2
    weights = [jnp.swapaxes(w, -1, -2) if w.shape[-1] < skel else w for w in weights]
    vm = lambda *shape: pltpu.VMEM(shape, F32)
    half_of = lambda *shape: pltpu.VMEM(shape, BF16)
    widths = [skel >> level for level in range(4)]
    half, share = rows // 2, rows // 4
    kinds = 5 if size_y > REACH[3][1] else 3
    slots = 49 + kinds
    lanes = -(-widths[1] // 128) * 128
    scratch = [
        vm(rows, box), pltpu.VMEM((4, box), jnp.int32), vm(skel, skel), vm(2, widths[1], skel),
        vm(skel, skel), vm(2, widths[1], skel), vm(5, skel, skel), vm(5, widths[1], skel),
        vm(2, 5 * skel, rows), vm(box, rows), vm(2, 5 * skel, rows), vm(2, 4, skel, rows),
        vm(1, skel, rows), vm(box, rows), vm(box, rows),
        vm(box, rows), vm(2, skel, rows), vm(1, skel, rows),
        pltpu.VMEM((box, box), BF16), pltpu.VMEM((box, 8), jnp.int32),
        vm(skel, rows), vm(widths[1], rows), vm(2, widths[1], widths[1]), vm(skel, widths[1]), vm(2, 2, widths[1], widths[1]),
        vm(skel, rows), vm(2, widths[1], rows), vm(2, widths[1], rows),
        half_of(5, skel, skel), half_of(5, skel, skel), half_of(skel, box), half_of(skel, box),
        half_of(7, skel, skel), half_of(7, skel, skel), half_of(3 + kinds, skel, skel), half_of(3 + kinds, skel, skel),
        vm(7, 4, widths[2], skel), vm(rows, lanes), vm(4, half, lanes),
        vm(half, skel), vm(4, half, skel), vm(4, half, skel), vm(4, half, skel),
        vm(2, half, skel), vm(rows, skel), pltpu.VMEM((4 * lanes, box), BF16), vm(half, skel), vm(half, skel),
        vm(3 + kinds, 8, widths[3], skel), vm(2, share, skel),
        vm(share, skel), vm(kinds - 1, share, skel), vm(kinds - 1, share, skel), vm(kinds - 1, share, skel),
        vm(2, share, skel), pltpu.VMEM((box, box), BF16),
        pltpu.SemaphoreType.DMA((15,)), pltpu.SemaphoreType.REGULAR,
        pltpu.SemaphoreType.DMA((slots,)), pltpu.SemaphoreType.DMA((slots,)),
    ]
    return pl.pallas_call(
        functools.partial(kernel, size_x, size_y),
        out_shape=jax.ShapeDtypeStruct(right_sides.shape, F32),
        in_specs=[pl.BlockSpec(memory_space=pl.ANY)] * (2 + len(weights)),
        out_specs=pl.BlockSpec(memory_space=pl.ANY),
        scratch_shapes=scratch,
        compiler_params=pltpu.CompilerParams(
            collective_id=0, has_side_effects=True, vmem_limit_bytes=48 * 2**20
        ),
    )(*[pltpu.with_memory_space_constraint(a, pltpu.HBM) for a in (right_sides, skeleton_order, *weights)])


def solution(mesh):
    four = P("bx", "by", None, None)
    five = P("bx", "by", None, None, None)
    in_specs = (four,) * 10 + (five,) * 4 + (four,)
    return jax.shard_map(
        functools.partial(body, mesh.shape["bx"], mesh.shape["by"]),
        mesh=mesh, in_specs=in_specs, out_specs=four, check_vma=False,
    )
```

```python
import functools

import jax
import jax.numpy as jnp
from jax import lax
from jax.experimental import pallas as pl
from jax.experimental.pallas import tpu as pltpu
from jax.sharding import PartitionSpec as P

REACH = ((1, 1), (1, 2), (2, 2), (2, 4))
OPPOSITE = {1: 2, 2: 1, 3: 4, 4: 3}
F32 = jnp.float32
BF16 = jnp.bfloat16
MESH = pl.DeviceIdType.MESH
NN = (((1,), (0,)), ((), ()))
TN = (((0,), (0,)), ((), ()))
NT = (((1,), (1,)), ((), ()))


def halves(x):
    high = x.astype(BF16)
    return high, (x - high.astype(F32)).astype(BF16)


def product(a, b, dims):
    return lax.dot_general(a, b, dims, preferred_element_type=F32)


def dot3(a, b, dims):
    ah, al = halves(a)
    bh, bl = halves(b)
    return product(ah, bh, dims) + (product(ah, bl, dims) + product(al, bh, dims))


def lanes_summed(x):
    wide = x.shape[1] // 2
    return x[:, :wide] + x[:, wide:]


def rows_summed(x):
    tall = x.shape[0] // 2
    return x[:tall] + x[tall:]


def dot_left(a, b, dims):
    ah, al = halves(a)
    bh, bl = halves(b)
    return lanes_summed(product(ah, jnp.concatenate([bh, bl], axis=1), dims)) + product(al, bh, dims)


def dot_right(a, b, dims):
    ah, al = halves(a)
    bh, bl = halves(b)
    return rows_summed(product(jnp.concatenate([ah, al], axis=0), bh, dims)) + product(ah, bl, dims)


def pick_left(onehot, b, dims):
    return lanes_summed(product(onehot, jnp.concatenate(halves(b), axis=1 if dims == NN else 0), dims))


def pick_right(a, onehot, dims):
    if dims == TN:
        return rows_summed(product(jnp.concatenate(halves(a), axis=1), onehot, dims))
    return rows_summed(product(jnp.concatenate(halves(a), axis=0), onehot, dims))


def dot_left_of(ah, al, b, dims):
    bh, bl = halves(b)
    return lanes_summed(product(ah, jnp.concatenate([bh, bl], axis=1), dims)) + product(al, bh, dims)


def dot_right_of(a, bh, bl, dims):
    ah, al = halves(a)
    return rows_summed(product(jnp.concatenate([ah, al], axis=0), bh, dims)) + product(ah, bl, dims)


class Phases:
    def __init__(self):
        self.scope = None

    def __call__(self, name):
        if self.scope:
            self.scope.__exit__(None, None, None)
        self.scope = jax.named_scope(name) if name else None
        if self.scope:
            self.scope.__enter__()


def kernel(size_x, size_y, *refs):
    (rhs_in, order_in, t0_in, t1_in, t2_in, t3_in, g0_in, g1_in, g2_in, g3_in,
     k0_in, k1_in, k2_in, k3_in, root_in, out) = refs[:16]
    (rhs, order_row, t0, tg1, g0, g1, k0, k1,
     ybuf, vbuf, qsend, qrecv, xrecv1, xpart, base1,
     abuf, ypart, ssend, ptbuf, order_col, wbuf, wpart, kgive, kturn, krows, tfull, nsend, nrecv,
     k0h, k0l, n1h, n1l, midh, midl, toph, topl, mid, turned, v2, y2, yr2, q2, qr2, x2, back2, pick2, turn2, t2,
     top, v3, y3, yr3, q3, qr3, x3, pick3, pair, pairh, pairl, yq, x3n, qn2, local, ready, send, recv) = refs[16:]
    skel = t0.shape[0]
    box = 2 * skel
    rhs_count = ybuf.shape[2]
    half, share = v2.shape[1], v3.shape[1]
    kinds = top.shape[0] - 3
    phase = Phases()
    i, j = lax.axis_index("bx"), lax.axis_index("by")
    bits = (lax.rem(j, 2), lax.rem(i, 2), lax.rem(lax.div(j, 2), 2))
    inner = bits[0] != bits[2]
    outer = jnp.logical_not(inner)

    def flipped(b, m):
        return (1 - bits[b]) if m >> b & 1 else bits[b]

    def member(m):
        return (i + (flipped(1, m) - bits[1]), j + (flipped(0, m) - bits[0]) + 2 * (flipped(2, m) - bits[2]))

    def rank_of(level, m):
        rank = jnp.int32(0)
        for b in range(level):
            rank = rank + (1 << b) * flipped(b, m)
        return rank

    def span(start, size):
        return pl.ds(pl.multiple_of(start * size, size), size)

    def neighbour(level, k):
        rx, ry = REACH[level]
        if k == 1:
            return i >= rx, (i - rx, j)
        if k == 2:
            return i + rx < size_x, (i + rx, j)
        if k == 3:
            return j >= ry, (i, j - ry)
        return j + ry < size_y, (i, j + ry)

    has = [[k for k in (1, 2, 3, 4) if (REACH[l][0] < size_x if k < 3 else REACH[l][1] < size_y)] for l in range(4)]
    cross = [[k for k in has[l] if k < 3] for l in range(4)]
    along = [[k for k in has[l] if k > 2] for l in range(4)]

    count = [0]
    pending = []

    def slot():
        count[0] += 1
        return count[0] - 1

    def rcopy(src, dst, s, dev):
        return pltpu.make_async_remote_copy(src, dst, send.at[s], recv.at[s], device_id=dev, device_id_type=MESH)

    def go(c, when=None):
        make = c if callable(c) else lambda: c
        entry = (when, make)
        pending.append(entry)
        if when is None:
            make().start()
        else:
            @pl.when(when)
            def _():
                make().start()
        return entry

    def settle(entries):
        for when, make in entries:
            if when is None:
                make().wait_send()
            else:
                @pl.when(when)
                def _():
                    make().wait_send()
        pending[:] = [entry for entry in pending if not any(entry is e for e in entries)]

    def come(c, when=None):
        if when is None:
            c.wait_recv()
        else:
            @pl.when(when)
            def _():
                c.wait_recv()

    phase("start")
    rank = [rank_of(l, 0) for l in range(4)]
    loads = {}

    def load(name, src, dst):
        c = pltpu.make_async_copy(src, dst, local.at[len(loads)])
        loads[name] = c
        c.start()

    def need(*names):
        for name in names:
            loads[name].wait()

    load("order", order_in.at[0, 0], order_row)
    load("t0", t0_in.at[0, 0], t0)
    load("g0", g0_in.at[0, 0], g0)
    load("rhs", rhs_in.at[0, 0], rhs)
    load("t1", t1_in.at[0, 0], tg1.at[rank[1]])
    load("k0", k0_in.at[0, 0], k0)
    load("g1", g1_in.at[0, 0], g1.at[rank[1]])
    load("t2", t2_in.at[0, 0], mid.at[0, rank[2]])
    load("g2", g2_in.at[0, 0], mid.at[1, rank[2]])
    load("k2", k2_in.at[0, 0], mid.at[pl.ds(2, 5), rank[2]])
    load("kn", k2_in.at[0, 0, 4 - bits[2]], pair.at[rank[3]])
    load("t3", t3_in.at[0, 0], top.at[0, rank[3]])
    load("g3", g3_in.at[0, 0], top.at[1, rank[3]])
    load("root", root_in.at[0, 0], top.at[2, rank[3]])
    load("k3", k3_in.at[0, 0, pl.ds(0, kinds)], top.at[pl.ds(3, kinds), rank[3]])
    load("k1", k1_in.at[0, 0], k1)

    barrier = pltpu.get_barrier_semaphore()
    for m in range(1, 8):
        pl.semaphore_signal(barrier, 1, device_id=member(m), device_id_type=MESH)
    total = jnp.int32(7)
    greeted = set()
    for level in range(4):
        for k in has[level]:
            key = (k, REACH[level][0] if k < 3 else REACH[level][1])
            if key in greeted:
                continue
            greeted.add(key)
            there, dev = neighbour(level, k)

            @pl.when(there)
            def _():
                pl.semaphore_signal(barrier, 1, device_id=dev, device_id_type=MESH)
            total = total + there.astype(jnp.int32)

    for level in range(2):
        for k in (1, 2, 3, 4):
            there, _ = neighbour(level, k)

            @pl.when(jnp.logical_not(there))
            def _():
                ybuf[level, k * skel:(k + 1) * skel, :] = jnp.zeros((skel, rhs_count), F32)
                qrecv[level, k - 1] = jnp.zeros((skel, rhs_count), F32)
    for k in along[1]:
        there, _ = neighbour(1, k)

        @pl.when(jnp.logical_not(there))
        def _():
            nrecv[k - 3] = jnp.zeros(nrecv.shape[1:], F32)
    turned[...] = jnp.zeros_like(turned)

    chunks = range((top.shape[0] + 1) // 2)
    last = len(chunks)
    slots_in, slots_on = ([slot() for _ in range(last + 1)] for _ in range(2))
    slots_mate = [slot() for _ in range(4)]
    slots_pair = [slot() for _ in range(4)]
    slots_mid = [slot() for _ in range(7)]
    slots_own = slots_mid[:last + 1]
    among = slots_in + slots_on + slots_mate + slots_pair
    among = among + [slot() for _ in range(14 - len(among))]
    slots_mid_own, slots_mid_on = among[:7], among[7:14]

    def chunk_copy(c, block, dev, s):
        if c == last:
            return rcopy(pair.at[block], pair.at[block], s, dev)
        at = pl.ds(2 * c, min(2, top.shape[0] - 2 * c))
        return rcopy(top.at[at, block], top.at[at, block], s, dev)

    def mate_copy(n, mine):
        block = rank_of(3, (0, 1, 5, 4)[n] ^ (0 if mine else 2))
        return rcopy(top.at[:, block], top.at[:, block], slots_mate[n], member(2))

    def pair_copy(n, mine):
        block = rank_of(3, (0, 1, 5, 4)[n] ^ (0 if mine else 2))
        return rcopy(pair.at[block], pair.at[block], slots_pair[n], member(2))

    def outer_send(c):
        go(chunk_copy(c, rank[3], member(1), slots_own[c]), outer)

    def inner_send():
        for c in range(last + 1):
            go(chunk_copy(c, rank[3], member(5), slots_in[c]), inner)

    def inner_forward(c):
        come(chunk_copy(c, rank_of(3, 1), member(1), slots_own[c]), inner)
        go(chunk_copy(c, rank_of(3, 1), member(5), slots_on[c]), inner)

    def mate_send(n):
        for c in range(last + 1):
            if n == 2:
                come(chunk_copy(c, rank_of(3, 5), member(5), slots_in[c]), inner)
            if n == 3:
                come(chunk_copy(c, rank_of(3, 4), member(5), slots_on[c]), inner)
        go(lambda: mate_copy(n, True), inner)
        go(lambda: pair_copy(n, True), inner)

    sides = cross[2] + (along[2] if size_y > REACH[3][1] else [])
    near = [None, None, None] + [neighbour(2, k)[0] for k in (1, 2)] + [
        jnp.logical_and(neighbour(2, 3)[0], bits[2] == 0), jnp.logical_and(neighbour(2, 4)[0], bits[2] == 1)]

    near_in = [inner if there is None else jnp.logical_and(inner, there) for there in near]
    near_out = [outer if there is None else jnp.logical_and(outer, there) for there in near]

    def mid_copy(n, m, to, s):
        block = rank_of(2, m)
        return rcopy(mid.at[n, block], mid.at[n, block], s, member(to))

    def used(n):
        return n < 3 or n - 2 in sides

    def mid_send(*wanted):
        for n in filter(used, wanted):
            go(mid_copy(n, 0, 1, slots_mid[n]), near_in[n])

    def mid_share(*wanted):
        for n in filter(used, wanted):
            go(mid_copy(n, 0, 2, slots_mid_own[n]), near_out[n])

    def mid_forward(*wanted):
        for n in filter(used, wanted):
            come(mid_copy(n, 1, 1, slots_mid[n]), near_out[n])
            go(lambda n=n: mid_copy(n, 1, 2, slots_mid_on[n]), near_out[n])

    def mid_full(n):
        come(mid_copy(n, 2, 2, slots_mid_own[n]), near[n])
        come(mid_copy(n, 3, 2, slots_mid_on[n]), near[n])

    def onehot_pt(level):
        lanes = lax.broadcasted_iota(jnp.int32, (box, box), 1)
        return jnp.where(lanes == order_col[:, level:level + 1], 1.0, 0.0).astype(BF16)

    def onehot_p(level):
        rows = lax.broadcasted_iota(jnp.int32, (box, box), 0)
        return jnp.where(rows == order_row[level:level + 1, :], 1.0, 0.0).astype(BF16)

    need("order")
    order_f = order_row[...].astype(F32)
    order_f = jnp.concatenate([order_f, jnp.zeros((8 - order_f.shape[0], box), F32)], axis=0)
    order_col[...] = order_f.T.astype(jnp.int32)

    phase("f0_a")
    need("rhs")
    abuf[...] = pick_left(onehot_pt(0), rhs[...], NT)
    phase("f0_y")
    need("t0", "g0")
    y_own = dot_left(g0[...], abuf[skel:, :] - dot_left(t0[...], abuf[:skel, :], TN), TN)
    ybuf[0, :skel, :] = y_own
    ypart[0] = y_own
    phase("f0_barrier")
    pl.semaphore_wait(barrier, total)
    phase("f0_send")
    slots_y0 = {k: slot() for k in has[0]}
    early = []
    for k in along[0] + cross[0]:
        there, dev = neighbour(0, k)
        far = OPPOSITE[k]
        early.append(go(rcopy(ypart.at[0], ybuf.at[0, pl.ds(far * skel, skel), :], slots_y0[k], dev), there))
    need("t2", "g2", "k2", "kn", "t3", "g3", "root", "k3")
    mid_send(0)
    outer_send(0)
    inner_send()
    mate_send(0)
    phase("f0_split")
    need("k0")
    for k in range(5):
        k0h[k], k0l[k] = halves(k0[k])
    phase("f0_s")
    s_own = abuf[:skel, :] - dot_left_of(k0h[0], k0l[0], ypart[0], TN)
    ptbuf[...] = onehot_pt(1)
    for k in cross[0] + along[0]:
        there, dev = neighbour(0, k)
        phase(f"f0_wait{k}")
        come(rcopy(ypart.at[0], ybuf.at[0, pl.ds(k * skel, skel), :], slots_y0[OPPOSITE[k]], dev), there)
        phase(f"f0_s{k}")
        s_own = s_own - dot_left_of(k0h[k], k0l[k], ybuf[0, k * skel:(k + 1) * skel, :], TN)
    ssend[0] = s_own
    vbuf[span(rank[1], skel), :] = s_own
    s_give = slot()
    give = rcopy(ssend.at[0], vbuf.at[span(rank[1], skel), :], s_give, member(1))
    early.append(go(give))
    mid_send(1)
    outer_send(1)
    mid_share(*range(7))
    phase("f0_gwait")
    need("t1", "g1", "k1")
    come(give)

    phase("f1_a")
    cols = skel >> 1
    rows = span(rank[1], cols)
    abuf[...] = pick_left(ptbuf[...], vbuf[...], NN)
    phase("f1_w")
    w_own = abuf[pl.ds(pl.multiple_of(skel + rank[1] * cols, cols), cols), :] - dot_left(tg1[rank[1]], abuf[:skel, :], NN)
    wpart[...] = w_own
    wbuf[rows, :] = w_own
    give_w = rcopy(wpart, wbuf.at[rows, :], slot(), member(1))
    go(give_w)
    ptbuf[...] = onehot_p(1)
    phase("f1_wwait")
    come(give_w)
    phase("f1_y")
    y_own = dot_left(g1[rank[1]], wbuf[...], NN)
    ypart[1, :cols, :] = y_own
    ybuf[1, rows, :] = y_own

    def at(k, m):
        return ybuf.at[1, pl.ds(pl.multiple_of(k * skel + rank_of(1, m) * cols, cols), cols), :]

    own_src = ypart.at[1, pl.ds(0, cols), :]
    s_a = slot()
    s_c = {k: [slot(), slot()] for k in cross[1]}
    s_b = {k: slot() for k in along[1]}
    s_d = {k: slot() for k in along[1]}
    phase("f1_send")
    mate = rcopy(own_src, at(0, 0), s_a, member(1))
    go(mate)
    for k in along[1]:
        there, dev = neighbour(1, k)
        early.append(go(rcopy(own_src, at(OPPOSITE[k], 0), s_b[k], dev), there))
    for k in cross[1]:
        there, dev = neighbour(1, k)
        early.append(go(rcopy(own_src, at(OPPOSITE[k], 0), s_c[k][0], dev), there))
    mid_send(2)
    outer_send(2)
    base1[:skel, :] = -dot_left(tg1[rank[1]], y_own, TN)
    base1[skel:, :] = jnp.zeros((skel, rhs_count), F32)
    base1[pl.ds(pl.multiple_of(skel + rank[1] * cols, cols), cols), :] = y_own
    phase("f1_ywait")
    come(mate)
    for k in cross[1]:
        there, dev = neighbour(1, k)
        go(rcopy(at(0, 1), at(OPPOSITE[k], 1), s_c[k][1], dev), there)
    inner_forward(0)
    mid_forward(0)
    phase("f1_s0")
    s_own = abuf[rows, :] - dot_left(k1[0], ybuf[1, :skel, :], NN)
    phase("f1_relay")
    for k in cross[1]:
        there, dev = neighbour(1, k)
        come(rcopy(own_src, at(k, 0), s_c[OPPOSITE[k]][0], dev), there)
    for k in along[1]:
        there, dev = neighbour(1, k)
        come(rcopy(own_src, at(k, 0), s_b[OPPOSITE[k]], dev), there)
        go(rcopy(at(k, 0), at(k, 0), s_d[k], member(1)), there)
    mid_send(3)
    for k in cross[1]:
        there, dev = neighbour(1, k)
        phase(f"f1_cross{k}")
        come(rcopy(own_src, at(k, 1), s_c[OPPOSITE[k]][1], dev), there)
        s_own = s_own - dot_left(k1[k], ybuf[1, k * skel:(k + 1) * skel, :], NN)
    for k in along[1]:
        there, dev = neighbour(1, k)
        phase(f"f1_along{k}")
        come(rcopy(at(k, 1), at(k, 1), s_d[k], member(1)), there)
        s_own = s_own - dot_left(k1[k], ybuf[1, k * skel:(k + 1) * skel, :], NN)
    turned[:, :cols] = s_own.T

    phase("l2_send")
    s_t2 = {m: slot() for m in (1, 2, 3)}
    half_of = lambda m: span(flipped(1, m), half)
    go(rcopy(turned.at[half_of(1)], v2.at[rank[2]], s_t2[1], member(1)), inner)
    go(rcopy(turned.at[half_of(3)], v2.at[rank[2]], s_t2[3], member(3)), inner)
    across = go(rcopy(turned.at[half_of(2)], v2.at[rank[2]], s_t2[2], member(2)), outer)
    pending.pop()
    mid_send(4, 5, 6)
    outer_send(last)
    s_t1 = [slot(), slot(), slot()]
    s_k1 = {k: slot() for k in along[1]}
    near1 = {k: neighbour(1, k)[0] for k in along[1]}
    near1_in = {k: jnp.logical_and(inner, near1[k]) for k in along[1]}
    near1_out = {k: jnp.logical_and(outer, near1[k]) for k in along[1]}
    t1_copy = lambda: rcopy(tg1.at[rank[1]], tg1.at[rank[1]], s_t1[0], member(1))
    part = cols // 2
    g1_part = lambda n: g1.at[rank[1], pl.ds(n * part, part), :]
    g1_copy = lambda n: rcopy(g1_part(n), g1_part(n), s_t1[1 + n], member(1))
    k1_copy = lambda k: rcopy(kgive.at[k - 3], krows.at[k - 3, 1], s_k1[k], member(1))
    others = span(rank_of(1, 1), cols)
    for k in along[1]:
        @pl.when(near1[k])
        def _():
            kturn[...] = k1[k].T
            krows[k - 3, 0] = kturn[rows, :]
            kgive[k - 3] = kturn[others, :]
    part = cols // 2
    g1_part = lambda n: g1.at[rank[1], pl.ds(n * part, part), :]
    g1_copy = lambda n: rcopy(g1_part(n), g1_part(n), s_t1[1 + n], member(1))

    def late_send(when, near, *wanted):
        for n in wanted:
            if n == 3:
                for k in along[1]:
                    go(lambda k=k: k1_copy(k), near[k])
            else:
                go(t1_copy if n == 0 else lambda n=n: g1_copy(n - 1), when)

    def late_make():
        come(t1_copy())
        come(g1_copy(0))
        come(g1_copy(1))
        own = g1[...].reshape(skel, skel)
        n1h[:, :skel], n1l[:, :skel] = halves(-dot3(own, tg1[...].reshape(skel, skel), NN))
        n1h[:, skel:], n1l[:, skel:] = halves(own)

    inner_forward(1)
    inner_forward(2)
    inner_forward(last)

    def wide_pick(pick, level, width, lanes):
        o = order_row[level:level + 1, :]
        o = o + sum((lanes - width) * (o >= width * b).astype(jnp.int32) for b in range(1, box // width))
        lines = lax.broadcasted_iota(jnp.int32, pick.shape, 0)
        pick[...] = jnp.where(lines == o, 1.0, 0.0).astype(BF16)

    def beside(k):
        to = neighbour(2, k)[1] if k < 3 else (i, j + 1 if k == 4 else j - 1)
        return near[2 + k], to

    s_y2 = s_q2 = {k: slot() for k in sides}
    s_y3 = {k: s_y2[k] for k in has[3]}
    s_q3 = {k: slot() for k in has[3]}
    s_t3 = s_x3 = {m: slot() for m in (1, 4)}
    s_x2 = s_t2
    quarter_of = lambda m: span(flipped(2, m), share)
    y2_copy = lambda k: rcopy(y2, yr2.at[OPPOSITE[k] - 1], s_y2[k], beside(k)[1])
    q2_copy = lambda k: rcopy(q2.at[k - 1], qr2.at[OPPOSITE[k] - 1], s_q2[k], beside(k)[1])
    y3_copy = lambda k: rcopy(y3, yr3.at[OPPOSITE[k] - 1], s_y3[k], neighbour(3, k)[1])
    q3_copy = lambda k: rcopy(q3.at[k - 1], qr3.at[OPPOSITE[k] - 1], s_q3[k], neighbour(3, k)[1])
    s_yq = {1: slots_mid[5], 4: slots_mid[6]}
    s_qn = {m: slot() for m in (1, 4)}
    yq_copy = lambda m: rcopy(y2.at[quarter_of(m)], yq.at[bits[2]], s_yq[m], member(m))
    qn_copy = lambda m: rcopy(x3n.at[flipped(2, m)], qn2.at[quarter_of(0)], s_qn[m], member(m))
    up_copy = lambda m: rcopy(turn2.at[quarter_of(m)], v3.at[bits[2]], s_t3[m], member(m))
    down_copy = lambda m: rcopy(x3.at[flipped(2, m)], t2.at[quarter_of(0)], s_x3[m], member(m))
    out_copy = lambda m: rcopy(x2.at[flipped(1, m)], back2.at[half_of(0)], s_x2[m], member(m))

    @pl.when(outer)
    def _():
        phase("l2_pick")
        wide_pick(pick2, 2, cols, turned.shape[1])
        mid_forward(1)
        full = lambda n: mid[n].reshape(skel, skel)
        for n in (0, 1):
            mid_full(n)
            midh[n], midl[n] = halves(full(n))
        v2[rank[2]] = turned[half_of(0), :]
        phase("l2_in")
        come(rcopy(turned.at[half_of(0)], v2.at[rank_of(2, 2)], s_t2[2], member(2)))
        come(rcopy(turned.at[half_of(0)], v2.at[rank_of(2, 1)], s_t2[1], member(1)))
        come(rcopy(turned.at[half_of(0)], v2.at[rank_of(2, 3)], s_t2[3], member(3)))
        phase("l2_a")
        a = pick_right(jnp.concatenate([v2[b] for b in range(4)], axis=1), pick2[...], NN)
        s0, r0 = a[:, :skel], a[:, skel:]
        phase("l2_y")
        y = dot_right_of(r0 - dot_right_of(s0, midh[0], midl[0], NT), midh[1], midl[1], NT)
        y2[...] = y
        for m in (4, 1):
            yq_copy(m).start()
        for k in sides:
            @pl.when(beside(k)[0])
            def _():
                y2_copy(k).start()
        phase("l2_s")
        mid_forward(2)
        mid_full(2)
        turn2[...] = s0 - dot_right(y, full(2), NT)
        for k in sides:
            mid_forward(2 + k)
        for k in sides:
            phase(f"l2_s{k}")

            @pl.when(beside(k)[0])
            def _():
                mid_full(2 + k)
                rcopy(y2, yr2.at[k - 1], s_y2[OPPOSITE[k]], beside(k)[1]).wait_recv()
                turn2[...] = turn2[...] - dot_right(yr2[k - 1], full(2 + k), NT)
        for m in (4, 1):
            up_copy(m).start()
        late_send(outer, near1_out, 0, 1, 2, 3)
        phase("l2_split")
        midh[2], midl[2] = halves(full(2))
        for k in sides:
            @pl.when(beside(k)[0])
            def _():
                midh[2 + k], midl[2 + k] = halves(full(2 + k))
        phase(None)

    @pl.when(inner)
    def _():
        phase("l3_pick")
        wide_pick(pick3, 3, skel, skel)
        for n in (1, 2, 3):
            mate_send(n)
        for n in range(4):
            come(mate_copy(n, False))
            come(pair_copy(n, False))
        for n in range(3 + kinds):
            toph[n], topl[n] = halves(top[n].reshape(skel, skel))
        for n in range(2):
            pairh[n], pairl[n] = halves(pair[4 * n:4 * n + 4].reshape(skel, skel))
        phase("l3_pair")
        for m in (1, 4):
            come(rcopy(y2.at[quarter_of(0)], yq.at[flipped(2, m)], s_yq[m], member(m)))
        for n in range(2):
            x3n[n] = dot_right_of(yq[1 - n], pairh[n], pairl[n], NT)
        phase("l3_in")
        for m in (1, 4):
            come(rcopy(turn2.at[quarter_of(0)], v3.at[flipped(2, m)], s_t3[m], member(m)))
        late_send(inner, near1_in, 0, 1)
        phase("l3_y")
        a = pick_right(jnp.concatenate([v3[0] - x3n[0], v3[1] - x3n[1]], axis=1), pick3[...], NN)
        s0, r0 = a[:, :skel], a[:, skel:]
        y = dot_right_of(r0 - dot_right_of(s0, toph[0], topl[0], NT), toph[1], topl[1], NT)
        y3[...] = y
        for k in has[3]:
            @pl.when(neighbour(3, k)[0])
            def _():
                y3_copy(k).start()
        phase("l3_s")
        v3[0] = s0 - dot_right_of(y, toph[3], topl[3], NT)
        for k in has[3]:
            phase(f"l3_s{k}")

            @pl.when(neighbour(3, k)[0])
            def _():
                rcopy(y3, yr3.at[k - 1], s_y3[OPPOSITE[k]], neighbour(3, k)[1]).wait_recv()
                v3[0] = v3[0] - dot_right_of(yr3[k - 1], toph[3 + k], topl[3 + k], NT)
        phase("l3_q")
        t = dot_right_of(v3[0], toph[2], topl[2], NT)
        for k in has[3]:
            @pl.when(neighbour(3, k)[0])
            def _():
                q3[k - 1] = dot_right_of(t, toph[3 + k], topl[3 + k], NN)
                q3_copy(k).start()
        v3[0] = dot_right_of(t, toph[3], topl[3], NN)
        for k in has[3]:
            phase(f"l3_u{k}")

            @pl.when(neighbour(3, k)[0])
            def _():
                rcopy(q3.at[k - 1], qr3.at[k - 1], s_q3[OPPOSITE[k]], neighbour(3, k)[1]).wait_recv()
                v3[0] = v3[0] + qr3[k - 1]
        phase("l3_x")
        xr = y - dot_right_of(v3[0], toph[1], topl[1], NN)
        xs = t - dot_right_of(xr, toph[0], topl[0], NN)
        xv = pick_right(jnp.concatenate([xs, xr], axis=1), pick3[...], NT)
        x3[0], x3[1] = xv[:, :skel], xv[:, skel:]
        for m in (4, 1):
            down_copy(m).start()
        for n in range(2):
            x3n[1 - n] = dot_right_of(x3[n], pairh[n], pairl[n], NN)
        for m in (4, 1):
            qn_copy(m).start()
        pl.semaphore_wait(ready, 1)
        late_send(inner, near1_in, 3, 2)
        phase(None)

    @pl.when(outer)
    def _():
        phase("l2_tin")
        pick2[:box, :] = onehot_p(2)
        for m in (1, 4):
            come(rcopy(x3.at[bits[2]], t2.at[quarter_of(m)], s_x3[m], member(m)))
        pl.semaphore_signal(ready, 1, device_id=member(1), device_id_type=MESH)
        phase("l2_q")
        t = t2[...]
        for k in reversed(sides):
            @pl.when(beside(k)[0])
            def _():
                q2[k - 1] = dot_right_of(t, midh[2 + k], midl[2 + k], NN)
                y2_copy(k).wait_send()
                q2_copy(k).start()
        yr2[0] = dot_right_of(t, midh[2], midl[2], NN)
        for k in sides:
            phase(f"l2_u{k}")

            @pl.when(beside(k)[0])
            def _():
                rcopy(q2.at[k - 1], qr2.at[k - 1], s_q2[OPPOSITE[k]], beside(k)[1]).wait_recv()
                yr2[0] = yr2[0] + qr2[k - 1]
        phase("l2_qn")
        for m in (1, 4):
            come(rcopy(x3n.at[bits[2]], qn2.at[quarter_of(m)], s_qn[m], member(m)))
        yr2[0] = yr2[0] + qn2[...]
        phase("l2_x")
        xr = y2[...] - dot_right_of(yr2[0], midh[1], midl[1], NN)
        xs = t - dot_right_of(xr, midh[0], midl[0], NN)
        x = jnp.concatenate([xs, xr], axis=1)
        x2[bits[1]] = pick_right(x, pick2[span(bits[1], skel), :], NT)
        out_copy(1).start()
        x2[1 - bits[1]] = pick_right(x, pick2[span(1 - bits[1], skel), :], NT)
        out_copy(3).start()
        across[1]().wait_send()
        out_copy(2).start()
        back2[half_of(0), :] = x2[bits[1]]
        phase(None)

    phase("l2_out")
    come(rcopy(x2.at[bits[1]], back2.at[half_of(2)], s_x2[2], member(2)), outer)
    for m in (1, 3):
        come(rcopy(x2.at[bits[1]], back2.at[half_of(m)], s_x2[m], member(m)), inner)

    phase("b1_settle")
    settle(early)
    phase("b1_q")
    tfull[...] = back2[...].T
    t_own = tfull[rows, :]
    s_q = {k: s_c[k][0] if k < 3 else s_b[k] for k in has[1]}
    for k in cross[1]:
        at_k = pl.ds(k * skel, skel)
        qsend[1, at_k, :] = dot_left(k1[k], t_own, TN)
        there, dev = neighbour(1, k)
        go(rcopy(qsend.at[1, at_k, :], qrecv.at[1, OPPOSITE[k] - 1], s_q[k], dev), there)
    for k in along[1]:
        there, dev = neighbour(1, k)

        @pl.when(there)
        def _():
            k1_copy(k).wait_recv()
            nsend[k - 3] = dot_left(krows[k - 3, 0], t_own, NN) + dot_left(krows[k - 3, 1], tfull[others, :], NN)
        go(rcopy(nsend.at[k - 3], nrecv.at[OPPOSITE[k] - 3], s_q[k], dev), there)
    phase("b1_q0")
    u = dot_left(k1[0], t_own, TN)
    abuf[...] = base1[...]
    abuf[rows, :] = abuf[rows, :] + t_own
    phase("b1_late")
    late_make()
    for k in cross[1]:
        phase(f"b1_wait{k}")
        there, dev = neighbour(1, k)
        come(rcopy(qsend.at[1, pl.ds(k * skel, skel), :], qrecv.at[1, k - 1], s_q[OPPOSITE[k]], dev), there)
        u = u + qrecv[1, k - 1]
    qsend[1, :skel, :] = u
    for k in along[1]:
        phase(f"b1_wait{k}")
        there, dev = neighbour(1, k)
        come(rcopy(nsend.at[k - 3], nrecv.at[k - 3], s_q[OPPOSITE[k]], dev), there)
        qsend[1, rows, :] = qsend[1, rows, :] + nrecv[k - 3]
    phase("b1_comb")
    abuf[...] = abuf[...] - dot_left_of(n1h[...], n1l[...], qsend[1, :skel, :], TN)
    phase("b1_x")
    both = jnp.concatenate(halves(abuf[...]), axis=1)
    for m in (1, 0):
        spot = span(rank_of(1, m), skel)
        xpart[spot, :] = lanes_summed(product(ptbuf[spot, :], both, NN))
        if m:
            give_x = rcopy(xpart.at[spot, :], xrecv1.at[0], s_give, member(1))
            go(give_x)
    phase("b1_xwait")
    ptbuf[...] = onehot_pt(0)
    come(give_x)
    t_own = xpart[span(rank[1], skel), :] + xrecv1[0]

    phase("b0_q")
    s_q = slots_y0
    for k in cross[0] + along[0]:
        at_k = pl.ds(k * skel, skel)
        if k % 2:
            two = slice(k, k + 2)
            qsend[0, k * skel:(k + 2) * skel, :] = dot_left_of(
                k0h[two].reshape(2 * skel, skel), k0l[two].reshape(2 * skel, skel), t_own, NN)
        there, dev = neighbour(0, k)
        go(rcopy(qsend.at[0, at_k, :], qrecv.at[0, OPPOSITE[k] - 1], s_q[k], dev), there)
    u = dot_left_of(k0h[0], k0l[0], t_own, NN)
    for k in cross[0] + along[0]:
        phase(f"b0_wait{k}")
        there, dev = neighbour(0, k)
        come(rcopy(qsend.at[0, pl.ds(k * skel, skel), :], qrecv.at[0, k - 1], s_q[OPPOSITE[k]], dev), there)
        u = u + qrecv[0, k - 1]
    phase("b0_x")
    xr = ypart[0] - dot_left(g0[...], u, NN)
    abuf[skel:, :] = xr
    abuf[:skel, :] = t_own - dot_left(t0[...], xr, NN)
    phase("b0_out")
    rhs[...] = pick_right(abuf[...], ptbuf[...], TN)
    result = pltpu.make_async_copy(rhs, out.at[0, 0], local.at[0])
    result.start()

    assert count[0] <= send.shape[0], count[0]
    phase("drain")
    for when, make in pending:
        if when is None:
            make().wait_send()
        else:
            @pl.when(when)
            def _():
                make().wait_send()

    @pl.when(inner)
    def _():
        for k in has[3]:
            @pl.when(neighbour(3, k)[0])
            def _():
                y3_copy(k).wait_send()
                q3_copy(k).wait_send()
        for m in (4, 1):
            down_copy(m).wait_send()
            qn_copy(m).wait_send()

    @pl.when(outer)
    def _():
        for k in sides:
            @pl.when(beside(k)[0])
            def _():
                q2_copy(k).wait_send()
        for m in (4, 1):
            up_copy(m).wait_send()
            yq_copy(m).wait_send()
        for m in (3, 1, 2):
            out_copy(m).wait_send()
    result.wait()
    phase(None)


def body(size_x, size_y, right_sides, skeleton_order, *weights):
    rows = right_sides.shape[2]
    box = right_sides.shape[3]
    skel = box // 2
    weights = [jnp.swapaxes(w, -1, -2) if w.shape[-1] < skel else w for w in weights]
    vm = lambda *shape: pltpu.VMEM(shape, F32)
    half_of = lambda *shape: pltpu.VMEM(shape, BF16)
    widths = [skel >> level for level in range(4)]
    half, share = rows // 2, rows // 4
    kinds = 5 if size_y > REACH[3][1] else 3
    slots = 54 if kinds == 3 else 60
    lanes = -(-widths[1] // 128) * 128
    scratch = [
        vm(rows, box), pltpu.VMEM((4, box), jnp.int32), vm(skel, skel), vm(2, widths[1], skel),
        vm(skel, skel), vm(2, widths[1], skel), vm(5, skel, skel), vm(5, widths[1], skel),
        vm(2, 5 * skel, rows), vm(box, rows), vm(2, 5 * skel, rows), vm(2, 4, skel, rows),
        vm(1, skel, rows), vm(box, rows), vm(box, rows),
        vm(box, rows), vm(2, skel, rows), vm(1, skel, rows),
        pltpu.VMEM((box, box), BF16), pltpu.VMEM((box, 8), jnp.int32),
        vm(skel, rows), vm(widths[1], rows), vm(2, widths[1], widths[1]), vm(skel, widths[1]), vm(2, 2, widths[1], widths[1]),
        vm(skel, rows), vm(2, widths[1], rows), vm(2, widths[1], rows),
        half_of(5, skel, skel), half_of(5, skel, skel), half_of(skel, box), half_of(skel, box),
        half_of(7, skel, skel), half_of(7, skel, skel), half_of(3 + kinds, skel, skel), half_of(3 + kinds, skel, skel),
        vm(7, 4, widths[2], skel), vm(rows, lanes), vm(4, half, lanes),
        vm(half, skel), vm(4, half, skel), vm(4, half, skel), vm(4, half, skel),
        vm(2, half, skel), vm(rows, skel), pltpu.VMEM((4 * lanes, box), BF16), vm(half, skel), vm(half, skel),
        vm(3 + kinds, 8, widths[3], skel), vm(2, share, skel),
        vm(share, skel), vm(kinds - 1, share, skel), vm(kinds - 1, share, skel), vm(kinds - 1, share, skel),
        vm(2, share, skel), pltpu.VMEM((box, box), BF16),
        vm(8, widths[2], skel), half_of(2, skel, skel), half_of(2, skel, skel), vm(2, share, skel), vm(2, share, skel), vm(half, skel),
        pltpu.SemaphoreType.DMA((16,)), pltpu.SemaphoreType.REGULAR,
        pltpu.SemaphoreType.DMA((slots,)), pltpu.SemaphoreType.DMA((slots,)),
    ]
    return pl.pallas_call(
        functools.partial(kernel, size_x, size_y),
        out_shape=jax.ShapeDtypeStruct(right_sides.shape, F32),
        in_specs=[pl.BlockSpec(memory_space=pl.ANY)] * (2 + len(weights)),
        out_specs=pl.BlockSpec(memory_space=pl.ANY),
        scratch_shapes=scratch,
        compiler_params=pltpu.CompilerParams(
            collective_id=0, has_side_effects=True, vmem_limit_bytes=(48 if kinds == 3 else 58) * 2**20
        ),
    )(*[pltpu.with_memory_space_constraint(a, pltpu.HBM) for a in (right_sides, skeleton_order, *weights)])


def solution(mesh):
    four = P("bx", "by", None, None)
    five = P("bx", "by", None, None, None)
    in_specs = (four,) * 10 + (five,) * 4 + (four,)
    return jax.shard_map(
        functools.partial(body, mesh.shape["bx"], mesh.shape["by"]),
        mesh=mesh, in_specs=in_specs, out_specs=four, check_vma=False,
    )
```

```python
import functools

import jax
import jax.numpy as jnp
from jax import lax
from jax.experimental import pallas as pl
from jax.experimental.pallas import tpu as pltpu
from jax.sharding import PartitionSpec as P

REACH = ((1, 1), (1, 2), (2, 2), (2, 4))
OPPOSITE = {1: 2, 2: 1, 3: 4, 4: 3}
F32 = jnp.float32
BF16 = jnp.bfloat16
MESH = pl.DeviceIdType.MESH
NN = (((1,), (0,)), ((), ()))
TN = (((0,), (0,)), ((), ()))
NT = (((1,), (1,)), ((), ()))


def halves(x):
    high = x.astype(BF16)
    return high, (x - high.astype(F32)).astype(BF16)


def product(a, b, dims):
    return lax.dot_general(a, b, dims, preferred_element_type=F32)


def dot3(a, b, dims):
    ah, al = halves(a)
    bh, bl = halves(b)
    return product(ah, bh, dims) + (product(ah, bl, dims) + product(al, bh, dims))


def lanes_summed(x):
    wide = x.shape[1] // 2
    return x[:, :wide] + x[:, wide:]


def rows_summed(x):
    tall = x.shape[0] // 2
    return x[:tall] + x[tall:]


def dot_left(a, b, dims):
    ah, al = halves(a)
    bh, bl = halves(b)
    return lanes_summed(product(ah, jnp.concatenate([bh, bl], axis=1), dims)) + product(al, bh, dims)


def dot_right(a, b, dims):
    ah, al = halves(a)
    bh, bl = halves(b)
    return rows_summed(product(jnp.concatenate([ah, al], axis=0), bh, dims)) + product(ah, bl, dims)


def pick_left(onehot, b, dims):
    return lanes_summed(product(onehot, jnp.concatenate(halves(b), axis=1 if dims == NN else 0), dims))


def pick_right(a, onehot, dims):
    if dims == TN:
        return rows_summed(product(jnp.concatenate(halves(a), axis=1), onehot, dims))
    return rows_summed(product(jnp.concatenate(halves(a), axis=0), onehot, dims))


def dot_left_of(ah, al, b, dims):
    bh, bl = halves(b)
    return lanes_summed(product(ah, jnp.concatenate([bh, bl], axis=1), dims)) + product(al, bh, dims)


def dot_right_of(a, bh, bl, dims):
    ah, al = halves(a)
    return rows_summed(product(jnp.concatenate([ah, al], axis=0), bh, dims)) + product(ah, bl, dims)


class Phases:
    def __init__(self):
        self.scope = None

    def __call__(self, name):
        if self.scope:
            self.scope.__exit__(None, None, None)
        self.scope = jax.named_scope(name) if name else None
        if self.scope:
            self.scope.__enter__()


def kernel(size_x, size_y, *refs):
    (rhs_in, order_in, t0_in, t1_in, t2_in, t3_in, g0_in, g1_in, g2_in, g3_in,
     k0_in, k1_in, k2_in, k3_in, root_in, out) = refs[:16]
    (rhs, order_row, t0, tg1, g0, g1, k0, k1,
     ybuf, vbuf, qsend, qrecv, xrecv1, xpart, base1,
     abuf, ypart, ssend, ptbuf, order_col, wbuf, wpart, kgive, kturn, krows, kch, kcl, tfull, nsend, nrecv,
     k0h, k0l, n0h, n0l, base0, n1h, n1l, midh, midl, toph, topl, mid, turned, v2, y2, yr2, q2, qr2, x2, back2, pick2, turn2, t2,
     top, v3, y3, yr3, q3, qr3, x3, pick3, pair, pairh, pairl, yq, x3n, qn2, local, ready, send, recv) = refs[16:]
    skel = t0.shape[0]
    box = 2 * skel
    rhs_count = ybuf.shape[2]
    half, share = v2.shape[1], v3.shape[1]
    kinds = top.shape[0] - 3
    phase = Phases()
    i, j = lax.axis_index("bx"), lax.axis_index("by")
    bits = (lax.rem(j, 2), lax.rem(i, 2), lax.rem(lax.div(j, 2), 2))
    inner = bits[0] != bits[2]
    outer = jnp.logical_not(inner)

    def flipped(b, m):
        return (1 - bits[b]) if m >> b & 1 else bits[b]

    def member(m):
        return (i + (flipped(1, m) - bits[1]), j + (flipped(0, m) - bits[0]) + 2 * (flipped(2, m) - bits[2]))

    def rank_of(level, m):
        rank = jnp.int32(0)
        for b in range(level):
            rank = rank + (1 << b) * flipped(b, m)
        return rank

    def span(start, size):
        return pl.ds(pl.multiple_of(start * size, size), size)

    def neighbour(level, k):
        rx, ry = REACH[level]
        if k == 1:
            return i >= rx, (i - rx, j)
        if k == 2:
            return i + rx < size_x, (i + rx, j)
        if k == 3:
            return j >= ry, (i, j - ry)
        return j + ry < size_y, (i, j + ry)

    has = [[k for k in (1, 2, 3, 4) if (REACH[l][0] < size_x if k < 3 else REACH[l][1] < size_y)] for l in range(4)]
    cross = [[k for k in has[l] if k < 3] for l in range(4)]
    along = [[k for k in has[l] if k > 2] for l in range(4)]

    count = [0]
    pending = []

    def slot():
        count[0] += 1
        return count[0] - 1

    def rcopy(src, dst, s, dev):
        return pltpu.make_async_remote_copy(src, dst, send.at[s], recv.at[s], device_id=dev, device_id_type=MESH)

    def go(c, when=None):
        make = c if callable(c) else lambda: c
        entry = (when, make)
        pending.append(entry)
        if when is None:
            make().start()
        else:
            @pl.when(when)
            def _():
                make().start()
        return entry

    def settle(entries):
        for when, make in entries:
            if when is None:
                make().wait_send()
            else:
                @pl.when(when)
                def _():
                    make().wait_send()
        pending[:] = [entry for entry in pending if not any(entry is e for e in entries)]

    def come(c, when=None):
        if when is None:
            c.wait_recv()
        else:
            @pl.when(when)
            def _():
                c.wait_recv()

    phase("start")
    rank = [rank_of(l, 0) for l in range(4)]
    loads = {}

    def load(name, src, dst):
        c = pltpu.make_async_copy(src, dst, local.at[len(loads)])
        loads[name] = c
        c.start()

    def need(*names):
        for name in names:
            loads[name].wait()

    load("order", order_in.at[0, 0], order_row)
    load("t0", t0_in.at[0, 0], t0)
    load("g0", g0_in.at[0, 0], g0)
    load("rhs", rhs_in.at[0, 0], rhs)
    load("t1", t1_in.at[0, 0], tg1.at[rank[1]])
    load("k0", k0_in.at[0, 0], k0)
    load("g1", g1_in.at[0, 0], g1.at[rank[1]])
    load("t2", t2_in.at[0, 0], mid.at[0, rank[2]])
    load("g2", g2_in.at[0, 0], mid.at[1, rank[2]])
    load("k2", k2_in.at[0, 0], mid.at[pl.ds(2, 5), rank[2]])
    load("kn", k2_in.at[0, 0, 4 - bits[2]], pair.at[rank[3]])
    load("t3", t3_in.at[0, 0], top.at[0, rank[3]])
    load("g3", g3_in.at[0, 0], top.at[1, rank[3]])
    load("root", root_in.at[0, 0], top.at[2, rank[3]])
    load("k3", k3_in.at[0, 0, pl.ds(0, kinds)], top.at[pl.ds(3, kinds), rank[3]])
    load("k1", k1_in.at[0, 0], k1)

    barrier = pltpu.get_barrier_semaphore()
    for m in range(1, 8):
        pl.semaphore_signal(barrier, 1, device_id=member(m), device_id_type=MESH)
    total = jnp.int32(7)
    greeted = set()
    for level in range(4):
        for k in has[level]:
            key = (k, REACH[level][0] if k < 3 else REACH[level][1])
            if key in greeted:
                continue
            greeted.add(key)
            there, dev = neighbour(level, k)

            @pl.when(there)
            def _():
                pl.semaphore_signal(barrier, 1, device_id=dev, device_id_type=MESH)
            total = total + there.astype(jnp.int32)

    chunks = range((top.shape[0] + 1) // 2)
    last = len(chunks)
    slots_in, slots_on = ([slot() for _ in range(last + 1)] for _ in range(2))
    slots_mate = [slot() for _ in range(4)]
    slots_pair = [slot() for _ in range(4)]
    slots_mid = [slot() for _ in range(7)]
    slots_own = slots_mid[:last + 1]
    among = slots_in + slots_on + slots_mate + slots_pair
    among = among + [slot() for _ in range(14 - len(among))]
    slots_mid_own, slots_mid_on = among[:7], among[7:14]

    def chunk_copy(c, block, dev, s):
        if c == last:
            return rcopy(pair.at[block], pair.at[block], s, dev)
        at = pl.ds(2 * c, min(2, top.shape[0] - 2 * c))
        return rcopy(top.at[at, block], top.at[at, block], s, dev)

    def mate_copy(n, mine):
        block = rank_of(3, (0, 1, 5, 4)[n] ^ (0 if mine else 2))
        return rcopy(top.at[:, block], top.at[:, block], slots_mate[n], member(2))

    def pair_copy(n, mine):
        block = rank_of(3, (0, 1, 5, 4)[n] ^ (0 if mine else 2))
        return rcopy(pair.at[block], pair.at[block], slots_pair[n], member(2))

    def outer_send(c):
        go(chunk_copy(c, rank[3], member(1), slots_own[c]), outer)

    def inner_send():
        for c in range(last + 1):
            go(chunk_copy(c, rank[3], member(5), slots_in[c]), inner)

    def inner_forward(c):
        come(chunk_copy(c, rank_of(3, 1), member(1), slots_own[c]), inner)
        go(chunk_copy(c, rank_of(3, 1), member(5), slots_on[c]), inner)

    def mate_send(n):
        for c in range(last + 1):
            if n == 2:
                come(chunk_copy(c, rank_of(3, 5), member(5), slots_in[c]), inner)
            if n == 3:
                come(chunk_copy(c, rank_of(3, 4), member(5), slots_on[c]), inner)
        go(lambda: mate_copy(n, True), inner)
        go(lambda: pair_copy(n, True), inner)

    sides = cross[2] + (along[2] if size_y > REACH[3][1] else [])
    near = [None, None, None] + [neighbour(2, k)[0] for k in (1, 2)] + [
        jnp.logical_and(neighbour(2, 3)[0], bits[2] == 0), jnp.logical_and(neighbour(2, 4)[0], bits[2] == 1)]

    near_in = [inner if there is None else jnp.logical_and(inner, there) for there in near]
    near_out = [outer if there is None else jnp.logical_and(outer, there) for there in near]

    def mid_copy(n, m, to, s):
        block = rank_of(2, m)
        return rcopy(mid.at[n, block], mid.at[n, block], s, member(to))

    def used(n):
        return n < 3 or n - 2 in sides

    def mid_send(*wanted):
        for n in filter(used, wanted):
            go(mid_copy(n, 0, 1, slots_mid[n]), near_in[n])

    def mid_share(*wanted):
        for n in filter(used, wanted):
            go(mid_copy(n, 0, 2, slots_mid_own[n]), near_out[n])

    def mid_forward(*wanted):
        for n in filter(used, wanted):
            come(mid_copy(n, 1, 1, slots_mid[n]), near_out[n])
            go(lambda n=n: mid_copy(n, 1, 2, slots_mid_on[n]), near_out[n])

    def mid_full(n):
        come(mid_copy(n, 2, 2, slots_mid_own[n]), near[n])
        come(mid_copy(n, 3, 2, slots_mid_on[n]), near[n])

    def onehot_pt(level):
        lanes = lax.broadcasted_iota(jnp.int32, (box, box), 1)
        return jnp.where(lanes == order_col[:, level:level + 1], 1.0, 0.0).astype(BF16)

    def onehot_p(level):
        rows = lax.broadcasted_iota(jnp.int32, (box, box), 0)
        return jnp.where(rows == order_row[level:level + 1, :], 1.0, 0.0).astype(BF16)

    need("order")
    order_f = order_row[...].astype(F32)
    order_f = jnp.concatenate([order_f, jnp.zeros((8 - order_f.shape[0], box), F32)], axis=0)
    order_col[...] = order_f.T.astype(jnp.int32)

    phase("f0_a")
    need("rhs")
    abuf[...] = pick_left(onehot_pt(0), rhs[...], NT)
    phase("f0_y")
    need("t0", "g0")
    y_own = dot_left(g0[...], abuf[skel:, :] - dot_left(t0[...], abuf[:skel, :], TN), TN)
    ybuf[0, :skel, :] = y_own
    ypart[0] = y_own
    phase("f0_barrier")
    pl.semaphore_wait(barrier, total)
    phase("f0_send")
    slots_y0 = {k: slot() for k in has[0]}
    early = []
    for k in along[0] + cross[0]:
        there, dev = neighbour(0, k)
        far = OPPOSITE[k]
        early.append(go(rcopy(ypart.at[0], ybuf.at[0, pl.ds(far * skel, skel), :], slots_y0[k], dev), there))
    for level in range(2):
        for k in (1, 2, 3, 4):
            there, _ = neighbour(level, k)

            @pl.when(jnp.logical_not(there))
            def _():
                ybuf[level, k * skel:(k + 1) * skel, :] = jnp.zeros((skel, rhs_count), F32)
                qrecv[level, k - 1] = jnp.zeros((skel, rhs_count), F32)
    for k in along[1]:
        there, _ = neighbour(1, k)

        @pl.when(jnp.logical_not(there))
        def _():
            nrecv[k - 3] = jnp.zeros(nrecv.shape[1:], F32)
    turned[...] = jnp.zeros_like(turned)
    need("t2", "g2", "k2", "kn", "t3", "g3", "root", "k3")
    mid_send(0)
    outer_send(0)
    inner_send()
    mate_send(0)
    phase("f0_split")
    need("k0")
    for k in range(5):
        k0h[k], k0l[k] = halves(k0[k])
    phase("f0_s")
    s_own = abuf[:skel, :] - dot_left_of(k0h[0], k0l[0], ypart[0], TN)
    ptbuf[...] = onehot_pt(1)
    for k in cross[0] + along[0]:
        there, dev = neighbour(0, k)
        phase(f"f0_wait{k}")
        come(rcopy(ypart.at[0], ybuf.at[0, pl.ds(k * skel, skel), :], slots_y0[OPPOSITE[k]], dev), there)
        phase(f"f0_s{k}")
        s_own = s_own - dot_left_of(k0h[k], k0l[k], ybuf[0, k * skel:(k + 1) * skel, :], TN)
    ssend[0] = s_own
    vbuf[span(rank[1], skel), :] = s_own
    s_give = slot()
    give = rcopy(ssend.at[0], vbuf.at[span(rank[1], skel), :], s_give, member(1))
    early.append(go(give))
    mid_send(1)
    outer_send(1)
    mid_share(*range(7))
    halves_at = [span(rank_of(1, m), skel) for m in (0, 1)]
    abuf[...] = pick_left(ptbuf[:, halves_at[0]], ssend[0], NN)
    phase("f0_gwait")
    need("t1", "g1", "k1")
    come(give)

    phase("f1_a")
    cols = skel >> 1
    rows = span(rank[1], cols)
    abuf[...] = abuf[...] + pick_left(ptbuf[:, halves_at[1]], vbuf[halves_at[1], :], NN)
    phase("f1_w")
    w_own = abuf[pl.ds(pl.multiple_of(skel + rank[1] * cols, cols), cols), :] - dot_left(tg1[rank[1]], abuf[:skel, :], NN)
    wpart[...] = w_own
    wbuf[rows, :] = w_own
    give_w = rcopy(wpart, wbuf.at[rows, :], slot(), member(1))
    go(give_w)
    ptbuf[...] = onehot_p(1)
    phase("f1_wwait")
    come(give_w)
    phase("f1_y")
    y_own = dot_left(g1[rank[1]], wbuf[...], NN)
    ypart[1, :cols, :] = y_own
    ybuf[1, rows, :] = y_own

    def at(k, m):
        return ybuf.at[1, pl.ds(pl.multiple_of(k * skel + rank_of(1, m) * cols, cols), cols), :]

    own_src = ypart.at[1, pl.ds(0, cols), :]
    s_a = slot()
    s_c = {k: [slot(), slot()] for k in cross[1]}
    s_b = {k: slot() for k in along[1]}
    s_d = {k: slot() for k in along[1]}
    phase("f1_send")
    mate = rcopy(own_src, at(0, 0), s_a, member(1))
    go(mate)
    for k in along[1]:
        there, dev = neighbour(1, k)
        early.append(go(rcopy(own_src, at(OPPOSITE[k], 0), s_b[k], dev), there))
    for k in cross[1]:
        there, dev = neighbour(1, k)
        early.append(go(rcopy(own_src, at(OPPOSITE[k], 0), s_c[k][0], dev), there))
    mid_send(2)
    outer_send(2)
    base1[:skel, :] = -dot_left(tg1[rank[1]], y_own, TN)
    base1[skel:, :] = jnp.zeros((skel, rhs_count), F32)
    base1[pl.ds(pl.multiple_of(skel + rank[1] * cols, cols), cols), :] = y_own
    phase("f1_ywait")
    come(mate)
    for k in cross[1]:
        there, dev = neighbour(1, k)
        go(rcopy(at(0, 1), at(OPPOSITE[k], 1), s_c[k][1], dev), there)
    inner_forward(0)
    mid_forward(0)
    phase("f1_s0")
    s_own = abuf[rows, :] - dot_left(k1[0], ybuf[1, :skel, :], NN)
    phase("f1_relay")
    for k in cross[1]:
        there, dev = neighbour(1, k)
        come(rcopy(own_src, at(k, 0), s_c[OPPOSITE[k]][0], dev), there)
    for k in along[1]:
        there, dev = neighbour(1, k)
        come(rcopy(own_src, at(k, 0), s_b[OPPOSITE[k]], dev), there)
        go(rcopy(at(k, 0), at(k, 0), s_d[k], member(1)), there)
    mid_send(3)
    for k in cross[1]:
        there, dev = neighbour(1, k)
        phase(f"f1_cross{k}")
        come(rcopy(own_src, at(k, 1), s_c[OPPOSITE[k]][1], dev), there)
        s_own = s_own - dot_left(k1[k], ybuf[1, k * skel:(k + 1) * skel, :], NN)
    for k in along[1]:
        there, dev = neighbour(1, k)
        phase(f"f1_along{k}")
        come(rcopy(at(k, 1), at(k, 1), s_d[k], member(1)), there)
        s_own = s_own - dot_left(k1[k], ybuf[1, k * skel:(k + 1) * skel, :], NN)
    turned[:, :cols] = s_own.T

    phase("l2_send")
    s_t2 = {m: slot() for m in (1, 2, 3)}
    half_of = lambda m: span(flipped(1, m), half)
    go(rcopy(turned.at[half_of(1)], v2.at[rank[2]], s_t2[1], member(1)), inner)
    go(rcopy(turned.at[half_of(3)], v2.at[rank[2]], s_t2[3], member(3)), inner)
    across = go(rcopy(turned.at[half_of(2)], v2.at[rank[2]], s_t2[2], member(2)), outer)
    pending.pop()
    mid_send(4, 5, 6)
    outer_send(last)
    s_t1 = [slot(), slot(), slot()]
    s_k1 = {k: slot() for k in along[1]}
    near1 = {k: neighbour(1, k)[0] for k in along[1]}
    near1_in = {k: jnp.logical_and(inner, near1[k]) for k in along[1]}
    near1_out = {k: jnp.logical_and(outer, near1[k]) for k in along[1]}
    t1_copy = lambda: rcopy(tg1.at[rank[1]], tg1.at[rank[1]], s_t1[0], member(1))
    if cross[1]:
        kch[...], kcl[...] = halves(jnp.concatenate([k1[1], k1[2]], axis=1))
    part = cols // 2
    g1_part = lambda n: g1.at[rank[1], pl.ds(n * part, part), :]
    g1_copy = lambda n: rcopy(g1_part(n), g1_part(n), s_t1[1 + n], member(1))
    k1_copy = lambda k: rcopy(kgive.at[k - 3], krows.at[k - 3, 1], s_k1[k], member(1))
    others = span(rank_of(1, 1), cols)
    for k in along[1]:
        @pl.when(near1[k])
        def _():
            kturn[...] = k1[k].T
            krows[k - 3, 0] = kturn[rows, :]
            kgive[k - 3] = kturn[others, :]
    part = cols // 2
    g1_part = lambda n: g1.at[rank[1], pl.ds(n * part, part), :]
    g1_copy = lambda n: rcopy(g1_part(n), g1_part(n), s_t1[1 + n], member(1))

    def late_send(when, near, *wanted):
        for n in wanted:
            if n == 3:
                for k in along[1]:
                    go(lambda k=k: k1_copy(k), near[k])
            else:
                go(t1_copy if n == 0 else lambda n=n: g1_copy(n - 1), when)

    def late_make():
        come(t1_copy())
        come(g1_copy(0))
        come(g1_copy(1))
        own = g1[...].reshape(skel, skel)
        n1h[:, :skel], n1l[:, :skel] = halves(-dot3(own, tg1[...].reshape(skel, skel), NN))
        n1h[:, skel:], n1l[:, skel:] = halves(own)

    inner_forward(1)
    inner_forward(2)
    inner_forward(last)

    def wide_pick(pick, level, width, lanes):
        o = order_row[level:level + 1, :]
        o = o + sum((lanes - width) * (o >= width * b).astype(jnp.int32) for b in range(1, box // width))
        lines = lax.broadcasted_iota(jnp.int32, pick.shape, 0)
        pick[...] = jnp.where(lines == o, 1.0, 0.0).astype(BF16)

    def beside(k):
        to = neighbour(2, k)[1] if k < 3 else (i, j + 1 if k == 4 else j - 1)
        return near[2 + k], to

    s_y2 = s_q2 = {k: slot() for k in sides}
    s_y3 = {k: s_y2[k] for k in has[3]}
    s_q3 = {k: slot() for k in has[3]}
    s_t3 = s_x3 = {m: slot() for m in (1, 4)}
    s_x2 = s_t2
    quarter_of = lambda m: span(flipped(2, m), share)
    y2_copy = lambda k: rcopy(y2, yr2.at[OPPOSITE[k] - 1], s_y2[k], beside(k)[1])
    q2_copy = lambda k: rcopy(q2.at[k - 1], qr2.at[OPPOSITE[k] - 1], s_q2[k], beside(k)[1])
    y3_copy = lambda k: rcopy(y3, yr3.at[OPPOSITE[k] - 1], s_y3[k], neighbour(3, k)[1])
    q3_copy = lambda k: rcopy(q3.at[k - 1], qr3.at[OPPOSITE[k] - 1], s_q3[k], neighbour(3, k)[1])
    s_yq = {1: slots_mid[5], 4: slots_mid[6]}
    s_qn = {m: slot() for m in (1, 4)}
    yq_copy = lambda m: rcopy(y2.at[quarter_of(m)], yq.at[bits[2]], s_yq[m], member(m))
    qn_copy = lambda m: rcopy(x3n.at[flipped(2, m)], qn2.at[quarter_of(0)], s_qn[m], member(m))
    up_copy = lambda m: rcopy(turn2.at[quarter_of(m)], v3.at[bits[2]], s_t3[m], member(m))
    down_copy = lambda m: rcopy(x3.at[flipped(2, m)], t2.at[quarter_of(0)], s_x3[m], member(m))
    out_copy = lambda m: rcopy(x2.at[flipped(1, m)], back2.at[half_of(0)], s_x2[m], member(m))

    def make_n0():
        n0h[:skel, :], n0l[:skel, :] = halves(-dot3(t0[...], g0[...], NN))
        n0h[skel:, :], n0l[skel:, :] = halves(g0[...])
        base0[...] = -dot_left(t0[...], ypart[0], NN)

    @pl.when(outer)
    def _():
        phase("l2_pick")
        wide_pick(pick2, 2, cols, turned.shape[1])
        mid_forward(1)
        full = lambda n: mid[n].reshape(skel, skel)
        for n in (0, 1):
            mid_full(n)
            midh[n], midl[n] = halves(full(n))
        v2[rank[2]] = turned[half_of(0), :]
        phase("l2_in")
        come(rcopy(turned.at[half_of(0)], v2.at[rank_of(2, 2)], s_t2[2], member(2)))
        come(rcopy(turned.at[half_of(0)], v2.at[rank_of(2, 1)], s_t2[1], member(1)))
        come(rcopy(turned.at[half_of(0)], v2.at[rank_of(2, 3)], s_t2[3], member(3)))
        phase("l2_a")
        a = pick_right(jnp.concatenate([v2[b] for b in range(4)], axis=1), pick2[...], NN)
        s0, r0 = a[:, :skel], a[:, skel:]
        phase("l2_y")
        y = dot_right_of(r0 - dot_right_of(s0, midh[0], midl[0], NT), midh[1], midl[1], NT)
        y2[...] = y
        for m in (4, 1):
            yq_copy(m).start()
        for k in sides:
            @pl.when(beside(k)[0])
            def _():
                y2_copy(k).start()
        phase("l2_s")
        mid_forward(2)
        mid_full(2)
        turn2[...] = s0 - dot_right(y, full(2), NT)
        for k in sides:
            mid_forward(2 + k)
        for k in sides:
            phase(f"l2_s{k}")

            @pl.when(beside(k)[0])
            def _():
                mid_full(2 + k)
                rcopy(y2, yr2.at[k - 1], s_y2[OPPOSITE[k]], beside(k)[1]).wait_recv()
                turn2[...] = turn2[...] - dot_right(yr2[k - 1], full(2 + k), NT)
        for m in (4, 1):
            up_copy(m).start()
        late_send(outer, near1_out, 0, 1, 2, 3)
        phase("l2_split")
        midh[2], midl[2] = halves(full(2))
        for k in sides:
            @pl.when(beside(k)[0])
            def _():
                midh[2 + k], midl[2 + k] = halves(full(2 + k))
        make_n0()
        phase(None)

    @pl.when(inner)
    def _():
        phase("l3_n0")
        make_n0()
        phase("l3_pick")
        wide_pick(pick3, 3, skel, skel)
        for n in (1, 2, 3):
            mate_send(n)
        for n in range(4):
            come(mate_copy(n, False))
            come(pair_copy(n, False))
        for n in range(3 + kinds):
            toph[n], topl[n] = halves(top[n].reshape(skel, skel))
        for n in range(2):
            pairh[n], pairl[n] = halves(pair[4 * n:4 * n + 4].reshape(skel, skel))
        phase("l3_pair")
        for m in (1, 4):
            come(rcopy(y2.at[quarter_of(0)], yq.at[flipped(2, m)], s_yq[m], member(m)))
        for n in range(2):
            x3n[n] = dot_right_of(yq[1 - n], pairh[n], pairl[n], NT)
        phase("l3_in")
        for m in (1, 4):
            come(rcopy(turn2.at[quarter_of(0)], v3.at[flipped(2, m)], s_t3[m], member(m)))
        late_send(inner, near1_in, 0, 1)
        phase("l3_y")
        a = pick_right(jnp.concatenate([v3[0] - x3n[0], v3[1] - x3n[1]], axis=1), pick3[...], NN)
        s0, r0 = a[:, :skel], a[:, skel:]
        y = dot_right_of(r0 - dot_right_of(s0, toph[0], topl[0], NT), toph[1], topl[1], NT)
        y3[...] = y
        for k in has[3]:
            @pl.when(neighbour(3, k)[0])
            def _():
                y3_copy(k).start()
        phase("l3_s")
        v3[0] = s0 - dot_right_of(y, toph[3], topl[3], NT)
        for k in has[3]:
            phase(f"l3_s{k}")

            @pl.when(neighbour(3, k)[0])
            def _():
                rcopy(y3, yr3.at[k - 1], s_y3[OPPOSITE[k]], neighbour(3, k)[1]).wait_recv()
                v3[0] = v3[0] - dot_right_of(yr3[k - 1], toph[3 + k], topl[3 + k], NT)
        phase("l3_q")
        t = dot_right_of(v3[0], toph[2], topl[2], NT)
        for k in has[3]:
            @pl.when(neighbour(3, k)[0])
            def _():
                q3[k - 1] = dot_right_of(t, toph[3 + k], topl[3 + k], NN)
                q3_copy(k).start()
        v3[0] = dot_right_of(t, toph[3], topl[3], NN)
        for k in has[3]:
            phase(f"l3_u{k}")

            @pl.when(neighbour(3, k)[0])
            def _():
                rcopy(q3.at[k - 1], qr3.at[k - 1], s_q3[OPPOSITE[k]], neighbour(3, k)[1]).wait_recv()
                v3[0] = v3[0] + qr3[k - 1]
        phase("l3_x")
        xr = y - dot_right_of(v3[0], toph[1], topl[1], NN)
        xs = t - dot_right_of(xr, toph[0], topl[0], NN)
        xv = pick_right(jnp.concatenate([xs, xr], axis=1), pick3[...], NT)
        x3[0], x3[1] = xv[:, :skel], xv[:, skel:]
        for m in (4, 1):
            down_copy(m).start()
        for n in range(2):
            x3n[1 - n] = dot_right_of(x3[n], pairh[n], pairl[n], NN)
        for m in (4, 1):
            qn_copy(m).start()
        pl.semaphore_wait(ready, 1)
        late_send(inner, near1_in, 3, 2)
        phase(None)

    @pl.when(outer)
    def _():
        phase("l2_tin")
        pick2[:box, :] = onehot_p(2)
        for m in (1, 4):
            come(rcopy(x3.at[bits[2]], t2.at[quarter_of(m)], s_x3[m], member(m)))
        pl.semaphore_signal(ready, 1, device_id=member(1), device_id_type=MESH)
        phase("l2_q")
        t = t2[...]
        for k in reversed(sides):
            @pl.when(beside(k)[0])
            def _():
                q2[k - 1] = dot_right_of(t, midh[2 + k], midl[2 + k], NN)
                y2_copy(k).wait_send()
                q2_copy(k).start()
        yr2[0] = dot_right_of(t, midh[2], midl[2], NN)
        for k in sides:
            phase(f"l2_u{k}")

            @pl.when(beside(k)[0])
            def _():
                rcopy(q2.at[k - 1], qr2.at[k - 1], s_q2[OPPOSITE[k]], beside(k)[1]).wait_recv()
                yr2[0] = yr2[0] + qr2[k - 1]
        phase("l2_qn")
        for m in (1, 4):
            come(rcopy(x3n.at[bits[2]], qn2.at[quarter_of(m)], s_qn[m], member(m)))
        yr2[0] = yr2[0] + qn2[...]
        phase("l2_x")
        xr = y2[...] - dot_right_of(yr2[0], midh[1], midl[1], NN)
        xs = t - dot_right_of(xr, midh[0], midl[0], NN)
        x = jnp.concatenate([xs, xr], axis=1)
        x2[bits[1]] = pick_right(x, pick2[span(bits[1], skel), :], NT)
        out_copy(1).start()
        x2[1 - bits[1]] = pick_right(x, pick2[span(1 - bits[1], skel), :], NT)
        out_copy(3).start()
        across[1]().wait_send()
        out_copy(2).start()
        back2[half_of(0), :] = x2[bits[1]]
        phase(None)

    phase("l2_out")
    come(rcopy(x2.at[bits[1]], back2.at[half_of(2)], s_x2[2], member(2)), outer)
    for m in (1, 3):
        come(rcopy(x2.at[bits[1]], back2.at[half_of(m)], s_x2[m], member(m)), inner)

    phase("b1_settle")
    settle(early)
    phase("b1_q")
    tfull[...] = back2[...].T
    t_own = tfull[rows, :]
    s_q = {k: s_c[k][0] if k < 3 else s_b[k] for k in has[1]}
    qsend[1, skel:3 * skel, :] = dot_left_of(kch[...], kcl[...], t_own, TN)
    for k in cross[1]:
        at_k = pl.ds(k * skel, skel)
        there, dev = neighbour(1, k)
        go(rcopy(qsend.at[1, at_k, :], qrecv.at[1, OPPOSITE[k] - 1], s_q[k], dev), there)
    for k in along[1]:
        there, dev = neighbour(1, k)

        @pl.when(there)
        def _():
            k1_copy(k).wait_recv()
            nsend[k - 3] = dot_left(krows[k - 3, 0], t_own, NN) + dot_left(krows[k - 3, 1], tfull[others, :], NN)
        go(rcopy(nsend.at[k - 3], nrecv.at[OPPOSITE[k] - 3], s_q[k], dev), there)
    phase("b1_q0")
    u = dot_left(k1[0], t_own, TN)
    abuf[...] = base1[...]
    abuf[rows, :] = abuf[rows, :] + t_own
    phase("b1_late")
    late_make()
    for k in cross[1]:
        phase(f"b1_wait{k}")
        there, dev = neighbour(1, k)
        come(rcopy(qsend.at[1, pl.ds(k * skel, skel), :], qrecv.at[1, k - 1], s_q[OPPOSITE[k]], dev), there)
        u = u + qrecv[1, k - 1]
    qsend[1, :skel, :] = u
    for k in along[1]:
        phase(f"b1_wait{k}")
        there, dev = neighbour(1, k)
        come(rcopy(nsend.at[k - 3], nrecv.at[k - 3], s_q[OPPOSITE[k]], dev), there)
        qsend[1, rows, :] = qsend[1, rows, :] + nrecv[k - 3]
    phase("b1_comb")
    abuf[...] = abuf[...] - dot_left_of(n1h[...], n1l[...], qsend[1, :skel, :], TN)
    phase("b1_x")
    both = jnp.concatenate(halves(abuf[...]), axis=1)
    for m in (1, 0):
        spot = span(rank_of(1, m), skel)
        xpart[spot, :] = lanes_summed(product(ptbuf[spot, :], both, NN))
        if m:
            give_x = rcopy(xpart.at[spot, :], xrecv1.at[0], s_give, member(1))
            go(give_x)
    phase("b1_xwait")
    ptbuf[...] = onehot_pt(0)
    come(give_x)
    t_own = xpart[span(rank[1], skel), :] + xrecv1[0]

    phase("b0_q")
    s_q = slots_y0
    for k in cross[0] + along[0]:
        at_k = pl.ds(k * skel, skel)
        if k % 2:
            two = slice(k, k + 2)
            qsend[0, k * skel:(k + 2) * skel, :] = dot_left_of(
                k0h[two].reshape(2 * skel, skel), k0l[two].reshape(2 * skel, skel), t_own, NN)
        there, dev = neighbour(0, k)
        go(rcopy(qsend.at[0, at_k, :], qrecv.at[0, OPPOSITE[k] - 1], s_q[k], dev), there)
    u = dot_left_of(k0h[0], k0l[0], t_own, NN)
    abuf[:skel, :] = base0[...] + t_own
    abuf[skel:, :] = ypart[0]
    for k in cross[0] + along[0]:
        phase(f"b0_wait{k}")
        there, dev = neighbour(0, k)
        come(rcopy(qsend.at[0, pl.ds(k * skel, skel), :], qrecv.at[0, k - 1], s_q[OPPOSITE[k]], dev), there)
        u = u + qrecv[0, k - 1]
    phase("b0_x")
    abuf[...] = abuf[...] - dot_left_of(n0h[...], n0l[...], u, NN)
    phase("b0_out")
    rhs[...] = pick_right(abuf[...], ptbuf[...], TN)
    result = pltpu.make_async_copy(rhs, out.at[0, 0], local.at[0])
    result.start()

    assert count[0] <= send.shape[0], count[0]
    phase("drain")
    for when, make in pending:
        if when is None:
            make().wait_send()
        else:
            @pl.when(when)
            def _():
                make().wait_send()

    @pl.when(inner)
    def _():
        for k in has[3]:
            @pl.when(neighbour(3, k)[0])
            def _():
                y3_copy(k).wait_send()
                q3_copy(k).wait_send()
        for m in (4, 1):
            down_copy(m).wait_send()
            qn_copy(m).wait_send()

    @pl.when(outer)
    def _():
        for k in sides:
            @pl.when(beside(k)[0])
            def _():
                q2_copy(k).wait_send()
        for m in (4, 1):
            up_copy(m).wait_send()
            yq_copy(m).wait_send()
        for m in (3, 1, 2):
            out_copy(m).wait_send()
    result.wait()
    phase(None)


def body(size_x, size_y, right_sides, skeleton_order, *weights):
    rows = right_sides.shape[2]
    box = right_sides.shape[3]
    skel = box // 2
    weights = [jnp.swapaxes(w, -1, -2) if w.shape[-1] < skel else w for w in weights]
    vm = lambda *shape: pltpu.VMEM(shape, F32)
    half_of = lambda *shape: pltpu.VMEM(shape, BF16)
    widths = [skel >> level for level in range(4)]
    half, share = rows // 2, rows // 4
    kinds = 5 if size_y > REACH[3][1] else 3
    slots = 54 if kinds == 3 else 60
    lanes = -(-widths[1] // 128) * 128
    scratch = [
        vm(rows, box), pltpu.VMEM((4, box), jnp.int32), vm(skel, skel), vm(2, widths[1], skel),
        vm(skel, skel), vm(2, widths[1], skel), vm(5, skel, skel), vm(5, widths[1], skel),
        vm(2, 5 * skel, rows), vm(box, rows), vm(2, 5 * skel, rows), vm(2, 4, skel, rows),
        vm(1, skel, rows), vm(box, rows), vm(box, rows),
        vm(box, rows), vm(2, skel, rows), vm(1, skel, rows),
        pltpu.VMEM((box, box), BF16), pltpu.VMEM((box, 8), jnp.int32),
        vm(skel, rows), vm(widths[1], rows), vm(2, widths[1], widths[1]), vm(skel, widths[1]), vm(2, 2, widths[1], widths[1]), half_of(widths[1], box), half_of(widths[1], box),
        vm(skel, rows), vm(2, widths[1], rows), vm(2, widths[1], rows),
        half_of(5, skel, skel), half_of(5, skel, skel), half_of(box, skel), half_of(box, skel), vm(skel, rows), half_of(skel, box), half_of(skel, box),
        half_of(7, skel, skel), half_of(7, skel, skel), half_of(3 + kinds, skel, skel), half_of(3 + kinds, skel, skel),
        vm(7, 4, widths[2], skel), vm(rows, lanes), vm(4, half, lanes),
        vm(half, skel), vm(4, half, skel), vm(4, half, skel), vm(4, half, skel),
        vm(2, half, skel), vm(rows, skel), pltpu.VMEM((4 * lanes, box), BF16), vm(half, skel), vm(half, skel),
        vm(3 + kinds, 8, widths[3], skel), vm(2, share, skel),
        vm(share, skel), vm(kinds - 1, share, skel), vm(kinds - 1, share, skel), vm(kinds - 1, share, skel),
        vm(2, share, skel), pltpu.VMEM((box, box), BF16),
        vm(8, widths[2], skel), half_of(2, skel, skel), half_of(2, skel, skel), vm(2, share, skel), vm(2, share, skel), vm(half, skel),
        pltpu.SemaphoreType.DMA((16,)), pltpu.SemaphoreType.REGULAR,
        pltpu.SemaphoreType.DMA((slots,)), pltpu.SemaphoreType.DMA((slots,)),
    ]
    return pl.pallas_call(
        functools.partial(kernel, size_x, size_y),
        out_shape=jax.ShapeDtypeStruct(right_sides.shape, F32),
        in_specs=[pl.BlockSpec(memory_space=pl.ANY)] * (2 + len(weights)),
        out_specs=pl.BlockSpec(memory_space=pl.ANY),
        scratch_shapes=scratch,
        compiler_params=pltpu.CompilerParams(
            collective_id=0, has_side_effects=True, vmem_limit_bytes=(52 if kinds == 3 else 62) * 2**20
        ),
    )(*[pltpu.with_memory_space_constraint(a, pltpu.HBM) for a in (right_sides, skeleton_order, *weights)])


def solution(mesh):
    four = P("bx", "by", None, None)
    five = P("bx", "by", None, None, None)
    in_specs = (four,) * 10 + (five,) * 4 + (four,)
    return jax.shard_map(
        functools.partial(body, mesh.shape["bx"], mesh.shape["by"]),
        mesh=mesh, in_specs=in_specs, out_specs=four, check_vma=False,
    )
```
